128 devices in a mesh: bx: 4 (over x), by: 8 (over y, core), bz: 4 (over z).
Axes of the slice: x: 4, y: 4, z: 4, core: 2. Of those that a mesh axis runs over, the one named last changes fastest.
Arguments:
- counts: bfloat16 [256, 64, 128, 128], P(('bx', 'by', 'bz')), may hold values from 0.099609375 to 10
- row_split: bfloat16 [256, 64, 128, 256], P(('bx', 'by', 'bz')), may hold values from 0 to 0.03125
- col_split: bfloat16 [256, 64, 128, 256], P(('bx', 'by', 'bz')), may hold values from 0 to 0.03125
- efficiency: bfloat16 [64, 128, 128], replicated, may hold values from 0.5 to 1.5
- lorentz: float32 [3600], replicated, may hold values from 0.3 to 3
- angles: int32 [256], P(('bx', 'by', 'bz')), may hold values from 0 to 3599
- tile_owner: int32 [16384, 1], P(('bx', 'by', 'bz')), may hold values from 0 to 127; in each aligned block of 128 rows (0 to 127, 128 to 255, ...) at most 4 rows name the same one
- tile_box: int32 [16384], P(('bx', 'by', 'bz')), may hold values from 0 to 127
Outputs:
- intensity: float32 [8, 8, 4, 64, 256], P('bx', 'by', 'bz')
The draws below stay inside these ranges and needn't reach their ends.
Inputs may be any that keep to these rules, and one draw needn't show every extreme that they name: `tile_owner`: among the 128 tiles of one device, no owner is named more than 4 times, a bound that some block reaches.
All inputs are finite; a program needn't handle non-finite values.
Results may differ from the reference program's by a relative error of at most 0.0003.
Values sent between devices are 32-bit elements; how exact they have to be, the bound alone decides.
A program may use at most 128 MiB of HBM per device.

```python
import math
import jax
import jax.numpy as jnp
import numpy as np
from jax import lax

PIX = 128
VX = 8
VY = 8
VZ = 4
VOX = 256
GX = 8
GY = 8
GZ = 4
BOXX = 4
BOXY = 4
BOXZ = 4
BOX_BRICK = 64
TILE_FRAME = 64
NANG = 3600
FRAMES = 256
TILE_DEV = 128
TILES = 16384
LX = 2
LY = 1
LZ = 1
BOX_DEV = 128
CAP = 4
N_BY = 8
N_BZ = 4
DEVICES = 128


def place_ends(values, stream_key, low, largest):
    longest = values.shape.index(max(values.shape))
    spots = []
    for shift in (0, 1):
        where = [jax.random.randint(jax.random.fold_in(stream_key, axis), (), 0, length) for axis, length in enumerate(values.shape)]
        where[longest] = (where[longest] + shift) % values.shape[longest]
        spots.append(tuple(where))
    return values.at[spots[0]].set(low).at[spots[1]].set(largest)


def block_levels(rng, extent, cuts, smallest, top_value):
    gain, own = 1.0, jax.random.fold_in(rng, 6)
    for axis_at, blocks in cuts:
        steps = jnp.exp(jax.random.uniform(jax.random.fold_in(own, axis_at), (blocks,), jnp.float32, smallest / len(cuts), top_value / len(cuts)))
        gain = gain * jnp.repeat(steps, extent[axis_at] // blocks).reshape([-1 if axis == axis_at else 1 for axis in range(len(extent))])
    return gain


def deal_out(stream_key, own, number, rows, amount, top, limit, skew):
    ranking = jax.random.permutation(stream_key, amount)
    packed, usual = portions_of(amount, rows * top, limit, skew, True), portions_of(amount, rows * top, limit, skew, False)
    places = jnp.arange(amount)

    def named(lengths, rotation):
        used = int((lengths > 0).sum())
        fixed = max(1, used // 4)
        passed = fixed + (places - fixed + rotation * (used - fixed)) % max(1, amount - fixed)
        return jnp.zeros((amount,), jnp.int32).at[ranking[jnp.where(places < fixed, places, passed)]].set(jnp.asarray(lengths, jnp.int32))

    lengths = jnp.where(number % 4 == 0, named(packed, number // 4), named(usual, number - number // 4 - 1))
    mixed = jax.random.permutation(jax.random.fold_in(own, 3), amount)
    donor, receiver = mixed[0:amount // 2 * 2:2], mixed[1:amount // 2 * 2:2]
    slack = jnp.minimum(lengths[donor] - 1, limit - lengths[receiver]) // 2
    slack = jnp.where((donor == ranking[0]) | (receiver == ranking[0]) | (lengths[receiver] == 0), 0, jnp.maximum(slack, 0))
    passed = jax.random.randint(jax.random.fold_in(own, 4), (amount // 2,), 0, 1 << 20) % (slack + 1)
    lengths = lengths.at[donor].add(-passed).at[receiver].add(passed)
    labels = jnp.searchsorted(jnp.cumsum(lengths), jnp.arange(rows * top), side="right").astype(jnp.int32)
    table = labels.reshape(top, rows).T
    table = table[jax.random.permutation(jax.random.fold_in(own, 1), rows)]
    rotation = jax.random.randint(jax.random.fold_in(own, 2), (rows, 1), 0, top)
    return jnp.take_along_axis(table, (jnp.arange(top)[None, :] + rotation) % top, axis=1)


def portions_of(count, total, bound, skew, full):
    weights = [(1 << 20) // math.isqrt(grade ** skew) + 1 for grade in range(1, count + 1)]
    largest = bound if full else min(bound, max(-(-total // count), total * weights[0] // sum(weights)))
    least = 1 if total - largest >= count - 1 else 0
    given, spare = [largest] + [least] * (count - 1), total - largest - least * (count - 1)
    while spare > 0:
        candidates = [i for i in range(1, count) if given[i] < largest] or [i for i in range(1, count) if given[i] < bound]
        pool, left = sum([weights[i] for i in candidates]), spare
        for i in candidates:
            extra = min(bound - given[i], max(1, left * weights[i] // pool), spare)
            given[i] = given[i] + extra
            spare = spare - extra
    return np.array(given)


def setup_inputs(seed: int = 0) -> dict:
    streams_of = jax.random.split(jax.random.key(seed), 9)
    counts = jnp.clip(jnp.exp(math.log(10.0) - 4.609084 * jax.random.uniform(streams_of[0], (FRAMES, TILE_FRAME, PIX, PIX), jnp.float32) ** block_levels(streams_of[0], (FRAMES, TILE_FRAME, PIX, PIX), ((0, 128),), -0.2, 0.2)), 0.099609375, 10.0).astype(jnp.bfloat16)
    row_split = jnp.clip(0.03125 * jax.random.uniform(streams_of[1], (FRAMES, TILE_FRAME, PIX, VOX), jnp.float32) ** block_levels(streams_of[1], (FRAMES, TILE_FRAME, PIX, VOX), ((0, 128),), -0.2, 0.2), 0.0, 0.03125).astype(jnp.bfloat16)
    col_split = jnp.clip(0.03125 * jax.random.uniform(streams_of[2], (FRAMES, TILE_FRAME, PIX, VOX), jnp.float32) ** block_levels(streams_of[2], (FRAMES, TILE_FRAME, PIX, VOX), ((0, 128),), -0.2, 0.2), 0.0, 0.03125).astype(jnp.bfloat16)
    efficiency = jnp.clip(1.0 + 0.1 * jax.random.normal(streams_of[3], (TILE_FRAME, PIX, PIX), jnp.float32), 0.5, 1.5).astype(jnp.bfloat16)
    lorentz = jnp.clip(jnp.exp(jax.random.uniform(streams_of[4], (NANG,), jnp.float32, math.log(0.3), math.log(3.0))), 0.3, 3.0)
    angles = place_ends(jax.random.randint(streams_of[5], (FRAMES,), 0, NANG), jax.random.fold_in(streams_of[5], 1), 0, NANG - 1).astype(jnp.int32)
    tile_owner_keys = jax.random.split(jax.random.fold_in(streams_of[6], 1), TILES // TILE_DEV)
    tile_owner_turns = jax.random.permutation(jax.random.fold_in(streams_of[6], 3), TILES // TILE_DEV)
    tile_owner = jax.vmap(lambda own, number: deal_out(jax.random.fold_in(streams_of[6], 2), own, number, TILE_DEV, DEVICES, 1, CAP, 2))(tile_owner_keys, tile_owner_turns).reshape((TILES, 1))
    tile_box = place_ends(jax.random.randint(streams_of[7], (TILES,), 0, BOX_DEV), jax.random.fold_in(streams_of[7], 1), 0, BOX_DEV - 1).astype(jnp.int32)
    return dict(counts=counts, row_split=row_split, col_split=col_split, efficiency=efficiency, lorentz=lorentz, angles=angles, tile_owner=tile_owner, tile_box=tile_box)


def contributions(item, efficiency):
    frame_counts, frame_rows, frame_cols, frame_factor = item
    cols = frame_cols.astype(jnp.float32)
    rows = frame_rows.astype(jnp.float32)
    counted = jnp.einsum("tpq,tqv->tpv", frame_counts.astype(jnp.float32), cols)
    value = jnp.sum(rows * counted, axis=1) * frame_factor
    seen = jnp.einsum("tpq,tqv->tpv", efficiency.astype(jnp.float32), cols)
    weight = jnp.sum(rows * seen, axis=1)
    return jnp.stack([value, weight], axis=1)


def reference(counts, row_split, col_split, efficiency, lorentz, angles, tile_owner, tile_box):
    factor = lorentz[angles]
    payload = lax.map(lambda item: contributions(item, efficiency), (counts, row_split, col_split, factor))
    payload = payload.reshape(-1, 2, VOX)
    owner = tile_owner[:, 0]
    dev_x = owner // (N_BY * N_BZ)
    dev_y = (owner // N_BZ) % N_BY
    dev_z = owner % N_BZ
    brick_local = tile_box // BOX_BRICK
    box_index = tile_box % BOX_BRICK
    part_a = brick_local // (LY * LZ)
    part_b = (brick_local // LZ) % LY
    part_c = brick_local % LZ
    gx_index = dev_x * LX + part_a
    gy_index = dev_y * LY + part_b
    gz_index = dev_z * LZ + part_c
    flat = (((gx_index * GY + gy_index) * GZ + gz_index) * BOX_BRICK + box_index).astype(jnp.int32)
    sums = jax.ops.segment_sum(payload, flat, num_segments=GX * GY * GZ * BOX_BRICK)
    volume = sums.reshape(GX, GY, GZ, BOXX, BOXY, BOXZ, 2, VX, VY, VZ)
    volume = 0.5 * (volume + jnp.flip(volume, (0, 3, 7)))
    volume = 0.5 * (volume + jnp.flip(volume, (1, 4, 8)))
    volume = 0.5 * (volume + jnp.flip(volume, (2, 5, 9)))
    result = volume[:, :, :, :, :, :, 0] / jnp.maximum(volume[:, :, :, :, :, :, 1], 1.0)
    return result.reshape(GX, GY, GZ, BOX_BRICK, VOX)
```

```python
import numpy as np
import jax
import jax.numpy as jnp
from jax import lax
from jax.sharding import PartitionSpec as P

VX = 8
VY = 8
VZ = 4
GX = 8
GY = 8
GZ = 4
BOXX = 4
BOXY = 4
BOXZ = 4
BOX_BRICK = 64


def mirrored(array, axis):
    size = lax.axis_size(axis)
    if size == 1:
        return array
    return lax.ppermute(array, axis, [(i, size - 1 - i) for i in range(size)])


def flip_table(sizes, flipped):
    index = np.arange(int(np.prod(sizes))).reshape(sizes)
    return np.flip(index, flipped).reshape(-1).astype(np.int32)


def permuting(table):
    size = table.shape[0]
    return (jnp.asarray(table)[:, None] == lax.iota(jnp.int32, size)[None, :]).astype(jnp.float32)


def laue_step(volume, axis, row_table, lane_table):
    partner = mirrored(volume, axis)
    rows = permuting(row_table)
    lanes = permuting(np.concatenate([lane_table, lane_table + lane_table.shape[0]])).T
    moved = jnp.dot(rows, partner, precision=lax.Precision.HIGHEST, preferred_element_type=jnp.float32)
    moved = jnp.dot(moved, lanes, precision=lax.Precision.HIGHEST, preferred_element_type=jnp.float32)
    return 0.5 * (volume + moved)


def shards(counts, row_split, col_split, efficiency, lorentz, angles, tile_owner, tile_box):
    frames_here, tiles_frame, pixels, unused_width = counts.shape
    voxels = row_split.shape[-1]
    size_x = lax.axis_size("bx")
    size_y = lax.axis_size("by")
    size_z = lax.axis_size("bz")
    devices_all = size_x * size_y * size_z
    tiles_here = frames_here * tiles_frame
    capacity = max(4, 4 * tiles_here // devices_all)
    local_x = GX // size_x
    local_y = GY // size_y
    local_z = GZ // size_z
    boxes_here = local_x * local_y * local_z * BOX_BRICK
    picks = angles[:, None] == jnp.arange(lorentz.shape[0], dtype=jnp.int32)[None, :]
    factor = jnp.sum(jnp.where(picks, lorentz[None, :], 0.0), axis=1)
    counted = jnp.einsum("ftpq,ftqv->ftpv", counts, col_split, preferred_element_type=jnp.float32)
    value = jnp.sum(row_split * counted, axis=2) * factor[:, None, None]
    seen = jnp.einsum("tpq,ftqv->ftpv", efficiency, col_split, preferred_element_type=jnp.float32)
    weight = jnp.sum(row_split * seen, axis=2)
    payload = jnp.concatenate(
        [value.reshape(tiles_here, voxels), weight.reshape(tiles_here, voxels)], axis=1
    )
    owner = tile_owner[:, 0]
    marks = (owner[:, None] == jnp.arange(devices_all, dtype=jnp.int32)[None, :]).astype(jnp.int32)
    before = jnp.cumsum(marks, axis=0) - marks
    rank = jnp.sum(before * marks, axis=1)
    slot = owner * capacity + rank
    outgoing = jnp.zeros((devices_all * capacity, 2 * voxels), jnp.float32).at[slot].set(payload)
    labels = jnp.full((devices_all * capacity,), -1.0, jnp.float32).at[slot].set(
        tile_box.astype(jnp.float32)
    )
    label_width = 128
    labels = jnp.pad(labels.reshape(devices_all, capacity), ((0, 0), (0, label_width - capacity)))
    packed = jnp.concatenate(
        [outgoing.reshape(devices_all, capacity * 2 * voxels), labels], axis=1
    )
    arrived = lax.all_to_all(packed, ("bx", "by", "bz"), split_axis=0, concat_axis=0, tiled=True)
    arrived_payload = arrived[:, : capacity * 2 * voxels].reshape(devices_all * capacity, 2 * voxels)
    arrived_ids = arrived[:, capacity * 2 * voxels : capacity * 2 * voxels + capacity].reshape(
        devices_all * capacity
    )
    wanted = (
        jnp.arange(boxes_here, dtype=jnp.float32)[:, None] == arrived_ids[None, :]
    ).astype(jnp.float32)
    sums = jnp.dot(
        wanted, arrived_payload, precision=lax.Precision.HIGHEST, preferred_element_type=jnp.float32
    )
    row_sizes = (local_x, local_y, local_z, BOXX, BOXY, BOXZ)
    lane_sizes = (VX, VY, VZ)
    volume = laue_step(sums, "bx", flip_table(row_sizes, (0, 3)), flip_table(lane_sizes, (0,)))
    volume = laue_step(volume, "by", flip_table(row_sizes, (1, 4)), flip_table(lane_sizes, (1,)))
    volume = laue_step(volume, "bz", flip_table(row_sizes, (2, 5)), flip_table(lane_sizes, (2,)))
    result = volume[:, :voxels] / jnp.maximum(volume[:, voxels:], 1.0)
    return result.reshape(local_x, local_y, local_z, BOX_BRICK, voxels)


def solution(mesh):
    return jax.shard_map(
        shards,
        mesh=mesh,
        in_specs=(
            P(("bx", "by", "bz"), None, None, None),
            P(("bx", "by", "bz"), None, None, None),
            P(("bx", "by", "bz"), None, None, None),
            P(),
            P(),
            P(("bx", "by", "bz")),
            P(("bx", "by", "bz"), None),
            P(("bx", "by", "bz")),
        ),
        out_specs=P("bx", "by", "bz", None, None),
        check_vma=False,
    )
```

```python
import numpy as np
import jax
import jax.numpy as jnp
from jax import lax
from jax.sharding import PartitionSpec as P
from jax.experimental import pallas as pl
from jax.experimental.pallas import tpu as pltpu

VX = 8
VY = 8
VZ = 4
GX = 8
GY = 8
GZ = 4
BOXX = 4
BOXY = 4
BOXZ = 4
BOX_BRICK = 64


def mirrored(array, axis):
    size = lax.axis_size(axis)
    if size == 1:
        return array
    return lax.ppermute(array, axis, [(i, size - 1 - i) for i in range(size)])


def flip_table(sizes, flipped):
    index = np.arange(int(np.prod(sizes))).reshape(sizes)
    return np.flip(index, flipped).reshape(-1).astype(np.int32)


def permuting(table):
    size = table.shape[0]
    return (jnp.asarray(table)[:, None] == lax.iota(jnp.int32, size)[None, :]).astype(jnp.float32)


def laue_step(volume, axis, row_table, lane_table):
    partner = mirrored(volume, axis)
    rows = permuting(row_table)
    lanes = permuting(np.concatenate([lane_table, lane_table + lane_table.shape[0]])).T
    moved = jnp.dot(rows, partner, precision=lax.Precision.HIGHEST, preferred_element_type=jnp.float32)
    moved = jnp.dot(moved, lanes, precision=lax.Precision.HIGHEST, preferred_element_type=jnp.float32)
    return 0.5 * (volume + moved)


def tile_kernel(factor_ref, counts_ref, eff_ref, rows_ref, cols_ref, out_ref):
    block, unused_pixels, voxels = rows_ref.shape
    for t in range(block):
        cols = cols_ref[t]
        rows = rows_ref[t].astype(jnp.float32)
        counted = jnp.dot(counts_ref[t], cols, preferred_element_type=jnp.float32)
        seen = jnp.dot(eff_ref[t], cols, preferred_element_type=jnp.float32)
        value = jnp.sum(rows * counted, axis=0, keepdims=True)
        weight = jnp.sum(rows * seen, axis=0, keepdims=True)
        out_ref[t : t + 1, :voxels] = value * factor_ref[t : t + 1, :]
        out_ref[t : t + 1, voxels:] = weight


def tile_payload(counts, row_split, col_split, efficiency, factor):
    frames_here, tiles_frame, pixels, columns = counts.shape
    voxels = row_split.shape[-1]
    tiles_here = frames_here * tiles_frame
    block = 8
    per_frame = tiles_frame // block
    tile_factor = jnp.repeat(factor, tiles_frame)[:, None]
    return pl.pallas_call(
        tile_kernel,
        grid=(tiles_here // block,),
        in_specs=[
            pl.BlockSpec((block, 1), lambda i: (i, 0)),
            pl.BlockSpec((block, pixels, columns), lambda i: (i, 0, 0)),
            pl.BlockSpec((block, pixels, columns), lambda i: (i % per_frame, 0, 0)),
            pl.BlockSpec((block, pixels, voxels), lambda i: (i, 0, 0)),
            pl.BlockSpec((block, pixels, voxels), lambda i: (i, 0, 0)),
        ],
        out_specs=pl.BlockSpec((block, 2 * voxels), lambda i: (i, 0)),
        out_shape=jax.ShapeDtypeStruct((tiles_here, 2 * voxels), jnp.float32),
    )(
        tile_factor,
        counts.reshape(tiles_here, pixels, columns),
        efficiency,
        row_split.reshape(tiles_here, pixels, voxels),
        col_split.reshape(tiles_here, pixels, voxels),
    )


def shards(counts, row_split, col_split, efficiency, lorentz, angles, tile_owner, tile_box):
    frames_here, tiles_frame, pixels, unused_width = counts.shape
    voxels = row_split.shape[-1]
    size_x = lax.axis_size("bx")
    size_y = lax.axis_size("by")
    size_z = lax.axis_size("bz")
    devices_all = size_x * size_y * size_z
    tiles_here = frames_here * tiles_frame
    capacity = max(4, 4 * tiles_here // devices_all)
    local_x = GX // size_x
    local_y = GY // size_y
    local_z = GZ // size_z
    boxes_here = local_x * local_y * local_z * BOX_BRICK
    picks = angles[:, None] == jnp.arange(lorentz.shape[0], dtype=jnp.int32)[None, :]
    factor = jnp.sum(jnp.where(picks, lorentz[None, :], 0.0), axis=1)
    payload = tile_payload(counts, row_split, col_split, efficiency, factor)
    owner = tile_owner[:, 0]
    marks = (owner[:, None] == jnp.arange(devices_all, dtype=jnp.int32)[None, :]).astype(jnp.int32)
    before = jnp.cumsum(marks, axis=0) - marks
    rank = jnp.sum(before * marks, axis=1)
    slot = owner * capacity + rank
    outgoing = jnp.zeros((devices_all * capacity, 2 * voxels), jnp.float32).at[slot].set(payload)
    labels = jnp.full((devices_all * capacity,), -1.0, jnp.float32).at[slot].set(
        tile_box.astype(jnp.float32)
    )
    label_width = 128
    labels = jnp.pad(labels.reshape(devices_all, capacity), ((0, 0), (0, label_width - capacity)))
    packed = jnp.concatenate(
        [outgoing.reshape(devices_all, capacity * 2 * voxels), labels], axis=1
    )
    arrived = lax.all_to_all(packed, ("bx", "by", "bz"), split_axis=0, concat_axis=0, tiled=True)
    arrived_payload = arrived[:, : capacity * 2 * voxels].reshape(devices_all * capacity, 2 * voxels)
    arrived_ids = arrived[:, capacity * 2 * voxels : capacity * 2 * voxels + capacity].reshape(
        devices_all * capacity
    )
    wanted = (
        jnp.arange(boxes_here, dtype=jnp.float32)[:, None] == arrived_ids[None, :]
    ).astype(jnp.float32)
    sums = jnp.dot(
        wanted, arrived_payload, precision=lax.Precision.HIGHEST, preferred_element_type=jnp.float32
    )
    row_sizes = (local_x, local_y, local_z, BOXX, BOXY, BOXZ)
    lane_sizes = (VX, VY, VZ)
    volume = laue_step(sums, "bx", flip_table(row_sizes, (0, 3)), flip_table(lane_sizes, (0,)))
    volume = laue_step(volume, "by", flip_table(row_sizes, (1, 4)), flip_table(lane_sizes, (1,)))
    volume = laue_step(volume, "bz", flip_table(row_sizes, (2, 5)), flip_table(lane_sizes, (2,)))
    result = volume[:, :voxels] / jnp.maximum(volume[:, voxels:], 1.0)
    return result.reshape(local_x, local_y, local_z, BOX_BRICK, voxels)


def solution(mesh):
    return jax.shard_map(
        shards,
        mesh=mesh,
        in_specs=(
            P(("bx", "by", "bz"), None, None, None),
            P(("bx", "by", "bz"), None, None, None),
            P(("bx", "by", "bz"), None, None, None),
            P(),
            P(),
            P(("bx", "by", "bz")),
            P(("bx", "by", "bz"), None),
            P(("bx", "by", "bz")),
        ),
        out_specs=P("bx", "by", "bz", None, None),
        check_vma=False,
    )
```

```python
import functools

import numpy as np
import jax
import jax.numpy as jnp
from jax import lax
from jax.sharding import PartitionSpec as P
from jax.experimental import pallas as pl
from jax.experimental.pallas import tpu as pltpu

VX = 8
VY = 8
VZ = 4
GX = 8
GY = 8
GZ = 4
BOXX = 4
BOXY = 4
BOXZ = 4
BOX_BRICK = 64


def digits_flipped(index, sizes, flipped):
    result = jnp.zeros_like(index)
    stride = 1
    rest = index
    for dim in reversed(range(len(sizes))):
        digit = rest % sizes[dim]
        rest = rest // sizes[dim]
        if dim in flipped:
            digit = sizes[dim] - 1 - digit
        result = result + digit * stride
        stride = stride * sizes[dim]
    return result


def flip_matrices(row_sizes, lane_sizes, stage):
    rows = int(np.prod(row_sizes))
    lanes = int(np.prod(lane_sizes))
    out_row = lax.broadcasted_iota(jnp.int32, (rows, rows), 0)
    in_row = lax.broadcasted_iota(jnp.int32, (rows, rows), 1)
    row_flip = (in_row == digits_flipped(out_row, row_sizes, (stage, stage + 3))).astype(jnp.float32)
    in_lane = lax.broadcasted_iota(jnp.int32, (lanes, lanes), 0)
    out_lane = lax.broadcasted_iota(jnp.int32, (lanes, lanes), 1)
    lane_flip = (in_lane == digits_flipped(out_lane, lane_sizes, (stage,))).astype(jnp.float32)
    return row_flip, lane_flip


def flipped_volume(volume, row_flip, lane_flip, voxels):
    exact = lax.Precision.HIGHEST
    moved = jnp.dot(row_flip, volume, precision=exact, preferred_element_type=jnp.float32)
    value = jnp.dot(moved[:, :voxels], lane_flip, precision=exact, preferred_element_type=jnp.float32)
    weight = jnp.dot(moved[:, voxels:], lane_flip, precision=exact, preferred_element_type=jnp.float32)
    return value, weight


def laue_kernel(row_sizes, lane_sizes, sums_ref, out_ref, received, held, send_sems, recv_sems):
    voxels = int(np.prod(lane_sizes))
    axes = ("bx", "by", "bz")
    here = tuple(lax.axis_index(axis) for axis in axes)
    sizes = tuple(lax.axis_size(axis) for axis in axes)
    partners = []
    for stage in range(3):
        partner = list(here)
        partner[stage] = sizes[stage] - 1 - here[stage]
        partners.append(tuple(partner))
    remote = [stage for stage in range(3) if sizes[stage] > 1]
    if remote:
        barrier = pltpu.get_barrier_semaphore()
        for stage in remote:
            pl.semaphore_signal(
                barrier, 1, device_id=partners[stage], device_id_type=pl.DeviceIdType.MESH
            )
        pl.semaphore_wait(barrier, len(remote))
    current = sums_ref
    for stage in range(3):
        source = current
        if stage in remote:
            copy = pltpu.make_async_remote_copy(
                src_ref=current,
                dst_ref=received.at[stage],
                send_sem=send_sems.at[stage],
                recv_sem=recv_sems.at[stage],
                device_id=partners[stage],
                device_id_type=pl.DeviceIdType.MESH,
            )
            copy.start()
            copy.wait()
            source = received.at[stage]
        row_flip, lane_flip = flip_matrices(row_sizes, lane_sizes, stage)
        value, weight = flipped_volume(source[...], row_flip, lane_flip, voxels)
        held[stage, :, :voxels] = 0.5 * (current[:, :voxels] + value)
        held[stage, :, voxels:] = 0.5 * (current[:, voxels:] + weight)
        current = held.at[stage]
    out_ref[...] = current[:, :voxels] / jnp.maximum(current[:, voxels:], 1.0)


def laue_average(sums, row_sizes, lane_sizes):
    rows, width = sums.shape
    voxels = width // 2
    return pl.pallas_call(
        functools.partial(laue_kernel, row_sizes, lane_sizes),
        in_specs=[pl.BlockSpec(memory_space=pltpu.VMEM)],
        out_specs=pl.BlockSpec(memory_space=pltpu.VMEM),
        out_shape=jax.ShapeDtypeStruct((rows, voxels), jnp.float32),
        scratch_shapes=[
            pltpu.VMEM((3, rows, width), jnp.float32),
            pltpu.VMEM((3, rows, width), jnp.float32),
            pltpu.SemaphoreType.DMA((3,)),
            pltpu.SemaphoreType.DMA((3,)),
        ],
        compiler_params=pltpu.CompilerParams(collective_id=0, has_side_effects=True),
    )(sums)


def tile_kernel(factor_ref, counts_ref, eff_ref, rows_ref, cols_ref, out_ref):
    block, unused_pixels, voxels = rows_ref.shape
    for t in range(block):
        cols = cols_ref[t]
        rows = rows_ref[t].astype(jnp.float32)
        counted = jnp.dot(counts_ref[t], cols, preferred_element_type=jnp.float32)
        seen = jnp.dot(eff_ref[t], cols, preferred_element_type=jnp.float32)
        value = jnp.sum(rows * counted, axis=0, keepdims=True)
        weight = jnp.sum(rows * seen, axis=0, keepdims=True)
        out_ref[t : t + 1, :voxels] = value * factor_ref[t : t + 1, :]
        out_ref[t : t + 1, voxels:] = weight


def tile_payload(counts, row_split, col_split, efficiency, factor):
    frames_here, tiles_frame, pixels, columns = counts.shape
    voxels = row_split.shape[-1]
    tiles_here = frames_here * tiles_frame
    block = 8
    per_frame = tiles_frame // block
    tile_factor = jnp.repeat(factor, tiles_frame)[:, None]
    return pl.pallas_call(
        tile_kernel,
        grid=(tiles_here // block,),
        in_specs=[
            pl.BlockSpec((block, 1), lambda i: (i, 0)),
            pl.BlockSpec((block, pixels, columns), lambda i: (i, 0, 0)),
            pl.BlockSpec((block, pixels, columns), lambda i: (i % per_frame, 0, 0)),
            pl.BlockSpec((block, pixels, voxels), lambda i: (i, 0, 0)),
            pl.BlockSpec((block, pixels, voxels), lambda i: (i, 0, 0)),
        ],
        out_specs=pl.BlockSpec((block, 2 * voxels), lambda i: (i, 0)),
        out_shape=jax.ShapeDtypeStruct((tiles_here, 2 * voxels), jnp.float32),
    )(
        tile_factor,
        counts.reshape(tiles_here, pixels, columns),
        efficiency,
        row_split.reshape(tiles_here, pixels, voxels),
        col_split.reshape(tiles_here, pixels, voxels),
    )


def shards(counts, row_split, col_split, efficiency, lorentz, angles, tile_owner, tile_box):
    frames_here, tiles_frame, pixels, unused_width = counts.shape
    voxels = row_split.shape[-1]
    size_x = lax.axis_size("bx")
    size_y = lax.axis_size("by")
    size_z = lax.axis_size("bz")
    devices_all = size_x * size_y * size_z
    tiles_here = frames_here * tiles_frame
    capacity = max(4, 4 * tiles_here // devices_all)
    local_x = GX // size_x
    local_y = GY // size_y
    local_z = GZ // size_z
    boxes_here = local_x * local_y * local_z * BOX_BRICK
    picks = angles[:, None] == jnp.arange(lorentz.shape[0], dtype=jnp.int32)[None, :]
    factor = jnp.sum(jnp.where(picks, lorentz[None, :], 0.0), axis=1)
    payload = tile_payload(counts, row_split, col_split, efficiency, factor)
    owner = tile_owner[:, 0]
    marks = (owner[:, None] == jnp.arange(devices_all, dtype=jnp.int32)[None, :]).astype(jnp.int32)
    before = jnp.cumsum(marks, axis=0) - marks
    rank = jnp.sum(before * marks, axis=1)
    slot = owner * capacity + rank
    outgoing = jnp.zeros((devices_all * capacity, 2 * voxels), jnp.float32).at[slot].set(payload)
    labels = jnp.full((devices_all * capacity,), -1.0, jnp.float32).at[slot].set(
        tile_box.astype(jnp.float32)
    )
    label_width = 128
    labels = jnp.pad(labels.reshape(devices_all, capacity), ((0, 0), (0, label_width - capacity)))
    packed = jnp.concatenate(
        [outgoing.reshape(devices_all, capacity * 2 * voxels), labels], axis=1
    )
    arrived = lax.all_to_all(packed, ("bx", "by", "bz"), split_axis=0, concat_axis=0, tiled=True)
    arrived_payload = arrived[:, : capacity * 2 * voxels].reshape(devices_all * capacity, 2 * voxels)
    arrived_ids = arrived[:, capacity * 2 * voxels : capacity * 2 * voxels + capacity].reshape(
        devices_all * capacity
    )
    wanted = (
        jnp.arange(boxes_here, dtype=jnp.float32)[:, None] == arrived_ids[None, :]
    ).astype(jnp.float32)
    sums = jnp.dot(
        wanted, arrived_payload, precision=lax.Precision.HIGHEST, preferred_element_type=jnp.float32
    )
    row_sizes = (local_x, local_y, local_z, BOXX, BOXY, BOXZ)
    lane_sizes = (VX, VY, VZ)
    result = laue_average(sums, row_sizes, lane_sizes)
    return result.reshape(local_x, local_y, local_z, BOX_BRICK, voxels)


def solution(mesh):
    return jax.shard_map(
        shards,
        mesh=mesh,
        in_specs=(
            P(("bx", "by", "bz"), None, None, None),
            P(("bx", "by", "bz"), None, None, None),
            P(("bx", "by", "bz"), None, None, None),
            P(),
            P(),
            P(("bx", "by", "bz")),
            P(("bx", "by", "bz"), None),
            P(("bx", "by", "bz")),
        ),
        out_specs=P("bx", "by", "bz", None, None),
        check_vma=False,
    )
```

```python
import functools

import numpy as np
import jax
import jax.numpy as jnp
from jax import lax
from jax.sharding import PartitionSpec as P
from jax.experimental import pallas as pl
from jax.experimental.pallas import tpu as pltpu

VX = 8
VY = 8
VZ = 4
GX = 8
GY = 8
GZ = 4
BOXX = 4
BOXY = 4
BOXZ = 4
BOX_BRICK = 64


def digits_flipped(index, sizes, flipped):
    result = jnp.zeros_like(index)
    stride = 1
    rest = index
    for dim in reversed(range(len(sizes))):
        digit = rest % sizes[dim]
        rest = rest // sizes[dim]
        if dim in flipped:
            digit = sizes[dim] - 1 - digit
        result = result + digit * stride
        stride = stride * sizes[dim]
    return result


def flip_matrices(row_sizes, lane_sizes, stage):
    rows = int(np.prod(row_sizes))
    lanes = int(np.prod(lane_sizes))
    out_row = lax.broadcasted_iota(jnp.int32, (rows, rows), 0)
    in_row = lax.broadcasted_iota(jnp.int32, (rows, rows), 1)
    row_flip = (in_row == digits_flipped(out_row, row_sizes, (stage, stage + 3))).astype(jnp.float32)
    in_lane = lax.broadcasted_iota(jnp.int32, (lanes, lanes), 0)
    out_lane = lax.broadcasted_iota(jnp.int32, (lanes, lanes), 1)
    lane_flip = (in_lane == digits_flipped(out_lane, lane_sizes, (stage,))).astype(jnp.float32)
    return row_flip, lane_flip


def flipped_volume(volume, row_flip, lane_flip, voxels):
    exact = lax.Precision.HIGHEST
    moved = jnp.dot(row_flip, volume, precision=exact, preferred_element_type=jnp.float32)
    value = jnp.dot(moved[:, :voxels], lane_flip, precision=exact, preferred_element_type=jnp.float32)
    weight = jnp.dot(moved[:, voxels:], lane_flip, precision=exact, preferred_element_type=jnp.float32)
    return value, weight


def laue_kernel(row_sizes, lane_sizes, sums_ref, out_ref, received, held, send_sems, recv_sems):
    voxels = int(np.prod(lane_sizes))
    axes = ("bx", "by", "bz")
    here = tuple(lax.axis_index(axis) for axis in axes)
    sizes = tuple(lax.axis_size(axis) for axis in axes)
    partners = []
    for stage in range(3):
        partner = list(here)
        partner[stage] = sizes[stage] - 1 - here[stage]
        partners.append(tuple(partner))
    remote = [stage for stage in range(3) if sizes[stage] > 1]
    if remote:
        barrier = pltpu.get_barrier_semaphore()
        for stage in remote:
            pl.semaphore_signal(
                barrier, 1, device_id=partners[stage], device_id_type=pl.DeviceIdType.MESH
            )
        pl.semaphore_wait(barrier, len(remote))
    current = sums_ref
    for stage in range(3):
        source = current
        if stage in remote:
            copy = pltpu.make_async_remote_copy(
                src_ref=current,
                dst_ref=received.at[stage],
                send_sem=send_sems.at[stage],
                recv_sem=recv_sems.at[stage],
                device_id=partners[stage],
                device_id_type=pl.DeviceIdType.MESH,
            )
            copy.start()
            copy.wait()
            source = received.at[stage]
        row_flip, lane_flip = flip_matrices(row_sizes, lane_sizes, stage)
        value, weight = flipped_volume(source[...], row_flip, lane_flip, voxels)
        held[stage, :, :voxels] = 0.5 * (current[:, :voxels] + value)
        held[stage, :, voxels:] = 0.5 * (current[:, voxels:] + weight)
        current = held.at[stage]
    out_ref[...] = current[:, :voxels] / jnp.maximum(current[:, voxels:], 1.0)


def laue_average(sums, row_sizes, lane_sizes):
    rows, width = sums.shape
    voxels = width // 2
    return pl.pallas_call(
        functools.partial(laue_kernel, row_sizes, lane_sizes),
        in_specs=[pl.BlockSpec(memory_space=pltpu.VMEM)],
        out_specs=pl.BlockSpec(memory_space=pltpu.VMEM),
        out_shape=jax.ShapeDtypeStruct((rows, voxels), jnp.float32),
        scratch_shapes=[
            pltpu.VMEM((3, rows, width), jnp.float32),
            pltpu.VMEM((3, rows, width), jnp.float32),
            pltpu.SemaphoreType.DMA((3,)),
            pltpu.SemaphoreType.DMA((3,)),
        ],
        compiler_params=pltpu.CompilerParams(collective_id=0, has_side_effects=True),
    )(sums)


def tile_kernel(factor_ref, counts_ref, eff_ref, rows_ref, cols_ref, out_ref):
    block, unused_pixels, voxels = rows_ref.shape
    for t in range(block):
        cols = cols_ref[t]
        rows = rows_ref[t].astype(jnp.float32)
        counted = jnp.dot(counts_ref[t], cols, preferred_element_type=jnp.float32)
        seen = jnp.dot(eff_ref[t], cols, preferred_element_type=jnp.float32)
        value = jnp.sum(rows * counted, axis=0, keepdims=True)
        weight = jnp.sum(rows * seen, axis=0, keepdims=True)
        out_ref[t : t + 1, :voxels] = value * factor_ref[t : t + 1, :]
        out_ref[t : t + 1, voxels:] = weight


def tile_payload(counts, row_split, col_split, efficiency, factor):
    frames_here, tiles_frame, pixels, columns = counts.shape
    voxels = row_split.shape[-1]
    tiles_here = frames_here * tiles_frame
    block = 8
    per_frame = tiles_frame // block
    tile_factor = jnp.repeat(factor, tiles_frame)[:, None]
    return pl.pallas_call(
        tile_kernel,
        grid=(tiles_here // block,),
        in_specs=[
            pl.BlockSpec((block, 1), lambda i: (i, 0)),
            pl.BlockSpec((block, pixels, columns), lambda i: (i, 0, 0)),
            pl.BlockSpec((block, pixels, columns), lambda i: (i % per_frame, 0, 0)),
            pl.BlockSpec((block, pixels, voxels), lambda i: (i, 0, 0)),
            pl.BlockSpec((block, pixels, voxels), lambda i: (i, 0, 0)),
        ],
        out_specs=pl.BlockSpec((block, 2 * voxels), lambda i: (i, 0)),
        out_shape=jax.ShapeDtypeStruct((tiles_here, 2 * voxels), jnp.float32),
    )(
        tile_factor,
        counts.reshape(tiles_here, pixels, columns),
        efficiency,
        row_split.reshape(tiles_here, pixels, voxels),
        col_split.reshape(tiles_here, pixels, voxels),
    )


def flat_device(flat, sizes):
    return (flat // (sizes[1] * sizes[2]), (flat // sizes[2]) % sizes[1], flat % sizes[2])


def exchange_kernel(packed_ref, arrived_ref, inbox, send_sem, recv_sem):
    axes = ("bx", "by", "bz")
    sizes = tuple(lax.axis_size(axis) for axis in axes)
    count = sizes[0] * sizes[1] * sizes[2]
    me = (lax.axis_index("bx") * sizes[1] + lax.axis_index("by")) * sizes[2] + lax.axis_index("bz")
    barrier = pltpu.get_barrier_semaphore()

    def greet(step, carry):
        target = flat_device((me + step) % count, sizes)
        pl.semaphore_signal(barrier, 1, device_id=target, device_id_type=pl.DeviceIdType.MESH)
        return carry

    lax.fori_loop(1, count, greet, 0)
    pl.semaphore_wait(barrier, count - 1)

    def send(step, carry):
        target = (me + step) % count
        pltpu.make_async_remote_copy(
            src_ref=packed_ref.at[target],
            dst_ref=inbox.at[me],
            send_sem=send_sem,
            recv_sem=recv_sem,
            device_id=flat_device(target, sizes),
            device_id_type=pl.DeviceIdType.MESH,
        ).start()
        return carry

    lax.fori_loop(1, count, send, 0)
    every = pltpu.make_async_remote_copy(
        src_ref=packed_ref.at[pl.ds(0, count - 1)],
        dst_ref=inbox.at[pl.ds(0, count - 1)],
        send_sem=send_sem,
        recv_sem=recv_sem,
        device_id=flat_device((me + 1) % count, sizes),
        device_id_type=pl.DeviceIdType.MESH,
    )
    every.wait_send()
    every.wait_recv()
    arrived_ref[...] = inbox[...]
    arrived_ref[me] = packed_ref[me]


def exchange(packed):
    return pl.pallas_call(
        exchange_kernel,
        in_specs=[pl.BlockSpec(memory_space=pltpu.VMEM)],
        out_specs=pl.BlockSpec(memory_space=pltpu.VMEM),
        out_shape=jax.ShapeDtypeStruct(packed.shape, packed.dtype),
        scratch_shapes=[
            pltpu.VMEM(packed.shape, packed.dtype),
            pltpu.SemaphoreType.DMA(()),
            pltpu.SemaphoreType.DMA(()),
        ],
        compiler_params=pltpu.CompilerParams(collective_id=1, has_side_effects=True),
    )(packed)


def shards(counts, row_split, col_split, efficiency, lorentz, angles, tile_owner, tile_box):
    frames_here, tiles_frame, pixels, unused_width = counts.shape
    voxels = row_split.shape[-1]
    size_x = lax.axis_size("bx")
    size_y = lax.axis_size("by")
    size_z = lax.axis_size("bz")
    devices_all = size_x * size_y * size_z
    tiles_here = frames_here * tiles_frame
    capacity = max(4, 4 * tiles_here // devices_all)
    local_x = GX // size_x
    local_y = GY // size_y
    local_z = GZ // size_z
    boxes_here = local_x * local_y * local_z * BOX_BRICK
    picks = angles[:, None] == jnp.arange(lorentz.shape[0], dtype=jnp.int32)[None, :]
    factor = jnp.sum(jnp.where(picks, lorentz[None, :], 0.0), axis=1)
    payload = tile_payload(counts, row_split, col_split, efficiency, factor)
    owner = tile_owner[:, 0]
    marks = (owner[:, None] == jnp.arange(devices_all, dtype=jnp.int32)[None, :]).astype(jnp.int32)
    before = jnp.cumsum(marks, axis=0) - marks
    rank = jnp.sum(before * marks, axis=1)
    slot = owner * capacity + rank
    outgoing = jnp.zeros((devices_all * capacity, 2 * voxels), jnp.float32).at[slot].set(payload)
    arrived = exchange(outgoing.reshape(devices_all, capacity * 2, voxels))
    arrived_payload = arrived.reshape(devices_all * capacity, 2 * voxels)
    ids = jnp.concatenate([owner, tile_box])
    everyone = lax.all_gather(ids, ("bx", "by", "bz"), tiled=True).reshape(devices_all, 2, tiles_here)
    me = (lax.axis_index("bx") * size_y + lax.axis_index("by")) * size_z + lax.axis_index("bz")
    mine = everyone[:, 0, :] == me
    order = jnp.cumsum(mine.astype(jnp.int32), axis=1) - 1
    labels = []
    for k in range(capacity):
        hit = mine & (order == k)
        found = jnp.sum(jnp.where(hit, everyone[:, 1, :], 0), axis=1)
        labels.append(jnp.where(jnp.any(hit, axis=1), found, -1))
    arrived_ids = jnp.stack(labels, axis=1).reshape(devices_all * capacity)
    wanted = (
        jnp.arange(boxes_here, dtype=jnp.int32)[:, None] == arrived_ids[None, :]
    ).astype(jnp.float32)
    sums = jnp.dot(
        wanted, arrived_payload, precision=lax.Precision.HIGHEST, preferred_element_type=jnp.float32
    )
    row_sizes = (local_x, local_y, local_z, BOXX, BOXY, BOXZ)
    lane_sizes = (VX, VY, VZ)
    result = laue_average(sums, row_sizes, lane_sizes)
    return result.reshape(local_x, local_y, local_z, BOX_BRICK, voxels)


def solution(mesh):
    return jax.shard_map(
        shards,
        mesh=mesh,
        in_specs=(
            P(("bx", "by", "bz"), None, None, None),
            P(("bx", "by", "bz"), None, None, None),
            P(("bx", "by", "bz"), None, None, None),
            P(),
            P(),
            P(("bx", "by", "bz")),
            P(("bx", "by", "bz"), None),
            P(("bx", "by", "bz")),
        ),
        out_specs=P("bx", "by", "bz", None, None),
        check_vma=False,
    )
```

```python
import functools

import numpy as np
import jax
import jax.numpy as jnp
from jax import lax
from jax.sharding import PartitionSpec as P
from jax.experimental import pallas as pl
from jax.experimental.pallas import tpu as pltpu

VX = 8
VY = 8
VZ = 4
GX = 8
GY = 8
GZ = 4
BOXX = 4
BOXY = 4
BOXZ = 4
BOX_BRICK = 64


def digits_flipped(index, sizes, flipped):
    result = jnp.zeros_like(index)
    stride = 1
    rest = index
    for dim in reversed(range(len(sizes))):
        digit = rest % sizes[dim]
        rest = rest // sizes[dim]
        if dim in flipped:
            digit = sizes[dim] - 1 - digit
        result = result + digit * stride
        stride = stride * sizes[dim]
    return result


def flip_matrices(row_sizes, lane_sizes, stage):
    rows = int(np.prod(row_sizes))
    lanes = int(np.prod(lane_sizes))
    out_row = lax.broadcasted_iota(jnp.int32, (rows, rows), 0)
    in_row = lax.broadcasted_iota(jnp.int32, (rows, rows), 1)
    row_flip = (in_row == digits_flipped(out_row, row_sizes, (stage, stage + 3))).astype(jnp.float32)
    in_lane = lax.broadcasted_iota(jnp.int32, (lanes, lanes), 0)
    out_lane = lax.broadcasted_iota(jnp.int32, (lanes, lanes), 1)
    lane_flip = (in_lane == digits_flipped(out_lane, lane_sizes, (stage,))).astype(jnp.float32)
    return row_flip, lane_flip


def flipped(pair, row_sizes, lane_sizes, stage):
    exact = lax.Precision.HIGHEST
    row_flip, lane_flip = flip_matrices(row_sizes, lane_sizes, stage)
    result = []
    for half in pair:
        moved = jnp.dot(row_flip, half, precision=exact, preferred_element_type=jnp.float32)
        result.append(jnp.dot(moved, lane_flip, precision=exact, preferred_element_type=jnp.float32))
    return result


def averaged(pair, other):
    return [0.5 * (mine + moved) for mine, moved in zip(pair, other)]


def laue_kernel(row_sizes, lane_sizes, sums_ref, out_ref, received, held, send_sems, recv_sems):
    voxels = int(np.prod(lane_sizes))
    axes = ("bx", "by", "bz")
    here = tuple(lax.axis_index(axis) for axis in axes)
    sizes = tuple(lax.axis_size(axis) for axis in axes)

    def mirror(flags):
        return tuple(sizes[a] - 1 - here[a] if flags[a] else here[a] for a in range(3))

    first = (mirror((1, 0, 0)), mirror((0, 1, 0)), mirror((1, 1, 0)))
    last = mirror((0, 0, 1))
    barrier = pltpu.get_barrier_semaphore()
    for target in first + (last,):
        pl.semaphore_signal(barrier, 1, device_id=target, device_id_type=pl.DeviceIdType.MESH)
    pl.semaphore_wait(barrier, 4)

    def send(source, slot, target):
        copy = pltpu.make_async_remote_copy(
            src_ref=source,
            dst_ref=received.at[slot],
            send_sem=send_sems.at[slot],
            recv_sem=recv_sems.at[slot],
            device_id=target,
            device_id_type=pl.DeviceIdType.MESH,
        )
        copy.start()
        return copy

    copies = [send(sums_ref, slot, target) for slot, target in enumerate(first)]
    for copy in copies:
        copy.wait()

    def halves(ref):
        return [ref[:, :voxels], ref[:, voxels:]]

    stage_x = averaged(halves(sums_ref), flipped(halves(received.at[0]), row_sizes, lane_sizes, 0))
    stage_x_there = averaged(
        halves(received.at[1]), flipped(halves(received.at[2]), row_sizes, lane_sizes, 0)
    )
    stage_y = averaged(stage_x, flipped(stage_x_there, row_sizes, lane_sizes, 1))
    held[:, :voxels] = stage_y[0]
    held[:, voxels:] = stage_y[1]
    copy = send(held, 3, last)
    copy.wait()
    stage_z = averaged(halves(held), flipped(halves(received.at[3]), row_sizes, lane_sizes, 2))
    out_ref[...] = stage_z[0] / jnp.maximum(stage_z[1], 1.0)


def laue_average(sums, row_sizes, lane_sizes):
    rows, width = sums.shape
    voxels = width // 2
    return pl.pallas_call(
        functools.partial(laue_kernel, row_sizes, lane_sizes),
        in_specs=[pl.BlockSpec(memory_space=pltpu.VMEM)],
        out_specs=pl.BlockSpec(memory_space=pltpu.VMEM),
        out_shape=jax.ShapeDtypeStruct((rows, voxels), jnp.float32),
        scratch_shapes=[
            pltpu.VMEM((4, rows, width), jnp.float32),
            pltpu.VMEM((rows, width), jnp.float32),
            pltpu.SemaphoreType.DMA((4,)),
            pltpu.SemaphoreType.DMA((4,)),
        ],
        compiler_params=pltpu.CompilerParams(collective_id=0, has_side_effects=True),
    )(sums)


def tile_kernel(tiles_frame, factor_ref, counts_ref, eff_ref, rows_ref, cols_ref, out_ref):
    block, unused_pixels, voxels = rows_ref.shape
    factor = factor_ref[(pl.program_id(0) * block) // tiles_frame]

    def one_tile(t, carry):
        cols = cols_ref[t]
        rows = rows_ref[t].astype(jnp.float32)
        counted = jnp.dot(counts_ref[t], cols, preferred_element_type=jnp.float32)
        seen = jnp.dot(eff_ref[t], cols, preferred_element_type=jnp.float32)
        value = jnp.sum(rows * counted, axis=0, keepdims=True)
        weight = jnp.sum(rows * seen, axis=0, keepdims=True)
        out_ref[pl.ds(t, 1), :voxels] = value * factor
        out_ref[pl.ds(t, 1), voxels:] = weight
        return carry

    lax.fori_loop(0, block, one_tile, 0, unroll=2)


def tile_payload(counts, row_split, col_split, efficiency, factor):
    frames_here, tiles_frame, pixels, columns = counts.shape
    voxels = row_split.shape[-1]
    tiles_here = frames_here * tiles_frame
    block = 32
    per_frame = tiles_frame // block
    return pl.pallas_call(
        functools.partial(tile_kernel, tiles_frame),
        grid_spec=pltpu.PrefetchScalarGridSpec(
            num_scalar_prefetch=1,
            grid=(tiles_here // block,),
            in_specs=[
                pl.BlockSpec((block, pixels, columns), lambda i, f: (i, 0, 0)),
                pl.BlockSpec((block, pixels, columns), lambda i, f: (i % per_frame, 0, 0)),
                pl.BlockSpec((block, pixels, voxels), lambda i, f: (i, 0, 0)),
                pl.BlockSpec((block, pixels, voxels), lambda i, f: (i, 0, 0)),
            ],
            out_specs=pl.BlockSpec((block, 2 * voxels), lambda i, f: (i, 0)),
        ),
        out_shape=jax.ShapeDtypeStruct((tiles_here, 2 * voxels), jnp.float32),
    )(
        factor,
        counts.reshape(tiles_here, pixels, columns),
        efficiency,
        row_split.reshape(tiles_here, pixels, voxels),
        col_split.reshape(tiles_here, pixels, voxels),
    )


def shards(counts, row_split, col_split, efficiency, lorentz, angles, tile_owner, tile_box):
    frames_here, tiles_frame, pixels, unused_width = counts.shape
    voxels = row_split.shape[-1]
    size_x = lax.axis_size("bx")
    size_y = lax.axis_size("by")
    size_z = lax.axis_size("bz")
    devices_all = size_x * size_y * size_z
    tiles_here = frames_here * tiles_frame
    capacity = max(4, 4 * tiles_here // devices_all)
    local_x = GX // size_x
    local_y = GY // size_y
    local_z = GZ // size_z
    boxes_here = local_x * local_y * local_z * BOX_BRICK
    picks = angles[:, None] == jnp.arange(lorentz.shape[0], dtype=jnp.int32)[None, :]
    factor = jnp.sum(jnp.where(picks, lorentz[None, :], 0.0), axis=1)
    payload = tile_payload(counts, row_split, col_split, efficiency, factor)
    owner = tile_owner[:, 0]
    marks = (owner[:, None] == jnp.arange(devices_all, dtype=jnp.int32)[None, :]).astype(jnp.int32)
    before = jnp.cumsum(marks, axis=0) - marks
    rank = jnp.sum(before * marks, axis=1)
    slot = owner * capacity + rank
    outgoing = jnp.zeros((devices_all * capacity, 2 * voxels), jnp.float32).at[slot].set(payload)
    labels = jnp.full((devices_all * capacity,), -1.0, jnp.float32).at[slot].set(
        tile_box.astype(jnp.float32)
    )
    label_width = 128
    labels = jnp.pad(labels.reshape(devices_all, capacity), ((0, 0), (0, label_width - capacity)))
    packed = jnp.concatenate(
        [outgoing.reshape(devices_all, capacity * 2 * voxels), labels], axis=1
    )
    arrived = lax.all_to_all(packed, ("bx", "by", "bz"), split_axis=0, concat_axis=0, tiled=True)
    arrived_payload = arrived[:, : capacity * 2 * voxels].reshape(devices_all * capacity, 2 * voxels)
    arrived_ids = arrived[:, capacity * 2 * voxels : capacity * 2 * voxels + capacity].reshape(
        devices_all * capacity
    )
    wanted = (
        jnp.arange(boxes_here, dtype=jnp.float32)[:, None] == arrived_ids[None, :]
    ).astype(jnp.float32)
    sums = jnp.dot(
        wanted, arrived_payload, precision=lax.Precision.HIGHEST, preferred_element_type=jnp.float32
    )
    row_sizes = (local_x, local_y, local_z, BOXX, BOXY, BOXZ)
    lane_sizes = (VX, VY, VZ)
    result = laue_average(sums, row_sizes, lane_sizes)
    return result.reshape(local_x, local_y, local_z, BOX_BRICK, voxels)


def solution(mesh):
    return jax.shard_map(
        shards,
        mesh=mesh,
        in_specs=(
            P(("bx", "by", "bz"), None, None, None),
            P(("bx", "by", "bz"), None, None, None),
            P(("bx", "by", "bz"), None, None, None),
            P(),
            P(),
            P(("bx", "by", "bz")),
            P(("bx", "by", "bz"), None),
            P(("bx", "by", "bz")),
        ),
        out_specs=P("bx", "by", "bz", None, None),
        check_vma=False,
    )
```

```python
import functools

import numpy as np
import jax
import jax.numpy as jnp
from jax import lax
from jax.sharding import PartitionSpec as P
from jax.experimental import pallas as pl
from jax.experimental.pallas import tpu as pltpu

VX = 8
VY = 8
VZ = 4
GX = 8
GY = 8
GZ = 4
BOXX = 4
BOXY = 4
BOXZ = 4
BOX_BRICK = 64


def flip_mask(sizes, flipped):
    mask, stride = 0, 1
    for dim in reversed(range(len(sizes))):
        assert sizes[dim] & (sizes[dim] - 1) == 0
        if dim in flipped:
            mask |= (sizes[dim] - 1) * stride
        stride *= sizes[dim]
    return mask


def flip_matrices(row_sizes, lane_sizes, stage):
    rows = int(np.prod(row_sizes))
    lanes = int(np.prod(lane_sizes))
    out_row = lax.broadcasted_iota(jnp.int32, (rows, rows), 0)
    in_row = lax.broadcasted_iota(jnp.int32, (rows, rows), 1)
    row_flip = (in_row == (out_row ^ flip_mask(row_sizes, (stage, stage + 3)))).astype(jnp.float32)
    in_lane = lax.broadcasted_iota(jnp.int32, (lanes, lanes), 0)
    out_lane = lax.broadcasted_iota(jnp.int32, (lanes, lanes), 1)
    lane_flip = (in_lane == (out_lane ^ flip_mask(lane_sizes, (stage,)))).astype(jnp.float32)
    return row_flip, lane_flip


def flipped(pair, row_sizes, lane_sizes, stage):
    exact = lax.Precision.HIGHEST
    row_flip, lane_flip = flip_matrices(row_sizes, lane_sizes, stage)
    result = []
    for half in pair:
        moved = jnp.dot(row_flip, half, precision=exact, preferred_element_type=jnp.float32)
        result.append(jnp.dot(moved, lane_flip, precision=exact, preferred_element_type=jnp.float32))
    return result


def averaged(pair, other):
    return [0.5 * (mine + moved) for mine, moved in zip(pair, other)]


def laue_kernel(row_sizes, lane_sizes, sums_ref, out_ref, received, held, send_sems, recv_sems):
    voxels = int(np.prod(lane_sizes))
    axes = ("bx", "by", "bz")
    here = tuple(lax.axis_index(axis) for axis in axes)
    sizes = tuple(lax.axis_size(axis) for axis in axes)

    def mirror(flags):
        return tuple(sizes[a] - 1 - here[a] if flags[a] else here[a] for a in range(3))

    first = (mirror((1, 0, 0)), mirror((0, 1, 0)), mirror((1, 1, 0)))
    last = mirror((0, 0, 1))
    barrier = pltpu.get_barrier_semaphore()
    for target in first + (last,):
        pl.semaphore_signal(barrier, 1, device_id=target, device_id_type=pl.DeviceIdType.MESH)
    pl.semaphore_wait(barrier, 4)

    def send(source, slot, target):
        copy = pltpu.make_async_remote_copy(
            src_ref=source,
            dst_ref=received.at[slot],
            send_sem=send_sems.at[slot],
            recv_sem=recv_sems.at[slot],
            device_id=target,
            device_id_type=pl.DeviceIdType.MESH,
        )
        copy.start()
        return copy

    copies = [send(sums_ref, slot, target) for slot, target in enumerate(first)]
    for copy in copies:
        copy.wait()

    def halves(ref):
        return [ref[:, :voxels], ref[:, voxels:]]

    stage_x = averaged(halves(sums_ref), flipped(halves(received.at[0]), row_sizes, lane_sizes, 0))
    stage_x_there = averaged(
        halves(received.at[1]), flipped(halves(received.at[2]), row_sizes, lane_sizes, 0)
    )
    stage_y = averaged(stage_x, flipped(stage_x_there, row_sizes, lane_sizes, 1))
    held[:, :voxels] = stage_y[0]
    held[:, voxels:] = stage_y[1]
    copy = send(held, 3, last)
    copy.wait()
    stage_z = averaged(halves(held), flipped(halves(received.at[3]), row_sizes, lane_sizes, 2))
    out_ref[...] = stage_z[0] / jnp.maximum(stage_z[1], 1.0)


def laue_average(sums, row_sizes, lane_sizes):
    rows, width = sums.shape
    voxels = width // 2
    return pl.pallas_call(
        functools.partial(laue_kernel, row_sizes, lane_sizes),
        in_specs=[pl.BlockSpec(memory_space=pltpu.VMEM)],
        out_specs=pl.BlockSpec(memory_space=pltpu.VMEM),
        out_shape=jax.ShapeDtypeStruct((rows, voxels), jnp.float32),
        scratch_shapes=[
            pltpu.VMEM((4, rows, width), jnp.float32),
            pltpu.VMEM((rows, width), jnp.float32),
            pltpu.SemaphoreType.DMA((4,)),
            pltpu.SemaphoreType.DMA((4,)),
        ],
        compiler_params=pltpu.CompilerParams(collective_id=0, has_side_effects=True),
    )(sums)


def tile_kernel(factor_ref, counts_ref, eff_ref, rows_ref, cols_ref, out_ref):
    block, unused_pixels, voxels = rows_ref.shape
    for t in range(block):
        cols = cols_ref[t]
        rows = rows_ref[t].astype(jnp.float32)
        counted = jnp.dot(counts_ref[t], cols, preferred_element_type=jnp.float32)
        seen = jnp.dot(eff_ref[t], cols, preferred_element_type=jnp.float32)
        value = jnp.sum(rows * counted, axis=0, keepdims=True)
        weight = jnp.sum(rows * seen, axis=0, keepdims=True)
        out_ref[t : t + 1, :voxels] = value * factor_ref[t : t + 1, :]
        out_ref[t : t + 1, voxels:] = weight


def tile_payload(counts, row_split, col_split, efficiency, factor):
    frames_here, tiles_frame, pixels, columns = counts.shape
    voxels = row_split.shape[-1]
    tiles_here = frames_here * tiles_frame
    block = 8
    per_frame = tiles_frame // block
    tile_factor = jnp.repeat(factor, tiles_frame)[:, None]
    return pl.pallas_call(
        tile_kernel,
        grid=(tiles_here // block,),
        in_specs=[
            pl.BlockSpec((block, 1), lambda i: (i, 0)),
            pl.BlockSpec((block, pixels, columns), lambda i: (i, 0, 0)),
            pl.BlockSpec((block, pixels, columns), lambda i: (i % per_frame, 0, 0)),
            pl.BlockSpec((block, pixels, voxels), lambda i: (i, 0, 0)),
            pl.BlockSpec((block, pixels, voxels), lambda i: (i, 0, 0)),
        ],
        out_specs=pl.BlockSpec((block, 2 * voxels), lambda i: (i, 0)),
        out_shape=jax.ShapeDtypeStruct((tiles_here, 2 * voxels), jnp.float32),
    )(
        tile_factor,
        counts.reshape(tiles_here, pixels, columns),
        efficiency,
        row_split.reshape(tiles_here, pixels, voxels),
        col_split.reshape(tiles_here, pixels, voxels),
    )


def shards(counts, row_split, col_split, efficiency, lorentz, angles, tile_owner, tile_box):
    frames_here, tiles_frame, pixels, unused_width = counts.shape
    voxels = row_split.shape[-1]
    size_x = lax.axis_size("bx")
    size_y = lax.axis_size("by")
    size_z = lax.axis_size("bz")
    devices_all = size_x * size_y * size_z
    tiles_here = frames_here * tiles_frame
    capacity = max(4, 4 * tiles_here // devices_all)
    local_x = GX // size_x
    local_y = GY // size_y
    local_z = GZ // size_z
    boxes_here = local_x * local_y * local_z * BOX_BRICK
    picks = angles[:, None] == jnp.arange(lorentz.shape[0], dtype=jnp.int32)[None, :]
    factor = jnp.sum(jnp.where(picks, lorentz[None, :], 0.0), axis=1)
    payload = tile_payload(counts, row_split, col_split, efficiency, factor)
    owner = tile_owner[:, 0]
    marks = (owner[:, None] == jnp.arange(devices_all, dtype=jnp.int32)[None, :]).astype(jnp.int32)
    before = jnp.cumsum(marks, axis=0) - marks
    rank = jnp.sum(before * marks, axis=1)
    slot = owner * capacity + rank
    outgoing = jnp.zeros((devices_all * capacity, 2 * voxels), jnp.float32).at[slot].set(payload)
    labels = jnp.full((devices_all * capacity,), -1.0, jnp.float32).at[slot].set(
        tile_box.astype(jnp.float32)
    )
    label_width = 128
    labels = jnp.pad(labels.reshape(devices_all, capacity), ((0, 0), (0, label_width - capacity)))
    packed = jnp.concatenate(
        [outgoing.reshape(devices_all, capacity * 2 * voxels), labels], axis=1
    )
    arrived = lax.all_to_all(packed, ("bx", "by", "bz"), split_axis=0, concat_axis=0, tiled=True)
    arrived_payload = arrived[:, : capacity * 2 * voxels].reshape(devices_all * capacity, 2 * voxels)
    arrived_ids = arrived[:, capacity * 2 * voxels : capacity * 2 * voxels + capacity].reshape(
        devices_all * capacity
    )
    wanted = (
        jnp.arange(boxes_here, dtype=jnp.float32)[:, None] == arrived_ids[None, :]
    ).astype(jnp.float32)
    sums = jnp.dot(
        wanted, arrived_payload, precision=lax.Precision.HIGHEST, preferred_element_type=jnp.float32
    )
    row_sizes = (local_x, local_y, local_z, BOXX, BOXY, BOXZ)
    lane_sizes = (VX, VY, VZ)
    result = laue_average(sums, row_sizes, lane_sizes)
    return result.reshape(local_x, local_y, local_z, BOX_BRICK, voxels)


def solution(mesh):
    return jax.shard_map(
        shards,
        mesh=mesh,
        in_specs=(
            P(("bx", "by", "bz"), None, None, None),
            P(("bx", "by", "bz"), None, None, None),
            P(("bx", "by", "bz"), None, None, None),
            P(),
            P(),
            P(("bx", "by", "bz")),
            P(("bx", "by", "bz"), None),
            P(("bx", "by", "bz")),
        ),
        out_specs=P("bx", "by", "bz", None, None),
        check_vma=False,
    )
```

```python
import functools

import numpy as np
import jax
import jax.numpy as jnp
from jax import lax
from jax.sharding import PartitionSpec as P
from jax.experimental import pallas as pl
from jax.experimental.pallas import tpu as pltpu

VX = 8
VY = 8
VZ = 4
GX = 8
GY = 8
GZ = 4
BOXX = 4
BOXY = 4
BOXZ = 4
BOX_BRICK = 64


def flip_mask(sizes, flipped):
    mask, stride = 0, 1
    for dim in reversed(range(len(sizes))):
        assert sizes[dim] & (sizes[dim] - 1) == 0
        if dim in flipped:
            mask |= (sizes[dim] - 1) * stride
        stride *= sizes[dim]
    return mask


def flip_matrices(row_sizes, lane_sizes, stage):
    rows = int(np.prod(row_sizes))
    lanes = int(np.prod(lane_sizes))
    out_row = lax.broadcasted_iota(jnp.int32, (rows, rows), 0)
    in_row = lax.broadcasted_iota(jnp.int32, (rows, rows), 1)
    row_flip = (in_row == (out_row ^ flip_mask(row_sizes, (stage, stage + 3)))).astype(jnp.float32)
    in_lane = lax.broadcasted_iota(jnp.int32, (lanes, lanes), 0)
    out_lane = lax.broadcasted_iota(jnp.int32, (lanes, lanes), 1)
    lane_flip = (in_lane == (out_lane ^ flip_mask(lane_sizes, (stage,)))).astype(jnp.float32)
    return row_flip, lane_flip


def split_three(x):
    hi = x.astype(jnp.bfloat16)
    rest = x - hi.astype(jnp.float32)
    mid = rest.astype(jnp.bfloat16)
    lo = (rest - mid.astype(jnp.float32)).astype(jnp.bfloat16)
    return hi, mid, lo


def flipped(pair, row_sizes, lane_sizes, stage):
    row_flip, lane_flip = flip_matrices(row_sizes, lane_sizes, stage)
    row_flip = row_flip.astype(jnp.bfloat16)
    lane_flip = lane_flip.astype(jnp.bfloat16)
    result = []
    for half in pair:
        parts = []
        for piece in split_three(half):
            moved = jnp.dot(row_flip, piece, preferred_element_type=jnp.float32).astype(jnp.bfloat16)
            parts.append(jnp.dot(moved, lane_flip, preferred_element_type=jnp.float32))
        result.append((parts[0] + parts[1]) + parts[2])
    return result


def averaged(pair, other):
    return [0.5 * (mine + moved) for mine, moved in zip(pair, other)]


def laue_kernel(row_sizes, lane_sizes, sums_ref, out_ref, received, held, send_sems, recv_sems):
    voxels = int(np.prod(lane_sizes))
    axes = ("bx", "by", "bz")
    here = tuple(lax.axis_index(axis) for axis in axes)
    sizes = tuple(lax.axis_size(axis) for axis in axes)

    def mirror(flags):
        return tuple(sizes[a] - 1 - here[a] if flags[a] else here[a] for a in range(3))

    first = (mirror((1, 0, 0)), mirror((0, 1, 0)), mirror((1, 1, 0)))
    last = mirror((0, 0, 1))
    barrier = pltpu.get_barrier_semaphore()
    for target in first + (last,):
        pl.semaphore_signal(barrier, 1, device_id=target, device_id_type=pl.DeviceIdType.MESH)
    pl.semaphore_wait(barrier, 4)

    def send(source, slot, target):
        copy = pltpu.make_async_remote_copy(
            src_ref=source,
            dst_ref=received.at[slot],
            send_sem=send_sems.at[slot],
            recv_sem=recv_sems.at[slot],
            device_id=target,
            device_id_type=pl.DeviceIdType.MESH,
        )
        copy.start()
        return copy

    copies = [send(sums_ref, slot, target) for slot, target in enumerate(first)]
    for copy in copies:
        copy.wait()

    def halves(ref):
        return [ref[:, :voxels], ref[:, voxels:]]

    stage_x = averaged(halves(sums_ref), flipped(halves(received.at[0]), row_sizes, lane_sizes, 0))
    stage_x_there = averaged(
        halves(received.at[1]), flipped(halves(received.at[2]), row_sizes, lane_sizes, 0)
    )
    stage_y = averaged(stage_x, flipped(stage_x_there, row_sizes, lane_sizes, 1))
    held[:, :voxels] = stage_y[0]
    held[:, voxels:] = stage_y[1]
    copy = send(held, 3, last)
    copy.wait()
    stage_z = averaged(halves(held), flipped(halves(received.at[3]), row_sizes, lane_sizes, 2))
    out_ref[...] = stage_z[0] / jnp.maximum(stage_z[1], 1.0)


def laue_average(sums, row_sizes, lane_sizes):
    rows, width = sums.shape
    voxels = width // 2
    return pl.pallas_call(
        functools.partial(laue_kernel, row_sizes, lane_sizes),
        in_specs=[pl.BlockSpec(memory_space=pltpu.VMEM)],
        out_specs=pl.BlockSpec(memory_space=pltpu.VMEM),
        out_shape=jax.ShapeDtypeStruct((rows, voxels), jnp.float32),
        scratch_shapes=[
            pltpu.VMEM((4, rows, width), jnp.float32),
            pltpu.VMEM((rows, width), jnp.float32),
            pltpu.SemaphoreType.DMA((4,)),
            pltpu.SemaphoreType.DMA((4,)),
        ],
        compiler_params=pltpu.CompilerParams(collective_id=0, has_side_effects=True),
    )(sums)


def tile_kernel(factor_ref, counts_ref, eff_ref, rows_ref, cols_ref, out_ref):
    block, unused_pixels, voxels = rows_ref.shape
    for t in range(block):
        cols = cols_ref[t]
        rows = rows_ref[t].astype(jnp.float32)
        counted = jnp.dot(counts_ref[t], cols, preferred_element_type=jnp.float32)
        seen = jnp.dot(eff_ref[t], cols, preferred_element_type=jnp.float32)
        value = jnp.sum(rows * counted, axis=0, keepdims=True)
        weight = jnp.sum(rows * seen, axis=0, keepdims=True)
        out_ref[t : t + 1, :voxels] = value * factor_ref[t : t + 1, :]
        out_ref[t : t + 1, voxels:] = weight


def tile_payload(counts, row_split, col_split, efficiency, factor):
    frames_here, tiles_frame, pixels, columns = counts.shape
    voxels = row_split.shape[-1]
    tiles_here = frames_here * tiles_frame
    block = 8
    per_frame = tiles_frame // block
    tile_factor = jnp.repeat(factor, tiles_frame)[:, None]
    return pl.pallas_call(
        tile_kernel,
        grid=(tiles_here // block,),
        in_specs=[
            pl.BlockSpec((block, 1), lambda i: (i, 0)),
            pl.BlockSpec((block, pixels, columns), lambda i: (i, 0, 0)),
            pl.BlockSpec((block, pixels, columns), lambda i: (i % per_frame, 0, 0)),
            pl.BlockSpec((block, pixels, voxels), lambda i: (i, 0, 0)),
            pl.BlockSpec((block, pixels, voxels), lambda i: (i, 0, 0)),
        ],
        out_specs=pl.BlockSpec((block, 2 * voxels), lambda i: (i, 0)),
        out_shape=jax.ShapeDtypeStruct((tiles_here, 2 * voxels), jnp.float32),
    )(
        tile_factor,
        counts.reshape(tiles_here, pixels, columns),
        efficiency,
        row_split.reshape(tiles_here, pixels, voxels),
        col_split.reshape(tiles_here, pixels, voxels),
    )


def shards(counts, row_split, col_split, efficiency, lorentz, angles, tile_owner, tile_box):
    frames_here, tiles_frame, pixels, unused_width = counts.shape
    voxels = row_split.shape[-1]
    size_x = lax.axis_size("bx")
    size_y = lax.axis_size("by")
    size_z = lax.axis_size("bz")
    devices_all = size_x * size_y * size_z
    tiles_here = frames_here * tiles_frame
    capacity = max(4, 4 * tiles_here // devices_all)
    local_x = GX // size_x
    local_y = GY // size_y
    local_z = GZ // size_z
    boxes_here = local_x * local_y * local_z * BOX_BRICK
    picks = angles[:, None] == jnp.arange(lorentz.shape[0], dtype=jnp.int32)[None, :]
    factor = jnp.sum(jnp.where(picks, lorentz[None, :], 0.0), axis=1)
    payload = tile_payload(counts, row_split, col_split, efficiency, factor)
    owner = tile_owner[:, 0]
    marks = (owner[:, None] == jnp.arange(devices_all, dtype=jnp.int32)[None, :]).astype(jnp.int32)
    before = jnp.cumsum(marks, axis=0) - marks
    rank = jnp.sum(before * marks, axis=1)
    slot = owner * capacity + rank
    outgoing = jnp.zeros((devices_all * capacity, 2 * voxels), jnp.float32).at[slot].set(payload)
    labels = jnp.full((devices_all * capacity,), -1.0, jnp.float32).at[slot].set(
        tile_box.astype(jnp.float32)
    )
    label_width = 128
    labels = jnp.pad(labels.reshape(devices_all, capacity), ((0, 0), (0, label_width - capacity)))
    packed = jnp.concatenate(
        [outgoing.reshape(devices_all, capacity * 2 * voxels), labels], axis=1
    )
    arrived = lax.all_to_all(packed, ("bx", "by", "bz"), split_axis=0, concat_axis=0, tiled=True)
    arrived_payload = arrived[:, : capacity * 2 * voxels].reshape(devices_all * capacity, 2 * voxels)
    arrived_ids = arrived[:, capacity * 2 * voxels : capacity * 2 * voxels + capacity].reshape(
        devices_all * capacity
    )
    wanted = (
        jnp.arange(boxes_here, dtype=jnp.float32)[:, None] == arrived_ids[None, :]
    ).astype(jnp.float32)
    sums = jnp.dot(
        wanted, arrived_payload, precision=lax.Precision.HIGHEST, preferred_element_type=jnp.float32
    )
    row_sizes = (local_x, local_y, local_z, BOXX, BOXY, BOXZ)
    lane_sizes = (VX, VY, VZ)
    result = laue_average(sums, row_sizes, lane_sizes)
    return result.reshape(local_x, local_y, local_z, BOX_BRICK, voxels)


def solution(mesh):
    return jax.shard_map(
        shards,
        mesh=mesh,
        in_specs=(
            P(("bx", "by", "bz"), None, None, None),
            P(("bx", "by", "bz"), None, None, None),
            P(("bx", "by", "bz"), None, None, None),
            P(),
            P(),
            P(("bx", "by", "bz")),
            P(("bx", "by", "bz"), None),
            P(("bx", "by", "bz")),
        ),
        out_specs=P("bx", "by", "bz", None, None),
        check_vma=False,
    )
```

```python
import functools

import numpy as np
import jax
import jax.numpy as jnp
from jax import lax
from jax.sharding import PartitionSpec as P
from jax.experimental import pallas as pl
from jax.experimental.pallas import tpu as pltpu

VX = 8
VY = 8
VZ = 4
GX = 8
GY = 8
GZ = 4
BOXX = 4
BOXY = 4
BOXZ = 4
BOX_BRICK = 64


def flip_mask(sizes, flipped):
    mask, stride = 0, 1
    for dim in reversed(range(len(sizes))):
        assert sizes[dim] & (sizes[dim] - 1) == 0
        if dim in flipped:
            mask |= (sizes[dim] - 1) * stride
        stride *= sizes[dim]
    return mask


def flip_matrices(row_sizes, lane_sizes, stage):
    rows = int(np.prod(row_sizes))
    lanes = int(np.prod(lane_sizes))
    out_row = lax.broadcasted_iota(jnp.int32, (rows, rows), 0)
    in_row = lax.broadcasted_iota(jnp.int32, (rows, rows), 1)
    row_flip = (in_row == (out_row ^ flip_mask(row_sizes, (stage, stage + 3)))).astype(jnp.float32)
    in_lane = lax.broadcasted_iota(jnp.int32, (lanes, lanes), 0)
    out_lane = lax.broadcasted_iota(jnp.int32, (lanes, lanes), 1)
    lane_flip = (in_lane == (out_lane ^ flip_mask(lane_sizes, (stage,)))).astype(jnp.float32)
    return row_flip, lane_flip


def split_three(x):
    hi = x.astype(jnp.bfloat16)
    rest = x - hi.astype(jnp.float32)
    mid = rest.astype(jnp.bfloat16)
    lo = (rest - mid.astype(jnp.float32)).astype(jnp.bfloat16)
    return hi, mid, lo


def flipped(pair, row_sizes, lane_sizes, stage):
    row_flip, lane_flip = flip_matrices(row_sizes, lane_sizes, stage)
    row_flip = row_flip.astype(jnp.bfloat16)
    lane_flip = lane_flip.astype(jnp.bfloat16)
    result = []
    for half in pair:
        parts = []
        for piece in split_three(half):
            moved = jnp.dot(row_flip, piece, preferred_element_type=jnp.float32).astype(jnp.bfloat16)
            parts.append(jnp.dot(moved, lane_flip, preferred_element_type=jnp.float32))
        result.append((parts[0] + parts[1]) + parts[2])
    return result


def averaged(pair, other):
    return [0.5 * (mine + moved) for mine, moved in zip(pair, other)]


def laue_kernel(row_sizes, lane_sizes, sums_ref, out_ref, received, held, send_sems, recv_sems):
    voxels = int(np.prod(lane_sizes))
    axes = ("bx", "by", "bz")
    here = tuple(lax.axis_index(axis) for axis in axes)
    sizes = tuple(lax.axis_size(axis) for axis in axes)

    def mirror(flags):
        return tuple(sizes[a] - 1 - here[a] if flags[a] else here[a] for a in range(3))

    first = (mirror((1, 0, 0)), mirror((0, 1, 0)), mirror((1, 1, 0)))
    last = mirror((0, 0, 1))
    barrier = pltpu.get_barrier_semaphore()
    for target in first + (last,):
        pl.semaphore_signal(barrier, 1, device_id=target, device_id_type=pl.DeviceIdType.MESH)
    pl.semaphore_wait(barrier, 4)

    def send(source, slot, target):
        copy = pltpu.make_async_remote_copy(
            src_ref=source,
            dst_ref=received.at[slot],
            send_sem=send_sems.at[slot],
            recv_sem=recv_sems.at[slot],
            device_id=target,
            device_id_type=pl.DeviceIdType.MESH,
        )
        copy.start()
        return copy

    copies = [send(sums_ref, slot, target) for slot, target in enumerate(first)]
    for copy in copies:
        copy.wait()

    def halves(ref):
        return [ref[:, :voxels], ref[:, voxels:]]

    stage_x = averaged(halves(sums_ref), flipped(halves(received.at[0]), row_sizes, lane_sizes, 0))
    stage_x_there = averaged(
        halves(received.at[1]), flipped(halves(received.at[2]), row_sizes, lane_sizes, 0)
    )
    stage_y = averaged(stage_x, flipped(stage_x_there, row_sizes, lane_sizes, 1))
    held[:, :voxels] = stage_y[0]
    held[:, voxels:] = stage_y[1]
    copy = send(held, 3, last)
    copy.wait()
    stage_z = averaged(halves(held), flipped(halves(received.at[3]), row_sizes, lane_sizes, 2))
    out_ref[...] = stage_z[0] / jnp.maximum(stage_z[1], 1.0)


def laue_average(sums, row_sizes, lane_sizes):
    rows, width = sums.shape
    voxels = width // 2
    return pl.pallas_call(
        functools.partial(laue_kernel, row_sizes, lane_sizes),
        in_specs=[pl.BlockSpec(memory_space=pltpu.VMEM)],
        out_specs=pl.BlockSpec(memory_space=pltpu.VMEM),
        out_shape=jax.ShapeDtypeStruct((rows, voxels), jnp.float32),
        scratch_shapes=[
            pltpu.VMEM((4, rows, width), jnp.float32),
            pltpu.VMEM((rows, width), jnp.float32),
            pltpu.SemaphoreType.DMA((4,)),
            pltpu.SemaphoreType.DMA((4,)),
        ],
        compiler_params=pltpu.CompilerParams(collective_id=0, has_side_effects=True),
    )(sums)


def tile_kernel(capacity, slot_ref, factor_ref, counts_ref, eff_ref, rows_ref, cols_ref, labels_ref, out_ref):
    block, unused_pixels, voxels = rows_ref.shape
    width = 2 * voxels
    step = pl.program_id(0)

    @pl.when(step == 0)
    def _():
        out_ref[:, : capacity * width] = jnp.zeros((out_ref.shape[0], capacity * width), jnp.float32)
        out_ref[:, capacity * width :] = labels_ref[...]

    for t in range(block):
        cols = cols_ref[t]
        rows = rows_ref[t].astype(jnp.float32)
        counted = jnp.dot(counts_ref[t], cols, preferred_element_type=jnp.float32)
        seen = jnp.dot(eff_ref[t], cols, preferred_element_type=jnp.float32)
        value = jnp.sum(rows * counted, axis=0, keepdims=True)
        weight = jnp.sum(rows * seen, axis=0, keepdims=True)
        slot = slot_ref[step * block + t]
        target = slot // capacity
        start = pl.multiple_of((slot % capacity) * width, width)
        out_ref[pl.ds(target, 1), pl.ds(start, voxels)] = value * factor_ref[t : t + 1, :]
        out_ref[pl.ds(target, 1), pl.ds(start + voxels, voxels)] = weight


def tile_payload(counts, row_split, col_split, efficiency, factor, slot, labels, capacity):
    frames_here, tiles_frame, pixels, columns = counts.shape
    voxels = row_split.shape[-1]
    tiles_here = frames_here * tiles_frame
    devices_all, label_width = labels.shape
    block = 8
    per_frame = tiles_frame // block
    tile_factor = jnp.repeat(factor, tiles_frame)[:, None]
    width = capacity * 2 * voxels + label_width
    return pl.pallas_call(
        functools.partial(tile_kernel, capacity),
        grid_spec=pltpu.PrefetchScalarGridSpec(
            num_scalar_prefetch=1,
            grid=(tiles_here // block,),
            in_specs=[
                pl.BlockSpec((block, 1), lambda i, s: (i, 0)),
                pl.BlockSpec((block, pixels, columns), lambda i, s: (i, 0, 0)),
                pl.BlockSpec((block, pixels, columns), lambda i, s: (i % per_frame, 0, 0)),
                pl.BlockSpec((block, pixels, voxels), lambda i, s: (i, 0, 0)),
                pl.BlockSpec((block, pixels, voxels), lambda i, s: (i, 0, 0)),
                pl.BlockSpec((devices_all, label_width), lambda i, s: (0, 0)),
            ],
            out_specs=pl.BlockSpec((devices_all, width), lambda i, s: (0, 0)),
        ),
        out_shape=jax.ShapeDtypeStruct((devices_all, width), jnp.float32),
    )(
        slot,
        tile_factor,
        counts.reshape(tiles_here, pixels, columns),
        efficiency,
        row_split.reshape(tiles_here, pixels, voxels),
        col_split.reshape(tiles_here, pixels, voxels),
        labels,
    )


def shards(counts, row_split, col_split, efficiency, lorentz, angles, tile_owner, tile_box):
    frames_here, tiles_frame, pixels, unused_width = counts.shape
    voxels = row_split.shape[-1]
    size_x = lax.axis_size("bx")
    size_y = lax.axis_size("by")
    size_z = lax.axis_size("bz")
    devices_all = size_x * size_y * size_z
    tiles_here = frames_here * tiles_frame
    capacity = max(4, 4 * tiles_here // devices_all)
    local_x = GX // size_x
    local_y = GY // size_y
    local_z = GZ // size_z
    boxes_here = local_x * local_y * local_z * BOX_BRICK
    picks = angles[:, None] == jnp.arange(lorentz.shape[0], dtype=jnp.int32)[None, :]
    factor = jnp.sum(jnp.where(picks, lorentz[None, :], 0.0), axis=1)
    owner = tile_owner[:, 0]
    same = owner[:, None] == owner[None, :]
    earlier = lax.broadcasted_iota(jnp.int32, same.shape, 1) < lax.broadcasted_iota(jnp.int32, same.shape, 0)
    rank = jnp.sum((same & earlier).astype(jnp.int32), axis=1)
    slot = owner * capacity + rank
    label_width = 128
    to_device = (owner[None, :] == jnp.arange(devices_all, dtype=jnp.int32)[:, None]).astype(jnp.bfloat16)
    at_rank = jnp.where(
        rank[:, None] == jnp.arange(label_width, dtype=jnp.int32)[None, :], tile_box[:, None] + 1, 0
    ).astype(jnp.bfloat16)
    labels = jnp.dot(to_device, at_rank, preferred_element_type=jnp.float32) - 1.0
    packed = tile_payload(counts, row_split, col_split, efficiency, factor, slot, labels, capacity)
    arrived = lax.all_to_all(packed, ("bx", "by", "bz"), split_axis=0, concat_axis=0, tiled=True)
    arrived_payload = arrived[:, : capacity * 2 * voxels].reshape(devices_all * capacity, 2 * voxels)
    arrived_ids = arrived[:, capacity * 2 * voxels : capacity * 2 * voxels + capacity].reshape(
        devices_all * capacity
    )
    wanted = (
        jnp.arange(boxes_here, dtype=jnp.float32)[:, None] == arrived_ids[None, :]
    ).astype(jnp.float32)
    sums = jnp.dot(
        wanted, arrived_payload, precision=lax.Precision.HIGHEST, preferred_element_type=jnp.float32
    )
    row_sizes = (local_x, local_y, local_z, BOXX, BOXY, BOXZ)
    lane_sizes = (VX, VY, VZ)
    result = laue_average(sums, row_sizes, lane_sizes)
    return result.reshape(local_x, local_y, local_z, BOX_BRICK, voxels)


def solution(mesh):
    return jax.shard_map(
        shards,
        mesh=mesh,
        in_specs=(
            P(("bx", "by", "bz"), None, None, None),
            P(("bx", "by", "bz"), None, None, None),
            P(("bx", "by", "bz"), None, None, None),
            P(),
            P(),
            P(("bx", "by", "bz")),
            P(("bx", "by", "bz"), None),
            P(("bx", "by", "bz")),
        ),
        out_specs=P("bx", "by", "bz", None, None),
        check_vma=False,
    )
```

```python
import functools

import numpy as np
import jax
import jax.numpy as jnp
from jax import lax
from jax.sharding import PartitionSpec as P
from jax.experimental import pallas as pl
from jax.experimental.pallas import tpu as pltpu

VX = 8
VY = 8
VZ = 4
GX = 8
GY = 8
GZ = 4
BOXX = 4
BOXY = 4
BOXZ = 4
BOX_BRICK = 64


def flip_mask(sizes, flipped):
    mask, stride = 0, 1
    for dim in reversed(range(len(sizes))):
        assert sizes[dim] & (sizes[dim] - 1) == 0
        if dim in flipped:
            mask |= (sizes[dim] - 1) * stride
        stride *= sizes[dim]
    return mask


def flip_matrices(row_sizes, lane_sizes, stage):
    rows = int(np.prod(row_sizes))
    lanes = int(np.prod(lane_sizes))
    out_row = lax.broadcasted_iota(jnp.int32, (rows, rows), 0)
    in_row = lax.broadcasted_iota(jnp.int32, (rows, rows), 1)
    row_flip = (in_row == (out_row ^ flip_mask(row_sizes, (stage, stage + 3)))).astype(jnp.float32)
    in_lane = lax.broadcasted_iota(jnp.int32, (lanes, lanes), 0)
    out_lane = lax.broadcasted_iota(jnp.int32, (lanes, lanes), 1)
    lane_flip = (in_lane == (out_lane ^ flip_mask(lane_sizes, (stage,)))).astype(jnp.float32)
    return row_flip, lane_flip


def split_three(x):
    hi = x.astype(jnp.bfloat16)
    rest = x - hi.astype(jnp.float32)
    mid = rest.astype(jnp.bfloat16)
    lo = (rest - mid.astype(jnp.float32)).astype(jnp.bfloat16)
    return hi, mid, lo


def flipped(pair, row_sizes, lane_sizes, stage):
    row_flip, lane_flip = flip_matrices(row_sizes, lane_sizes, stage)
    row_flip = row_flip.astype(jnp.bfloat16)
    lane_flip = lane_flip.astype(jnp.bfloat16)
    result = []
    for half in pair:
        parts = []
        for piece in split_three(half):
            moved = jnp.dot(row_flip, piece, preferred_element_type=jnp.float32).astype(jnp.bfloat16)
            parts.append(jnp.dot(moved, lane_flip, preferred_element_type=jnp.float32))
        result.append((parts[0] + parts[1]) + parts[2])
    return result


def averaged(pair, other):
    return [0.5 * (mine + moved) for mine, moved in zip(pair, other)]


def laue_kernel(row_sizes, lane_sizes, sums_ref, out_ref, received, held, send_sems, recv_sems):
    voxels = int(np.prod(lane_sizes))
    axes = ("bx", "by", "bz")
    here = tuple(lax.axis_index(axis) for axis in axes)
    sizes = tuple(lax.axis_size(axis) for axis in axes)

    def mirror(flags):
        return tuple(sizes[a] - 1 - here[a] if flags[a] else here[a] for a in range(3))

    first = (mirror((1, 0, 0)), mirror((0, 1, 0)), mirror((1, 1, 0)))
    last = mirror((0, 0, 1))
    barrier = pltpu.get_barrier_semaphore()
    for target in first + (last,):
        pl.semaphore_signal(barrier, 1, device_id=target, device_id_type=pl.DeviceIdType.MESH)
    pl.semaphore_wait(barrier, 4)

    def send(source, slot, target):
        copy = pltpu.make_async_remote_copy(
            src_ref=source,
            dst_ref=received.at[slot],
            send_sem=send_sems.at[slot],
            recv_sem=recv_sems.at[slot],
            device_id=target,
            device_id_type=pl.DeviceIdType.MESH,
        )
        copy.start()
        return copy

    copies = [send(sums_ref, slot, target) for slot, target in enumerate(first)]
    for copy in copies:
        copy.wait()

    def halves(ref):
        return [ref[:, :voxels], ref[:, voxels:]]

    stage_x = averaged(halves(sums_ref), flipped(halves(received.at[0]), row_sizes, lane_sizes, 0))
    stage_x_there = averaged(
        halves(received.at[1]), flipped(halves(received.at[2]), row_sizes, lane_sizes, 0)
    )
    stage_y = averaged(stage_x, flipped(stage_x_there, row_sizes, lane_sizes, 1))
    held[:, :voxels] = stage_y[0]
    held[:, voxels:] = stage_y[1]
    copy = send(held, 3, last)
    copy.wait()
    stage_z = averaged(halves(held), flipped(halves(received.at[3]), row_sizes, lane_sizes, 2))
    out_ref[...] = stage_z[0] / jnp.maximum(stage_z[1], 1.0)


def laue_average(sums, row_sizes, lane_sizes):
    rows, width = sums.shape
    voxels = width // 2
    return pl.pallas_call(
        functools.partial(laue_kernel, row_sizes, lane_sizes),
        in_specs=[pl.BlockSpec(memory_space=pltpu.VMEM)],
        out_specs=pl.BlockSpec(memory_space=pltpu.VMEM),
        out_shape=jax.ShapeDtypeStruct((rows, voxels), jnp.float32),
        scratch_shapes=[
            pltpu.VMEM((4, rows, width), jnp.float32),
            pltpu.VMEM((rows, width), jnp.float32),
            pltpu.SemaphoreType.DMA((4,)),
            pltpu.SemaphoreType.DMA((4,)),
        ],
        compiler_params=pltpu.CompilerParams(collective_id=0, has_side_effects=True),
    )(sums)


def tile_kernel(
    capacity, tiles_frame, owner_ref, box_ref, angle_ref, lorentz_ref,
    counts_ref, eff_ref, rows_ref, cols_ref, out_ref, taken,
):
    block, unused_pixels, voxels = rows_ref.shape
    devices_all, unused_one, total = out_ref.shape
    width = 2 * voxels
    step = pl.program_id(0)

    @pl.when(step == 0)
    def _():
        out_ref[:, :, : capacity * width] = jnp.zeros((devices_all, 1, capacity * width), jnp.float32)
        out_ref[:, :, capacity * width :] = jnp.full((devices_all, 1, total - capacity * width), -1.0, jnp.float32)

        def clear(d, carry):
            taken[d] = 0
            return carry

        lax.fori_loop(0, devices_all, clear, 0)

    lanes = lax.broadcasted_iota(jnp.int32, (1, total - capacity * width), 1)
    for t in range(block):
        tile = step * block + t
        target = owner_ref[tile]
        rank = taken[target]
        taken[target] = rank + 1
        factor = lorentz_ref[angle_ref[tile // tiles_frame]]
        cols = cols_ref[t]
        rows = rows_ref[t].astype(jnp.float32)
        counted = jnp.dot(counts_ref[t], cols, preferred_element_type=jnp.float32)
        seen = jnp.dot(eff_ref[t], cols, preferred_element_type=jnp.float32)
        value = jnp.sum(rows * counted, axis=0, keepdims=True)
        weight = jnp.sum(rows * seen, axis=0, keepdims=True)
        start = pl.multiple_of(rank * width, width)
        out_ref[target, :, pl.ds(start, voxels)] = value * factor
        out_ref[target, :, pl.ds(start + voxels, voxels)] = weight
        label = jnp.full(lanes.shape, box_ref[tile], jnp.int32).astype(jnp.float32)
        out_ref[target, :, capacity * width :] = jnp.where(
            lanes == rank, label, out_ref[target, :, capacity * width :]
        )


def tile_payload(counts, row_split, col_split, efficiency, lorentz, angles, owner, box, devices_all, capacity):
    frames_here, tiles_frame, pixels, columns = counts.shape
    voxels = row_split.shape[-1]
    tiles_here = frames_here * tiles_frame
    label_width = 128
    block = 8
    per_frame = tiles_frame // block
    total = capacity * 2 * voxels + label_width
    return pl.pallas_call(
        functools.partial(tile_kernel, capacity, tiles_frame),
        grid_spec=pltpu.PrefetchScalarGridSpec(
            num_scalar_prefetch=3,
            grid=(tiles_here // block,),
            in_specs=[
                pl.BlockSpec(memory_space=pltpu.SMEM),
                pl.BlockSpec((block, pixels, columns), lambda i, *s: (i, 0, 0)),
                pl.BlockSpec((block, pixels, columns), lambda i, *s: (i % per_frame, 0, 0)),
                pl.BlockSpec((block, pixels, voxels), lambda i, *s: (i, 0, 0)),
                pl.BlockSpec((block, pixels, voxels), lambda i, *s: (i, 0, 0)),
            ],
            out_specs=pl.BlockSpec((devices_all, 1, total), lambda i, *s: (0, 0, 0)),
            scratch_shapes=[pltpu.SMEM((devices_all,), jnp.int32)],
        ),
        out_shape=jax.ShapeDtypeStruct((devices_all, 1, total), jnp.float32),
    )(
        owner,
        box,
        angles,
        lorentz,
        counts.reshape(tiles_here, pixels, columns),
        efficiency,
        row_split.reshape(tiles_here, pixels, voxels),
        col_split.reshape(tiles_here, pixels, voxels),
    )


def shards(counts, row_split, col_split, efficiency, lorentz, angles, tile_owner, tile_box):
    frames_here, tiles_frame, pixels, unused_width = counts.shape
    voxels = row_split.shape[-1]
    size_x = lax.axis_size("bx")
    size_y = lax.axis_size("by")
    size_z = lax.axis_size("bz")
    devices_all = size_x * size_y * size_z
    tiles_here = frames_here * tiles_frame
    capacity = max(4, 4 * tiles_here // devices_all)
    local_x = GX // size_x
    local_y = GY // size_y
    local_z = GZ // size_z
    boxes_here = local_x * local_y * local_z * BOX_BRICK
    packed = tile_payload(
        counts, row_split, col_split, efficiency, lorentz, angles,
        tile_owner[:, 0], tile_box, devices_all, capacity,
    )
    arrived = lax.all_to_all(packed, ("bx", "by", "bz"), split_axis=0, concat_axis=0, tiled=True)
    arrived = arrived.reshape(devices_all, -1)
    arrived_payload = arrived[:, : capacity * 2 * voxels].reshape(devices_all * capacity, 2 * voxels)
    arrived_ids = arrived[:, capacity * 2 * voxels : capacity * 2 * voxels + capacity].reshape(
        devices_all * capacity
    )
    wanted = (
        jnp.arange(boxes_here, dtype=jnp.float32)[:, None] == arrived_ids[None, :]
    ).astype(jnp.float32)
    sums = jnp.dot(
        wanted, arrived_payload, precision=lax.Precision.HIGHEST, preferred_element_type=jnp.float32
    )
    row_sizes = (local_x, local_y, local_z, BOXX, BOXY, BOXZ)
    lane_sizes = (VX, VY, VZ)
    result = laue_average(sums, row_sizes, lane_sizes)
    return result.reshape(local_x, local_y, local_z, BOX_BRICK, voxels)


def solution(mesh):
    return jax.shard_map(
        shards,
        mesh=mesh,
        in_specs=(
            P(("bx", "by", "bz"), None, None, None),
            P(("bx", "by", "bz"), None, None, None),
            P(("bx", "by", "bz"), None, None, None),
            P(),
            P(),
            P(("bx", "by", "bz")),
            P(("bx", "by", "bz"), None),
            P(("bx", "by", "bz")),
        ),
        out_specs=P("bx", "by", "bz", None, None),
        check_vma=False,
    )
```

```python
import functools

import numpy as np
import jax
import jax.numpy as jnp
from jax import lax
from jax.sharding import PartitionSpec as P
from jax.experimental import pallas as pl
from jax.experimental.pallas import tpu as pltpu

VX = 8
VY = 8
VZ = 4
GX = 8
GY = 8
GZ = 4
BOXX = 4
BOXY = 4
BOXZ = 4
BOX_BRICK = 64


def flip_mask(sizes, flipped):
    mask, stride = 0, 1
    for dim in reversed(range(len(sizes))):
        assert sizes[dim] & (sizes[dim] - 1) == 0
        if dim in flipped:
            mask |= (sizes[dim] - 1) * stride
        stride *= sizes[dim]
    return mask


def flip_matrices(row_sizes, lane_sizes, stage):
    rows = int(np.prod(row_sizes))
    lanes = int(np.prod(lane_sizes))
    out_row = lax.broadcasted_iota(jnp.int32, (rows, rows), 0)
    in_row = lax.broadcasted_iota(jnp.int32, (rows, rows), 1)
    row_flip = (in_row == (out_row ^ flip_mask(row_sizes, (stage, stage + 3)))).astype(jnp.float32)
    in_lane = lax.broadcasted_iota(jnp.int32, (lanes, lanes), 0)
    out_lane = lax.broadcasted_iota(jnp.int32, (lanes, lanes), 1)
    lane_flip = (in_lane == (out_lane ^ flip_mask(lane_sizes, (stage,)))).astype(jnp.float32)
    return row_flip, lane_flip


def split_three(x):
    hi = x.astype(jnp.bfloat16)
    rest = x - hi.astype(jnp.float32)
    mid = rest.astype(jnp.bfloat16)
    lo = (rest - mid.astype(jnp.float32)).astype(jnp.bfloat16)
    return hi, mid, lo


def flipped(pair, row_sizes, lane_sizes, stage):
    row_flip, lane_flip = flip_matrices(row_sizes, lane_sizes, stage)
    row_flip = row_flip.astype(jnp.bfloat16)
    lane_flip = lane_flip.astype(jnp.bfloat16)
    result = []
    for half in pair:
        parts = []
        for piece in split_three(half):
            moved = jnp.dot(row_flip, piece, preferred_element_type=jnp.float32).astype(jnp.bfloat16)
            parts.append(jnp.dot(moved, lane_flip, preferred_element_type=jnp.float32))
        result.append((parts[0] + parts[1]) + parts[2])
    return result


def averaged(pair, other):
    return [0.5 * (mine + moved) for mine, moved in zip(pair, other)]


def flat_device(flat, sizes):
    return (flat // (sizes[1] * sizes[2]), (flat // sizes[2]) % sizes[1], flat % sizes[2])


def exact_dot(one_hot, values):
    parts = [
        jnp.dot(one_hot, piece, preferred_element_type=jnp.float32) for piece in split_three(values)
    ]
    return (parts[0] + parts[1]) + parts[2]


def exchange_kernel(
    row_sizes, lane_sizes, capacity, payload_ref, labels_ref, out_ref,
    inbox, label_inbox, received, held, bulk_sems, stage_sems,
):
    voxels = int(np.prod(lane_sizes))
    boxes = int(np.prod(row_sizes))
    axes = ("bx", "by", "bz")
    here = tuple(lax.axis_index(axis) for axis in axes)
    sizes = tuple(lax.axis_size(axis) for axis in axes)
    count = sizes[0] * sizes[1] * sizes[2]
    me = (here[0] * sizes[1] + here[1]) * sizes[2] + here[2]
    mesh_id = pl.DeviceIdType.MESH
    barrier = pltpu.get_barrier_semaphore()

    def greet(step, carry):
        pl.semaphore_signal(barrier, 1, device_id=flat_device((me + step) % count, sizes), device_id_type=mesh_id)
        return carry

    lax.fori_loop(1, count, greet, 0)
    pl.semaphore_wait(barrier, count - 1)

    def payload_copy(target, source_row, target_row):
        return pltpu.make_async_remote_copy(
            src_ref=payload_ref.at[source_row], dst_ref=inbox.at[target_row],
            send_sem=bulk_sems.at[0], recv_sem=bulk_sems.at[1],
            device_id=target, device_id_type=mesh_id,
        )

    def label_copy(target, source_rows, target_rows):
        return pltpu.make_async_remote_copy(
            src_ref=labels_ref.at[source_rows], dst_ref=label_inbox.at[target_rows],
            send_sem=bulk_sems.at[2], recv_sem=bulk_sems.at[3],
            device_id=target, device_id_type=mesh_id,
        )

    def send(step, carry):
        flat = (me + step) % count
        target = flat_device(flat, sizes)
        payload_copy(target, flat, me).start()
        label_copy(target, pl.ds(flat, 1), pl.ds(me, 1)).start()
        return carry

    lax.fori_loop(1, count, send, 0)
    neighbour = flat_device((me + 1) % count, sizes)
    every = payload_copy(neighbour, pl.ds(0, count - 1), pl.ds(0, count - 1))
    every.wait_send()
    every.wait_recv()
    every = label_copy(neighbour, pl.ds(0, count - 1), pl.ds(0, count - 1))
    every.wait_send()
    every.wait_recv()
    inbox[me] = payload_ref[me]
    label_inbox[pl.ds(me, 1), :] = labels_ref[pl.ds(me, 1), :]

    names = jnp.transpose(label_inbox[...])
    box_ids = lax.broadcasted_iota(jnp.int32, (boxes, count), 0).astype(jnp.float32)
    value = jnp.zeros((boxes, voxels), jnp.float32)
    weight = jnp.zeros((boxes, voxels), jnp.float32)
    for k in range(capacity):
        one_hot = (box_ids == names[k : k + 1, :]).astype(jnp.bfloat16)
        value = value + exact_dot(one_hot, inbox[:, 2 * k, :])
        weight = weight + exact_dot(one_hot, inbox[:, 2 * k + 1, :])
    held[0, :, :voxels] = value
    held[0, :, voxels:] = weight

    def halves(ref):
        return [ref[:, :voxels], ref[:, voxels:]]

    current = held.at[0]
    for stage in range(3):
        partner = list(here)
        partner[stage] = sizes[stage] - 1 - here[stage]
        copy = pltpu.make_async_remote_copy(
            src_ref=current, dst_ref=received.at[stage],
            send_sem=stage_sems.at[0, stage], recv_sem=stage_sems.at[1, stage],
            device_id=tuple(partner), device_id_type=mesh_id,
        )
        copy.start()
        copy.wait()
        result = averaged(halves(current), flipped(halves(received.at[stage]), row_sizes, lane_sizes, stage))
        if stage < 2:
            held[stage + 1, :, :voxels] = result[0]
            held[stage + 1, :, voxels:] = result[1]
            current = held.at[stage + 1]
    out_ref[...] = result[0] / jnp.maximum(result[1], 1.0)


def exchange_and_average(payload, labels, row_sizes, lane_sizes, capacity):
    devices_all, slots, voxels = payload.shape
    boxes = int(np.prod(row_sizes))
    return pl.pallas_call(
        functools.partial(exchange_kernel, row_sizes, lane_sizes, capacity),
        in_specs=[pl.BlockSpec(memory_space=pltpu.VMEM)] * 2,
        out_specs=pl.BlockSpec(memory_space=pltpu.VMEM),
        out_shape=jax.ShapeDtypeStruct((boxes, voxels), jnp.float32),
        scratch_shapes=[
            pltpu.VMEM(payload.shape, jnp.float32),
            pltpu.VMEM(labels.shape, jnp.float32),
            pltpu.VMEM((3, boxes, 2 * voxels), jnp.float32),
            pltpu.VMEM((3, boxes, 2 * voxels), jnp.float32),
            pltpu.SemaphoreType.DMA((4,)),
            pltpu.SemaphoreType.DMA((2, 3)),
        ],
        compiler_params=pltpu.CompilerParams(collective_id=0, has_side_effects=True),
    )(payload, labels)


def tile_kernel(
    capacity, tiles_frame, owner_ref, box_ref, angle_ref, lorentz_ref,
    counts_ref, eff_ref, rows_ref, cols_ref, out_ref, labels_ref, taken,
):
    block, unused_pixels, voxels = rows_ref.shape
    devices_all, label_width = labels_ref.shape
    step = pl.program_id(0)

    @pl.when(step == 0)
    def _():
        out_ref[...] = jnp.zeros(out_ref.shape, jnp.float32)
        labels_ref[...] = jnp.full(labels_ref.shape, -1.0, jnp.float32)

        def clear(d, carry):
            taken[d] = 0
            return carry

        lax.fori_loop(0, devices_all, clear, 0)

    lanes = lax.broadcasted_iota(jnp.int32, (1, label_width), 1)
    for t in range(block):
        tile = step * block + t
        target = owner_ref[tile]
        rank = taken[target]
        taken[target] = rank + 1
        factor = lorentz_ref[angle_ref[tile // tiles_frame]]
        cols = cols_ref[t]
        rows = rows_ref[t].astype(jnp.float32)
        counted = jnp.dot(counts_ref[t], cols, preferred_element_type=jnp.float32)
        seen = jnp.dot(eff_ref[t], cols, preferred_element_type=jnp.float32)
        value = jnp.sum(rows * counted, axis=0, keepdims=True)
        weight = jnp.sum(rows * seen, axis=0, keepdims=True)
        out_ref[target, pl.ds(2 * rank, 1), :] = value * factor
        out_ref[target, pl.ds(2 * rank + 1, 1), :] = weight
        label = jnp.full(lanes.shape, box_ref[tile], jnp.int32).astype(jnp.float32)
        labels_ref[pl.ds(target, 1), :] = jnp.where(lanes == rank, label, labels_ref[pl.ds(target, 1), :])


def tile_payload(counts, row_split, col_split, efficiency, lorentz, angles, owner, box, devices_all, capacity):
    frames_here, tiles_frame, pixels, columns = counts.shape
    voxels = row_split.shape[-1]
    tiles_here = frames_here * tiles_frame
    label_width = 128
    block = 8
    per_frame = tiles_frame // block
    return pl.pallas_call(
        functools.partial(tile_kernel, capacity, tiles_frame),
        grid_spec=pltpu.PrefetchScalarGridSpec(
            num_scalar_prefetch=3,
            grid=(tiles_here // block,),
            in_specs=[
                pl.BlockSpec(memory_space=pltpu.SMEM),
                pl.BlockSpec((block, pixels, columns), lambda i, *s: (i, 0, 0)),
                pl.BlockSpec((block, pixels, columns), lambda i, *s: (i % per_frame, 0, 0)),
                pl.BlockSpec((block, pixels, voxels), lambda i, *s: (i, 0, 0)),
                pl.BlockSpec((block, pixels, voxels), lambda i, *s: (i, 0, 0)),
            ],
            out_specs=[
                pl.BlockSpec((devices_all, 2 * capacity, voxels), lambda i, *s: (0, 0, 0)),
                pl.BlockSpec((devices_all, label_width), lambda i, *s: (0, 0)),
            ],
            scratch_shapes=[pltpu.SMEM((devices_all,), jnp.int32)],
        ),
        out_shape=[
            jax.ShapeDtypeStruct((devices_all, 2 * capacity, voxels), jnp.float32),
            jax.ShapeDtypeStruct((devices_all, label_width), jnp.float32),
        ],
    )(
        owner,
        box,
        angles,
        lorentz,
        counts.reshape(tiles_here, pixels, columns),
        efficiency,
        row_split.reshape(tiles_here, pixels, voxels),
        col_split.reshape(tiles_here, pixels, voxels),
    )


def shards(counts, row_split, col_split, efficiency, lorentz, angles, tile_owner, tile_box):
    frames_here, tiles_frame, pixels, unused_width = counts.shape
    voxels = row_split.shape[-1]
    size_x = lax.axis_size("bx")
    size_y = lax.axis_size("by")
    size_z = lax.axis_size("bz")
    devices_all = size_x * size_y * size_z
    tiles_here = frames_here * tiles_frame
    capacity = max(4, 4 * tiles_here // devices_all)
    local_x = GX // size_x
    local_y = GY // size_y
    local_z = GZ // size_z
    boxes_here = local_x * local_y * local_z * BOX_BRICK
    payload, labels = tile_payload(
        counts, row_split, col_split, efficiency, lorentz, angles,
        tile_owner[:, 0], tile_box, devices_all, capacity,
    )
    row_sizes = (local_x, local_y, local_z, BOXX, BOXY, BOXZ)
    lane_sizes = (VX, VY, VZ)
    result = exchange_and_average(payload, labels, row_sizes, lane_sizes, capacity)
    return result.reshape(local_x, local_y, local_z, BOX_BRICK, voxels)


def solution(mesh):
    return jax.shard_map(
        shards,
        mesh=mesh,
        in_specs=(
            P(("bx", "by", "bz"), None, None, None),
            P(("bx", "by", "bz"), None, None, None),
            P(("bx", "by", "bz"), None, None, None),
            P(),
            P(),
            P(("bx", "by", "bz")),
            P(("bx", "by", "bz"), None),
            P(("bx", "by", "bz")),
        ),
        out_specs=P("bx", "by", "bz", None, None),
        check_vma=False,
    )
```

```python
import functools

import numpy as np
import jax
import jax.numpy as jnp
from jax import lax
from jax.sharding import PartitionSpec as P
from jax.experimental import pallas as pl
from jax.experimental.pallas import tpu as pltpu

VX = 8
VY = 8
VZ = 4
GX = 8
GY = 8
GZ = 4
BOXX = 4
BOXY = 4
BOXZ = 4
BOX_BRICK = 64


def flip_mask(sizes, flipped):
    mask, stride = 0, 1
    for dim in reversed(range(len(sizes))):
        assert sizes[dim] & (sizes[dim] - 1) == 0
        if dim in flipped:
            mask |= (sizes[dim] - 1) * stride
        stride *= sizes[dim]
    return mask


def flip_matrices(row_sizes, lane_sizes, stage):
    rows = int(np.prod(row_sizes))
    lanes = int(np.prod(lane_sizes))
    out_row = lax.broadcasted_iota(jnp.int32, (rows, rows), 0)
    in_row = lax.broadcasted_iota(jnp.int32, (rows, rows), 1)
    row_flip = (in_row == (out_row ^ flip_mask(row_sizes, (stage, stage + 3)))).astype(jnp.float32)
    in_lane = lax.broadcasted_iota(jnp.int32, (lanes, lanes), 0)
    out_lane = lax.broadcasted_iota(jnp.int32, (lanes, lanes), 1)
    lane_flip = (in_lane == (out_lane ^ flip_mask(lane_sizes, (stage,)))).astype(jnp.float32)
    return row_flip, lane_flip


def split_three(x):
    hi = x.astype(jnp.bfloat16)
    rest = x - hi.astype(jnp.float32)
    mid = rest.astype(jnp.bfloat16)
    lo = (rest - mid.astype(jnp.float32)).astype(jnp.bfloat16)
    return hi, mid, lo


def flipped(pair, row_sizes, lane_sizes, stage):
    row_flip, lane_flip = flip_matrices(row_sizes, lane_sizes, stage)
    row_flip = row_flip.astype(jnp.bfloat16)
    lane_flip = lane_flip.astype(jnp.bfloat16)
    result = []
    for half in pair:
        parts = []
        for piece in split_three(half):
            moved = jnp.dot(row_flip, piece, preferred_element_type=jnp.float32).astype(jnp.bfloat16)
            parts.append(jnp.dot(moved, lane_flip, preferred_element_type=jnp.float32))
        result.append((parts[0] + parts[1]) + parts[2])
    return result


def averaged(pair, other):
    return [0.5 * (mine + moved) for mine, moved in zip(pair, other)]


def laue_kernel(row_sizes, lane_sizes, sums_ref, out_ref, received, held, send_sems, recv_sems):
    voxels = int(np.prod(lane_sizes))
    axes = ("bx", "by", "bz")
    here = tuple(lax.axis_index(axis) for axis in axes)
    sizes = tuple(lax.axis_size(axis) for axis in axes)

    def mirror(flags):
        return tuple(sizes[a] - 1 - here[a] if flags[a] else here[a] for a in range(3))

    first = (mirror((1, 0, 0)), mirror((0, 1, 0)), mirror((1, 1, 0)))
    last = mirror((0, 0, 1))
    barrier = pltpu.get_barrier_semaphore()
    for target in first + (last,):
        pl.semaphore_signal(barrier, 1, device_id=target, device_id_type=pl.DeviceIdType.MESH)
    pl.semaphore_wait(barrier, 4)

    def send(source, slot, target):
        copy = pltpu.make_async_remote_copy(
            src_ref=source,
            dst_ref=received.at[slot],
            send_sem=send_sems.at[slot],
            recv_sem=recv_sems.at[slot],
            device_id=target,
            device_id_type=pl.DeviceIdType.MESH,
        )
        copy.start()
        return copy

    copies = [send(sums_ref, slot, target) for slot, target in enumerate(first)]
    for copy in copies:
        copy.wait()

    def halves(ref):
        return [ref[:, :voxels], ref[:, voxels:]]

    stage_x = averaged(halves(sums_ref), flipped(halves(received.at[0]), row_sizes, lane_sizes, 0))
    stage_x_there = averaged(
        halves(received.at[1]), flipped(halves(received.at[2]), row_sizes, lane_sizes, 0)
    )
    stage_y = averaged(stage_x, flipped(stage_x_there, row_sizes, lane_sizes, 1))
    held[:, :voxels] = stage_y[0]
    held[:, voxels:] = stage_y[1]
    copy = send(held, 3, last)
    copy.wait()
    stage_z = averaged(halves(held), flipped(halves(received.at[3]), row_sizes, lane_sizes, 2))
    out_ref[...] = stage_z[0] / jnp.maximum(stage_z[1], 1.0)


def laue_average(sums, row_sizes, lane_sizes):
    rows, width = sums.shape
    voxels = width // 2
    return pl.pallas_call(
        functools.partial(laue_kernel, row_sizes, lane_sizes),
        in_specs=[pl.BlockSpec(memory_space=pltpu.VMEM)],
        out_specs=pl.BlockSpec(memory_space=pltpu.VMEM),
        out_shape=jax.ShapeDtypeStruct((rows, voxels), jnp.float32),
        scratch_shapes=[
            pltpu.VMEM((4, rows, width), jnp.float32),
            pltpu.VMEM((rows, width), jnp.float32),
            pltpu.SemaphoreType.DMA((4,)),
            pltpu.SemaphoreType.DMA((4,)),
        ],
        compiler_params=pltpu.CompilerParams(collective_id=0, has_side_effects=True),
    )(sums)


def tile_kernel(
    capacity, tiles_frame, owner_ref, box_ref, angle_ref, lorentz_ref,
    counts_ref, eff_ref, rows_ref, cols_ref, out_ref, taken,
):
    block, unused_pixels, voxels = rows_ref.shape
    devices_all, unused_one, total = out_ref.shape
    width = 2 * voxels
    step = pl.program_id(0)

    @pl.when(step == 0)
    def _():
        out_ref[:, :, : capacity * width] = jnp.zeros((devices_all, 1, capacity * width), jnp.float32)
        out_ref[:, :, capacity * width :] = jnp.full((devices_all, 1, total - capacity * width), -1.0, jnp.float32)

        def clear(d, carry):
            taken[d] = 0
            return carry

        lax.fori_loop(0, devices_all, clear, 0)

    lanes = lax.broadcasted_iota(jnp.int32, (1, total - capacity * width), 1)
    for t in range(block):
        tile = step * block + t
        target = owner_ref[tile]
        rank = taken[target]
        taken[target] = rank + 1
        factor = lorentz_ref[angle_ref[tile // tiles_frame]]
        cols = cols_ref[t]
        rows = rows_ref[t].astype(jnp.float32)
        both = jnp.dot(
            jnp.concatenate([counts_ref[t], eff_ref[t]], axis=0), cols, preferred_element_type=jnp.float32
        )
        counted = both[: counts_ref.shape[1]]
        seen = both[counts_ref.shape[1] :]
        value = jnp.sum(rows * counted, axis=0, keepdims=True)
        weight = jnp.sum(rows * seen, axis=0, keepdims=True)
        start = pl.multiple_of(rank * width, width)
        out_ref[target, :, pl.ds(start, voxels)] = value * factor
        out_ref[target, :, pl.ds(start + voxels, voxels)] = weight
        label = jnp.full(lanes.shape, box_ref[tile], jnp.int32).astype(jnp.float32)
        out_ref[target, :, capacity * width :] = jnp.where(
            lanes == rank, label, out_ref[target, :, capacity * width :]
        )


def tile_payload(counts, row_split, col_split, efficiency, lorentz, angles, owner, box, devices_all, capacity):
    frames_here, tiles_frame, pixels, columns = counts.shape
    voxels = row_split.shape[-1]
    tiles_here = frames_here * tiles_frame
    label_width = 128
    block = 8
    per_frame = tiles_frame // block
    total = capacity * 2 * voxels + label_width
    return pl.pallas_call(
        functools.partial(tile_kernel, capacity, tiles_frame),
        grid_spec=pltpu.PrefetchScalarGridSpec(
            num_scalar_prefetch=3,
            grid=(tiles_here // block,),
            in_specs=[
                pl.BlockSpec(memory_space=pltpu.SMEM),
                pl.BlockSpec((block, pixels, columns), lambda i, *s: (i, 0, 0)),
                pl.BlockSpec((block, pixels, columns), lambda i, *s: (i % per_frame, 0, 0)),
                pl.BlockSpec((block, pixels, voxels), lambda i, *s: (i, 0, 0)),
                pl.BlockSpec((block, pixels, voxels), lambda i, *s: (i, 0, 0)),
            ],
            out_specs=pl.BlockSpec((devices_all, 1, total), lambda i, *s: (0, 0, 0)),
            scratch_shapes=[pltpu.SMEM((devices_all,), jnp.int32)],
        ),
        out_shape=jax.ShapeDtypeStruct((devices_all, 1, total), jnp.float32),
    )(
        owner,
        box,
        angles,
        lorentz,
        counts.reshape(tiles_here, pixels, columns),
        efficiency,
        row_split.reshape(tiles_here, pixels, voxels),
        col_split.reshape(tiles_here, pixels, voxels),
    )


def shards(counts, row_split, col_split, efficiency, lorentz, angles, tile_owner, tile_box):
    frames_here, tiles_frame, pixels, unused_width = counts.shape
    voxels = row_split.shape[-1]
    size_x = lax.axis_size("bx")
    size_y = lax.axis_size("by")
    size_z = lax.axis_size("bz")
    devices_all = size_x * size_y * size_z
    tiles_here = frames_here * tiles_frame
    capacity = max(4, 4 * tiles_here // devices_all)
    local_x = GX // size_x
    local_y = GY // size_y
    local_z = GZ // size_z
    boxes_here = local_x * local_y * local_z * BOX_BRICK
    packed = tile_payload(
        counts, row_split, col_split, efficiency, lorentz, angles,
        tile_owner[:, 0], tile_box, devices_all, capacity,
    )
    arrived = lax.all_to_all(packed, ("bx", "by", "bz"), split_axis=0, concat_axis=0, tiled=True)
    arrived = arrived.reshape(devices_all, -1)
    arrived_payload = arrived[:, : capacity * 2 * voxels].reshape(devices_all * capacity, 2 * voxels)
    arrived_ids = arrived[:, capacity * 2 * voxels : capacity * 2 * voxels + capacity].reshape(
        devices_all * capacity
    )
    wanted = (
        jnp.arange(boxes_here, dtype=jnp.float32)[:, None] == arrived_ids[None, :]
    ).astype(jnp.float32)
    sums = jnp.dot(
        wanted, arrived_payload, precision=lax.Precision.HIGHEST, preferred_element_type=jnp.float32
    )
    row_sizes = (local_x, local_y, local_z, BOXX, BOXY, BOXZ)
    lane_sizes = (VX, VY, VZ)
    result = laue_average(sums, row_sizes, lane_sizes)
    return result.reshape(local_x, local_y, local_z, BOX_BRICK, voxels)


def solution(mesh):
    return jax.shard_map(
        shards,
        mesh=mesh,
        in_specs=(
            P(("bx", "by", "bz"), None, None, None),
            P(("bx", "by", "bz"), None, None, None),
            P(("bx", "by", "bz"), None, None, None),
            P(),
            P(),
            P(("bx", "by", "bz")),
            P(("bx", "by", "bz"), None),
            P(("bx", "by", "bz")),
        ),
        out_specs=P("bx", "by", "bz", None, None),
        check_vma=False,
    )
```

```python
import functools

import numpy as np
import jax
import jax.numpy as jnp
from jax import lax
from jax.sharding import PartitionSpec as P
from jax.experimental import pallas as pl
from jax.experimental.pallas import tpu as pltpu

VX = 8
VY = 8
VZ = 4
GX = 8
GY = 8
GZ = 4
BOXX = 4
BOXY = 4
BOXZ = 4
BOX_BRICK = 64


def flip_mask(sizes, flipped):
    mask, stride = 0, 1
    for dim in reversed(range(len(sizes))):
        assert sizes[dim] & (sizes[dim] - 1) == 0
        if dim in flipped:
            mask |= (sizes[dim] - 1) * stride
        stride *= sizes[dim]
    return mask


def flip_matrices(row_sizes, lane_sizes, stage):
    rows = int(np.prod(row_sizes))
    lanes = int(np.prod(lane_sizes))
    out_row = lax.broadcasted_iota(jnp.int32, (rows, rows), 0)
    in_row = lax.broadcasted_iota(jnp.int32, (rows, rows), 1)
    row_flip = (in_row == (out_row ^ flip_mask(row_sizes, (stage, stage + 3)))).astype(jnp.float32)
    in_lane = lax.broadcasted_iota(jnp.int32, (lanes, lanes), 0)
    out_lane = lax.broadcasted_iota(jnp.int32, (lanes, lanes), 1)
    lane_flip = (in_lane == (out_lane ^ flip_mask(lane_sizes, (stage,)))).astype(jnp.float32)
    return row_flip, lane_flip


def split_three(x):
    hi = x.astype(jnp.bfloat16)
    rest = x - hi.astype(jnp.float32)
    mid = rest.astype(jnp.bfloat16)
    lo = (rest - mid.astype(jnp.float32)).astype(jnp.bfloat16)
    return hi, mid, lo


def flipped(pair, row_sizes, lane_sizes, stage):
    row_flip, lane_flip = flip_matrices(row_sizes, lane_sizes, stage)
    row_flip = row_flip.astype(jnp.bfloat16)
    lane_flip = lane_flip.astype(jnp.bfloat16)
    result = []
    for half in pair:
        parts = []
        for piece in split_three(half):
            moved = jnp.dot(row_flip, piece, preferred_element_type=jnp.float32).astype(jnp.bfloat16)
            parts.append(jnp.dot(moved, lane_flip, preferred_element_type=jnp.float32))
        result.append((parts[0] + parts[1]) + parts[2])
    return result


def exact_dot(one_hot, values):
    parts = [
        jnp.dot(one_hot, piece, preferred_element_type=jnp.float32) for piece in split_three(values)
    ]
    return (parts[0] + parts[1]) + parts[2]


def averaged(pair, other):
    return [0.5 * (mine + moved) for mine, moved in zip(pair, other)]


def laue_kernel(
    row_sizes, lane_sizes, capacity, arrived_ref, out_ref, sums_ref, received, held, send_sems, recv_sems
):
    voxels = int(np.prod(lane_sizes))
    boxes = int(np.prod(row_sizes))
    sources = arrived_ref.shape[0]
    width = 2 * voxels
    names = jnp.transpose(arrived_ref[:, capacity * width : capacity * width + 128])
    box_ids = lax.broadcasted_iota(jnp.int32, (boxes, sources), 0).astype(jnp.float32)
    value = jnp.zeros((boxes, voxels), jnp.float32)
    weight = jnp.zeros((boxes, voxels), jnp.float32)
    for k in range(capacity):
        one_hot = (box_ids == names[k : k + 1, :]).astype(jnp.bfloat16)
        value = value + exact_dot(one_hot, arrived_ref[:, k * width : k * width + voxels])
        weight = weight + exact_dot(one_hot, arrived_ref[:, k * width + voxels : (k + 1) * width])
    sums_ref[:, :voxels] = value
    sums_ref[:, voxels:] = weight
    axes = ("bx", "by", "bz")
    here = tuple(lax.axis_index(axis) for axis in axes)
    sizes = tuple(lax.axis_size(axis) for axis in axes)

    def mirror(flags):
        return tuple(sizes[a] - 1 - here[a] if flags[a] else here[a] for a in range(3))

    first = (mirror((1, 0, 0)), mirror((0, 1, 0)), mirror((1, 1, 0)))
    last = mirror((0, 0, 1))
    barrier = pltpu.get_barrier_semaphore()
    for target in first + (last,):
        pl.semaphore_signal(barrier, 1, device_id=target, device_id_type=pl.DeviceIdType.MESH)
    pl.semaphore_wait(barrier, 4)

    def send(source, slot, target):
        copy = pltpu.make_async_remote_copy(
            src_ref=source,
            dst_ref=received.at[slot],
            send_sem=send_sems.at[slot],
            recv_sem=recv_sems.at[slot],
            device_id=target,
            device_id_type=pl.DeviceIdType.MESH,
        )
        copy.start()
        return copy

    copies = [send(sums_ref, slot, target) for slot, target in enumerate(first)]
    for copy in copies:
        copy.wait()

    def halves(ref):
        return [ref[:, :voxels], ref[:, voxels:]]

    stage_x = averaged(halves(sums_ref), flipped(halves(received.at[0]), row_sizes, lane_sizes, 0))
    stage_x_there = averaged(
        halves(received.at[1]), flipped(halves(received.at[2]), row_sizes, lane_sizes, 0)
    )
    stage_y = averaged(stage_x, flipped(stage_x_there, row_sizes, lane_sizes, 1))
    held[:, :voxels] = stage_y[0]
    held[:, voxels:] = stage_y[1]
    copy = send(held, 3, last)
    copy.wait()
    stage_z = averaged(halves(held), flipped(halves(received.at[3]), row_sizes, lane_sizes, 2))
    out_ref[:, :voxels] = stage_z[0]
    out_ref[:, voxels:] = stage_z[1]


def laue_average(arrived, row_sizes, lane_sizes, capacity):
    rows = int(np.prod(row_sizes))
    width = 2 * int(np.prod(lane_sizes))
    return pl.pallas_call(
        functools.partial(laue_kernel, row_sizes, lane_sizes, capacity),
        in_specs=[pl.BlockSpec(memory_space=pltpu.VMEM)],
        out_specs=pl.BlockSpec(memory_space=pltpu.VMEM),
        out_shape=jax.ShapeDtypeStruct((rows, width), jnp.float32),
        scratch_shapes=[
            pltpu.VMEM((rows, width), jnp.float32),
            pltpu.VMEM((4, rows, width), jnp.float32),
            pltpu.VMEM((rows, width), jnp.float32),
            pltpu.SemaphoreType.DMA((4,)),
            pltpu.SemaphoreType.DMA((4,)),
        ],
        compiler_params=pltpu.CompilerParams(collective_id=0, has_side_effects=True),
    )(arrived)


def tile_kernel(
    capacity, tiles_frame, owner_ref, box_ref, angle_ref, lorentz_ref,
    counts_ref, eff_ref, rows_ref, cols_ref, out_ref, taken,
):
    block, unused_pixels, voxels = rows_ref.shape
    devices_all, unused_one, total = out_ref.shape
    width = 2 * voxels
    step = pl.program_id(0)

    @pl.when(step == 0)
    def _():
        out_ref[:, :, : capacity * width] = jnp.zeros((devices_all, 1, capacity * width), jnp.float32)
        out_ref[:, :, capacity * width :] = jnp.full((devices_all, 1, total - capacity * width), -1.0, jnp.float32)

        def clear(d, carry):
            taken[d] = 0
            return carry

        lax.fori_loop(0, devices_all, clear, 0)

    lanes = lax.broadcasted_iota(jnp.int32, (1, total - capacity * width), 1)
    for t in range(block):
        tile = step * block + t
        target = owner_ref[tile]
        rank = taken[target]
        taken[target] = rank + 1
        factor = lorentz_ref[angle_ref[tile // tiles_frame]]
        cols = cols_ref[t]
        rows = rows_ref[t].astype(jnp.float32)
        both = jnp.dot(
            jnp.concatenate([counts_ref[t], eff_ref[t]], axis=0), cols, preferred_element_type=jnp.float32
        )
        counted = both[: counts_ref.shape[1]]
        seen = both[counts_ref.shape[1] :]
        value = jnp.sum(rows * counted, axis=0, keepdims=True)
        weight = jnp.sum(rows * seen, axis=0, keepdims=True)
        start = pl.multiple_of(rank * width, width)
        out_ref[target, :, pl.ds(start, voxels)] = value * factor
        out_ref[target, :, pl.ds(start + voxels, voxels)] = weight
        label = jnp.full(lanes.shape, box_ref[tile], jnp.int32).astype(jnp.float32)
        out_ref[target, :, capacity * width :] = jnp.where(
            lanes == rank, label, out_ref[target, :, capacity * width :]
        )


def tile_payload(counts, row_split, col_split, efficiency, lorentz, angles, owner, box, devices_all, capacity):
    frames_here, tiles_frame, pixels, columns = counts.shape
    voxels = row_split.shape[-1]
    tiles_here = frames_here * tiles_frame
    label_width = 128
    block = 8
    per_frame = tiles_frame // block
    total = capacity * 2 * voxels + label_width
    return pl.pallas_call(
        functools.partial(tile_kernel, capacity, tiles_frame),
        grid_spec=pltpu.PrefetchScalarGridSpec(
            num_scalar_prefetch=3,
            grid=(tiles_here // block,),
            in_specs=[
                pl.BlockSpec(memory_space=pltpu.SMEM),
                pl.BlockSpec((block, pixels, columns), lambda i, *s: (i, 0, 0)),
                pl.BlockSpec((block, pixels, columns), lambda i, *s: (i % per_frame, 0, 0)),
                pl.BlockSpec((block, pixels, voxels), lambda i, *s: (i, 0, 0)),
                pl.BlockSpec((block, pixels, voxels), lambda i, *s: (i, 0, 0)),
            ],
            out_specs=pl.BlockSpec((devices_all, 1, total), lambda i, *s: (0, 0, 0)),
            scratch_shapes=[pltpu.SMEM((devices_all,), jnp.int32)],
        ),
        out_shape=jax.ShapeDtypeStruct((devices_all, 1, total), jnp.float32),
    )(
        owner,
        box,
        angles,
        lorentz,
        counts.reshape(tiles_here, pixels, columns),
        efficiency,
        row_split.reshape(tiles_here, pixels, voxels),
        col_split.reshape(tiles_here, pixels, voxels),
    )


def shards(counts, row_split, col_split, efficiency, lorentz, angles, tile_owner, tile_box):
    frames_here, tiles_frame, pixels, unused_width = counts.shape
    voxels = row_split.shape[-1]
    size_x = lax.axis_size("bx")
    size_y = lax.axis_size("by")
    size_z = lax.axis_size("bz")
    devices_all = size_x * size_y * size_z
    tiles_here = frames_here * tiles_frame
    capacity = max(4, 4 * tiles_here // devices_all)
    local_x = GX // size_x
    local_y = GY // size_y
    local_z = GZ // size_z
    boxes_here = local_x * local_y * local_z * BOX_BRICK
    packed = tile_payload(
        counts, row_split, col_split, efficiency, lorentz, angles,
        tile_owner[:, 0], tile_box, devices_all, capacity,
    )
    arrived = lax.all_to_all(packed, ("bx", "by", "bz"), split_axis=0, concat_axis=0, tiled=True)
    arrived = arrived.reshape(devices_all, -1)
    row_sizes = (local_x, local_y, local_z, BOXX, BOXY, BOXZ)
    lane_sizes = (VX, VY, VZ)
    volume = laue_average(arrived, row_sizes, lane_sizes, capacity)
    result = volume[:, :voxels] / jnp.maximum(volume[:, voxels:], 1.0)
    return result.reshape(local_x, local_y, local_z, BOX_BRICK, voxels)


def solution(mesh):
    return jax.shard_map(
        shards,
        mesh=mesh,
        in_specs=(
            P(("bx", "by", "bz"), None, None, None),
            P(("bx", "by", "bz"), None, None, None),
            P(("bx", "by", "bz"), None, None, None),
            P(),
            P(),
            P(("bx", "by", "bz")),
            P(("bx", "by", "bz"), None),
            P(("bx", "by", "bz")),
        ),
        out_specs=P("bx", "by", "bz", None, None),
        check_vma=False,
    )
```

```python
import functools

import numpy as np
import jax
import jax.numpy as jnp
from jax import lax
from jax.sharding import PartitionSpec as P
from jax.experimental import pallas as pl
from jax.experimental.pallas import tpu as pltpu

VX = 8
VY = 8
VZ = 4
GX = 8
GY = 8
GZ = 4
BOXX = 4
BOXY = 4
BOXZ = 4
BOX_BRICK = 64


def flip_mask(sizes, flipped):
    mask, stride = 0, 1
    for dim in reversed(range(len(sizes))):
        assert sizes[dim] & (sizes[dim] - 1) == 0
        if dim in flipped:
            mask |= (sizes[dim] - 1) * stride
        stride *= sizes[dim]
    return mask


def flip_matrices(row_sizes, lane_sizes, stage):
    rows = int(np.prod(row_sizes))
    lanes = int(np.prod(lane_sizes))
    out_row = lax.broadcasted_iota(jnp.int32, (rows, rows), 0)
    in_row = lax.broadcasted_iota(jnp.int32, (rows, rows), 1)
    row_flip = (in_row == (out_row ^ flip_mask(row_sizes, (stage, stage + 3)))).astype(jnp.float32)
    in_lane = lax.broadcasted_iota(jnp.int32, (lanes, lanes), 0)
    out_lane = lax.broadcasted_iota(jnp.int32, (lanes, lanes), 1)
    lane_flip = (in_lane == (out_lane ^ flip_mask(lane_sizes, (stage,)))).astype(jnp.float32)
    return row_flip, lane_flip


def split_three(x):
    hi = x.astype(jnp.bfloat16)
    rest = x - hi.astype(jnp.float32)
    mid = rest.astype(jnp.bfloat16)
    lo = (rest - mid.astype(jnp.float32)).astype(jnp.bfloat16)
    return hi, mid, lo


def flipped(pair, row_sizes, lane_sizes, stage):
    row_flip, lane_flip = flip_matrices(row_sizes, lane_sizes, stage)
    row_flip = row_flip.astype(jnp.bfloat16)
    lane_flip = lane_flip.astype(jnp.bfloat16)
    result = []
    for half in pair:
        parts = []
        for piece in split_three(half):
            moved = jnp.dot(row_flip, piece, preferred_element_type=jnp.float32).astype(jnp.bfloat16)
            parts.append(jnp.dot(moved, lane_flip, preferred_element_type=jnp.float32))
        result.append((parts[0] + parts[1]) + parts[2])
    return result


def averaged(pair, other):
    return [0.5 * (mine + moved) for mine, moved in zip(pair, other)]


def laue_kernel(row_sizes, lane_sizes, sums_ref, out_ref, received, held, send_sems, recv_sems):
    voxels = int(np.prod(lane_sizes))
    axes = ("bx", "by", "bz")
    here = tuple(lax.axis_index(axis) for axis in axes)
    sizes = tuple(lax.axis_size(axis) for axis in axes)

    def mirror(flags):
        return tuple(sizes[a] - 1 - here[a] if flags[a] else here[a] for a in range(3))

    first = (mirror((1, 0, 0)), mirror((0, 1, 0)), mirror((1, 1, 0)))
    last = mirror((0, 0, 1))
    barrier = pltpu.get_barrier_semaphore()
    for target in first + (last,):
        pl.semaphore_signal(barrier, 1, device_id=target, device_id_type=pl.DeviceIdType.MESH)
    pl.semaphore_wait(barrier, 4)

    def send(source, slot, target):
        copy = pltpu.make_async_remote_copy(
            src_ref=source,
            dst_ref=received.at[slot],
            send_sem=send_sems.at[slot],
            recv_sem=recv_sems.at[slot],
            device_id=target,
            device_id_type=pl.DeviceIdType.MESH,
        )
        copy.start()
        return copy

    copies = [send(sums_ref, slot, target) for slot, target in enumerate(first)]
    for copy in copies:
        copy.wait()

    def halves(ref):
        return [ref[:, :voxels], ref[:, voxels:]]

    stage_x = averaged(halves(sums_ref), flipped(halves(received.at[0]), row_sizes, lane_sizes, 0))
    stage_x_there = averaged(
        halves(received.at[1]), flipped(halves(received.at[2]), row_sizes, lane_sizes, 0)
    )
    stage_y = averaged(stage_x, flipped(stage_x_there, row_sizes, lane_sizes, 1))
    held[:, :voxels] = stage_y[0]
    held[:, voxels:] = stage_y[1]
    copy = send(held, 3, last)
    copy.wait()
    stage_z = averaged(halves(held), flipped(halves(received.at[3]), row_sizes, lane_sizes, 2))
    out_ref[...] = stage_z[0] / jnp.maximum(stage_z[1], 1.0)


def laue_average(sums, row_sizes, lane_sizes):
    rows, width = sums.shape
    voxels = width // 2
    return pl.pallas_call(
        functools.partial(laue_kernel, row_sizes, lane_sizes),
        in_specs=[pl.BlockSpec(memory_space=pltpu.VMEM)],
        out_specs=pl.BlockSpec(memory_space=pltpu.VMEM),
        out_shape=jax.ShapeDtypeStruct((rows, voxels), jnp.float32),
        scratch_shapes=[
            pltpu.VMEM((4, rows, width), jnp.float32),
            pltpu.VMEM((rows, width), jnp.float32),
            pltpu.SemaphoreType.DMA((4,)),
            pltpu.SemaphoreType.DMA((4,)),
        ],
        compiler_params=pltpu.CompilerParams(collective_id=0, has_side_effects=True),
    )(sums)


def tile_kernel(
    capacity, tiles_frame, owner_ref, box_ref, angle_ref, lorentz_ref,
    counts_ref, eff_ref, rows_ref, cols_ref, out_ref, taken,
):
    block, unused_pixels, voxels = rows_ref.shape
    devices_all, unused_one, total = out_ref.shape
    width = 2 * voxels
    step = pl.program_id(0)

    @pl.when(step == 0)
    def _():
        out_ref[:, :, : capacity * width] = jnp.zeros((devices_all, 1, capacity * width), jnp.float32)
        out_ref[:, :, capacity * width :] = jnp.full((devices_all, 1, total - capacity * width), -1.0, jnp.float32)

        def clear(d, carry):
            taken[d] = 0
            return carry

        lax.fori_loop(0, devices_all, clear, 0)

    lanes = lax.broadcasted_iota(jnp.int32, (1, total - capacity * width), 1)
    for t in range(block):
        tile = step * block + t
        target = owner_ref[tile]
        rank = taken[target]
        taken[target] = rank + 1
        factor = lorentz_ref[angle_ref[tile // tiles_frame]]
        cols = cols_ref[t]
        rows = rows_ref[t].astype(jnp.float32)
        both = jnp.dot(
            jnp.concatenate([counts_ref[t], eff_ref[t]], axis=0), cols, preferred_element_type=jnp.float32
        )
        counted = both[: counts_ref.shape[1]]
        seen = both[counts_ref.shape[1] :]
        value = jnp.sum(rows * counted, axis=0, keepdims=True)
        weight = jnp.sum(rows * seen, axis=0, keepdims=True)
        start = pl.multiple_of(rank * width, width)
        out_ref[target, :, pl.ds(start, voxels)] = value * factor
        out_ref[target, :, pl.ds(start + voxels, voxels)] = weight
        label = jnp.full(lanes.shape, box_ref[tile], jnp.int32).astype(jnp.float32)
        out_ref[target, :, capacity * width :] = jnp.where(
            lanes == rank, label, out_ref[target, :, capacity * width :]
        )


def tile_payload(counts, row_split, col_split, efficiency, lorentz, angles, owner, box, devices_all, capacity):
    frames_here, tiles_frame, pixels, columns = counts.shape
    voxels = row_split.shape[-1]
    tiles_here = frames_here * tiles_frame
    label_width = 128
    block = 16
    per_frame = tiles_frame // block
    total = capacity * 2 * voxels + label_width
    return pl.pallas_call(
        functools.partial(tile_kernel, capacity, tiles_frame),
        grid_spec=pltpu.PrefetchScalarGridSpec(
            num_scalar_prefetch=3,
            grid=(tiles_here // block,),
            in_specs=[
                pl.BlockSpec(memory_space=pltpu.SMEM),
                pl.BlockSpec((block, pixels, columns), lambda i, *s: (i, 0, 0)),
                pl.BlockSpec((block, pixels, columns), lambda i, *s: (i % per_frame, 0, 0)),
                pl.BlockSpec((block, pixels, voxels), lambda i, *s: (i, 0, 0)),
                pl.BlockSpec((block, pixels, voxels), lambda i, *s: (i, 0, 0)),
            ],
            out_specs=pl.BlockSpec((devices_all, 1, total), lambda i, *s: (0, 0, 0)),
            scratch_shapes=[pltpu.SMEM((devices_all,), jnp.int32)],
        ),
        out_shape=jax.ShapeDtypeStruct((devices_all, 1, total), jnp.float32),
    )(
        owner,
        box,
        angles,
        lorentz,
        counts.reshape(tiles_here, pixels, columns),
        efficiency,
        row_split.reshape(tiles_here, pixels, voxels),
        col_split.reshape(tiles_here, pixels, voxels),
    )


def shards(counts, row_split, col_split, efficiency, lorentz, angles, tile_owner, tile_box):
    frames_here, tiles_frame, pixels, unused_width = counts.shape
    voxels = row_split.shape[-1]
    size_x = lax.axis_size("bx")
    size_y = lax.axis_size("by")
    size_z = lax.axis_size("bz")
    devices_all = size_x * size_y * size_z
    tiles_here = frames_here * tiles_frame
    capacity = max(4, 4 * tiles_here // devices_all)
    local_x = GX // size_x
    local_y = GY // size_y
    local_z = GZ // size_z
    boxes_here = local_x * local_y * local_z * BOX_BRICK
    packed = tile_payload(
        counts, row_split, col_split, efficiency, lorentz, angles,
        tile_owner[:, 0], tile_box, devices_all, capacity,
    )
    arrived = lax.all_to_all(packed, ("bx", "by", "bz"), split_axis=0, concat_axis=0, tiled=True)
    arrived = arrived.reshape(devices_all, -1)
    arrived_payload = arrived[:, : capacity * 2 * voxels].reshape(devices_all * capacity, 2 * voxels)
    arrived_ids = arrived[:, capacity * 2 * voxels : capacity * 2 * voxels + capacity].reshape(
        devices_all * capacity
    )
    wanted = (
        jnp.arange(boxes_here, dtype=jnp.float32)[:, None] == arrived_ids[None, :]
    ).astype(jnp.float32)
    sums = jnp.dot(
        wanted, arrived_payload, precision=lax.Precision.HIGHEST, preferred_element_type=jnp.float32
    )
    row_sizes = (local_x, local_y, local_z, BOXX, BOXY, BOXZ)
    lane_sizes = (VX, VY, VZ)
    result = laue_average(sums, row_sizes, lane_sizes)
    return result.reshape(local_x, local_y, local_z, BOX_BRICK, voxels)


def solution(mesh):
    return jax.shard_map(
        shards,
        mesh=mesh,
        in_specs=(
            P(("bx", "by", "bz"), None, None, None),
            P(("bx", "by", "bz"), None, None, None),
            P(("bx", "by", "bz"), None, None, None),
            P(),
            P(),
            P(("bx", "by", "bz")),
            P(("bx", "by", "bz"), None),
            P(("bx", "by", "bz")),
        ),
        out_specs=P("bx", "by", "bz", None, None),
        check_vma=False,
    )
```

```python
import functools

import numpy as np
import jax
import jax.numpy as jnp
from jax import lax
from jax.sharding import PartitionSpec as P
from jax.experimental import pallas as pl
from jax.experimental.pallas import tpu as pltpu

VX = 8
VY = 8
VZ = 4
GX = 8
GY = 8
GZ = 4
BOXX = 4
BOXY = 4
BOXZ = 4
BOX_BRICK = 64


def flip_mask(sizes, flipped):
    mask, stride = 0, 1
    for dim in reversed(range(len(sizes))):
        assert sizes[dim] & (sizes[dim] - 1) == 0
        if dim in flipped:
            mask |= (sizes[dim] - 1) * stride
        stride *= sizes[dim]
    return mask


def flip_matrices(row_sizes, lane_sizes, stage):
    rows = int(np.prod(row_sizes))
    lanes = int(np.prod(lane_sizes))
    out_row = lax.broadcasted_iota(jnp.int32, (rows, rows), 0)
    in_row = lax.broadcasted_iota(jnp.int32, (rows, rows), 1)
    row_flip = (in_row == (out_row ^ flip_mask(row_sizes, (stage, stage + 3)))).astype(jnp.float32)
    in_lane = lax.broadcasted_iota(jnp.int32, (lanes, lanes), 0)
    out_lane = lax.broadcasted_iota(jnp.int32, (lanes, lanes), 1)
    lane_flip = (in_lane == (out_lane ^ flip_mask(lane_sizes, (stage,)))).astype(jnp.float32)
    return row_flip, lane_flip


def split_three(x):
    hi = x.astype(jnp.bfloat16)
    rest = x - hi.astype(jnp.float32)
    mid = rest.astype(jnp.bfloat16)
    lo = (rest - mid.astype(jnp.float32)).astype(jnp.bfloat16)
    return hi, mid, lo


def flipped(pair, row_sizes, lane_sizes, stage):
    row_flip, lane_flip = flip_matrices(row_sizes, lane_sizes, stage)
    row_flip = row_flip.astype(jnp.bfloat16)
    lane_flip = lane_flip.astype(jnp.bfloat16)
    result = []
    for half in pair:
        parts = []
        for piece in split_three(half):
            moved = jnp.dot(row_flip, piece, preferred_element_type=jnp.float32).astype(jnp.bfloat16)
            parts.append(jnp.dot(moved, lane_flip, preferred_element_type=jnp.float32))
        result.append((parts[0] + parts[1]) + parts[2])
    return result


def averaged(pair, other):
    return [0.5 * (mine + moved) for mine, moved in zip(pair, other)]


def laue_kernel(row_sizes, lane_sizes, sums_ref, out_ref, received, held, send_sems, recv_sems):
    voxels = int(np.prod(lane_sizes))
    axes = ("bx", "by", "bz")
    here = tuple(lax.axis_index(axis) for axis in axes)
    sizes = tuple(lax.axis_size(axis) for axis in axes)

    def mirror(flags):
        return tuple(sizes[a] - 1 - here[a] if flags[a] else here[a] for a in range(3))

    first = (mirror((1, 0, 0)), mirror((0, 1, 0)), mirror((1, 1, 0)))
    last = mirror((0, 0, 1))
    barrier = pltpu.get_barrier_semaphore()
    for target in first + (last,):
        pl.semaphore_signal(barrier, 1, device_id=target, device_id_type=pl.DeviceIdType.MESH)
    pl.semaphore_wait(barrier, 4)

    def send(source, slot, target):
        copy = pltpu.make_async_remote_copy(
            src_ref=source,
            dst_ref=received.at[slot],
            send_sem=send_sems.at[slot],
            recv_sem=recv_sems.at[slot],
            device_id=target,
            device_id_type=pl.DeviceIdType.MESH,
        )
        copy.start()
        return copy

    copies = [send(sums_ref, slot, target) for slot, target in enumerate(first)]
    for copy in copies:
        copy.wait()

    def halves(ref):
        return [ref[:, :voxels], ref[:, voxels:]]

    stage_x = averaged(halves(sums_ref), flipped(halves(received.at[0]), row_sizes, lane_sizes, 0))
    stage_x_there = averaged(
        halves(received.at[1]), flipped(halves(received.at[2]), row_sizes, lane_sizes, 0)
    )
    stage_y = averaged(stage_x, flipped(stage_x_there, row_sizes, lane_sizes, 1))
    held[:, :voxels] = stage_y[0]
    held[:, voxels:] = stage_y[1]
    copy = send(held, 3, last)
    copy.wait()
    stage_z = averaged(halves(held), flipped(halves(received.at[3]), row_sizes, lane_sizes, 2))
    out_ref[...] = stage_z[0] / jnp.maximum(stage_z[1], 1.0)


def laue_average(sums, row_sizes, lane_sizes):
    rows, width = sums.shape
    voxels = width // 2
    return pl.pallas_call(
        functools.partial(laue_kernel, row_sizes, lane_sizes),
        in_specs=[pl.BlockSpec(memory_space=pltpu.VMEM)],
        out_specs=pl.BlockSpec(memory_space=pltpu.VMEM),
        out_shape=jax.ShapeDtypeStruct((rows, voxels), jnp.float32),
        scratch_shapes=[
            pltpu.VMEM((4, rows, width), jnp.float32),
            pltpu.VMEM((rows, width), jnp.float32),
            pltpu.SemaphoreType.DMA((4,)),
            pltpu.SemaphoreType.DMA((4,)),
        ],
        compiler_params=pltpu.CompilerParams(collective_id=0, has_side_effects=True),
    )(sums)


def tile_kernel(
    capacity, tiles_frame, owner_ref, box_ref, angle_ref, lorentz_ref,
    counts_ref, eff_ref, rows_ref, cols_ref, out_ref, taken,
):
    block, unused_pixels, voxels = rows_ref.shape
    devices_all, unused_one, total = out_ref.shape
    width = 2 * voxels
    step = pl.program_id(0)

    @pl.when(step == 0)
    def _():
        out_ref[:, :, : capacity * width] = jnp.zeros((devices_all, 1, capacity * width), jnp.float32)
        out_ref[:, :, capacity * width :] = jnp.full((devices_all, 1, total - capacity * width), -1.0, jnp.float32)

        def clear(d, carry):
            taken[d] = 0
            return carry

        lax.fori_loop(0, devices_all, clear, 0)

    lanes = lax.broadcasted_iota(jnp.int32, (1, total - capacity * width), 1)
    for t in range(block):
        tile = step * block + t
        target = owner_ref[tile]
        rank = taken[target]
        taken[target] = rank + 1
        factor = lorentz_ref[angle_ref[tile // tiles_frame]]
        cols = cols_ref[t]
        rows = rows_ref[t].astype(jnp.float32)
        both = jnp.dot(
            jnp.concatenate([counts_ref[t], eff_ref[t]], axis=0), cols, preferred_element_type=jnp.float32
        )
        counted = both[: counts_ref.shape[1]]
        seen = both[counts_ref.shape[1] :]
        value = jnp.sum(rows * counted, axis=0, keepdims=True)
        weight = jnp.sum(rows * seen, axis=0, keepdims=True)
        start = pl.multiple_of(rank * width, width)
        out_ref[target, :, pl.ds(start, voxels)] = value * factor
        out_ref[target, :, pl.ds(start + voxels, voxels)] = weight
        label = jnp.full(lanes.shape, box_ref[tile], jnp.int32).astype(jnp.float32)
        out_ref[target, :, capacity * width :] = jnp.where(
            lanes == rank, label, out_ref[target, :, capacity * width :]
        )


def tile_payload(counts, row_split, col_split, efficiency, lorentz, angles, owner, box, devices_all, capacity):
    frames_here, tiles_frame, pixels, columns = counts.shape
    voxels = row_split.shape[-1]
    tiles_here = frames_here * tiles_frame
    label_width = 128
    block = 32
    per_frame = tiles_frame // block
    total = capacity * 2 * voxels + label_width
    return pl.pallas_call(
        functools.partial(tile_kernel, capacity, tiles_frame),
        grid_spec=pltpu.PrefetchScalarGridSpec(
            num_scalar_prefetch=3,
            grid=(tiles_here // block,),
            in_specs=[
                pl.BlockSpec(memory_space=pltpu.SMEM),
                pl.BlockSpec((block, pixels, columns), lambda i, *s: (i, 0, 0)),
                pl.BlockSpec((block, pixels, columns), lambda i, *s: (i % per_frame, 0, 0)),
                pl.BlockSpec((block, pixels, voxels), lambda i, *s: (i, 0, 0)),
                pl.BlockSpec((block, pixels, voxels), lambda i, *s: (i, 0, 0)),
            ],
            out_specs=pl.BlockSpec((devices_all, 1, total), lambda i, *s: (0, 0, 0)),
            scratch_shapes=[pltpu.SMEM((devices_all,), jnp.int32)],
        ),
        out_shape=jax.ShapeDtypeStruct((devices_all, 1, total), jnp.float32),
    )(
        owner,
        box,
        angles,
        lorentz,
        counts.reshape(tiles_here, pixels, columns),
        efficiency,
        row_split.reshape(tiles_here, pixels, voxels),
        col_split.reshape(tiles_here, pixels, voxels),
    )


def shards(counts, row_split, col_split, efficiency, lorentz, angles, tile_owner, tile_box):
    frames_here, tiles_frame, pixels, unused_width = counts.shape
    voxels = row_split.shape[-1]
    size_x = lax.axis_size("bx")
    size_y = lax.axis_size("by")
    size_z = lax.axis_size("bz")
    devices_all = size_x * size_y * size_z
    tiles_here = frames_here * tiles_frame
    capacity = max(4, 4 * tiles_here // devices_all)
    local_x = GX // size_x
    local_y = GY // size_y
    local_z = GZ // size_z
    boxes_here = local_x * local_y * local_z * BOX_BRICK
    packed = tile_payload(
        counts, row_split, col_split, efficiency, lorentz, angles,
        tile_owner[:, 0], tile_box, devices_all, capacity,
    )
    arrived = lax.all_to_all(packed, ("bx", "by", "bz"), split_axis=0, concat_axis=0, tiled=True)
    arrived = arrived.reshape(devices_all, -1)
    arrived_payload = arrived[:, : capacity * 2 * voxels].reshape(devices_all * capacity, 2 * voxels)
    arrived_ids = arrived[:, capacity * 2 * voxels : capacity * 2 * voxels + capacity].reshape(
        devices_all * capacity
    )
    wanted = (
        jnp.arange(boxes_here, dtype=jnp.float32)[:, None] == arrived_ids[None, :]
    ).astype(jnp.float32)
    sums = jnp.dot(
        wanted, arrived_payload, precision=lax.Precision.HIGHEST, preferred_element_type=jnp.float32
    )
    row_sizes = (local_x, local_y, local_z, BOXX, BOXY, BOXZ)
    lane_sizes = (VX, VY, VZ)
    result = laue_average(sums, row_sizes, lane_sizes)
    return result.reshape(local_x, local_y, local_z, BOX_BRICK, voxels)


def solution(mesh):
    return jax.shard_map(
        shards,
        mesh=mesh,
        in_specs=(
            P(("bx", "by", "bz"), None, None, None),
            P(("bx", "by", "bz"), None, None, None),
            P(("bx", "by", "bz"), None, None, None),
            P(),
            P(),
            P(("bx", "by", "bz")),
            P(("bx", "by", "bz"), None),
            P(("bx", "by", "bz")),
        ),
        out_specs=P("bx", "by", "bz", None, None),
        check_vma=False,
    )
```

```python
import functools

import numpy as np
import jax
import jax.numpy as jnp
from jax import lax
from jax.sharding import PartitionSpec as P
from jax.experimental import pallas as pl
from jax.experimental.pallas import tpu as pltpu

VX = 8
VY = 8
VZ = 4
GX = 8
GY = 8
GZ = 4
BOXX = 4
BOXY = 4
BOXZ = 4
BOX_BRICK = 64


def flip_mask(sizes, flipped):
    mask, stride = 0, 1
    for dim in reversed(range(len(sizes))):
        assert sizes[dim] & (sizes[dim] - 1) == 0
        if dim in flipped:
            mask |= (sizes[dim] - 1) * stride
        stride *= sizes[dim]
    return mask


def flip_matrices(row_sizes, lane_sizes, stage):
    rows = int(np.prod(row_sizes))
    lanes = int(np.prod(lane_sizes))
    out_row = lax.broadcasted_iota(jnp.int32, (rows, rows), 0)
    in_row = lax.broadcasted_iota(jnp.int32, (rows, rows), 1)
    row_flip = (in_row == (out_row ^ flip_mask(row_sizes, (stage, stage + 3)))).astype(jnp.float32)
    in_lane = lax.broadcasted_iota(jnp.int32, (lanes, lanes), 0)
    out_lane = lax.broadcasted_iota(jnp.int32, (lanes, lanes), 1)
    lane_flip = (in_lane == (out_lane ^ flip_mask(lane_sizes, (stage,)))).astype(jnp.float32)
    return row_flip, lane_flip


def split_three(x):
    hi = x.astype(jnp.bfloat16)
    rest = x - hi.astype(jnp.float32)
    mid = rest.astype(jnp.bfloat16)
    lo = (rest - mid.astype(jnp.float32)).astype(jnp.bfloat16)
    return hi, mid, lo


def flipped(pair, row_sizes, lane_sizes, stage):
    row_flip, lane_flip = flip_matrices(row_sizes, lane_sizes, stage)
    row_flip = row_flip.astype(jnp.bfloat16)
    lane_flip = lane_flip.astype(jnp.bfloat16)
    result = []
    for half in pair:
        parts = []
        for piece in split_three(half):
            moved = jnp.dot(row_flip, piece, preferred_element_type=jnp.float32).astype(jnp.bfloat16)
            parts.append(jnp.dot(moved, lane_flip, preferred_element_type=jnp.float32))
        result.append((parts[0] + parts[1]) + parts[2])
    return result


def averaged(pair, other):
    return [0.5 * (mine + moved) for mine, moved in zip(pair, other)]


def laue_kernel(row_sizes, lane_sizes, sums_ref, out_ref, received, held, send_sems, recv_sems):
    voxels = int(np.prod(lane_sizes))
    axes = ("bx", "by", "bz")
    here = tuple(lax.axis_index(axis) for axis in axes)
    sizes = tuple(lax.axis_size(axis) for axis in axes)

    def mirror(flags):
        return tuple(sizes[a] - 1 - here[a] if flags[a] else here[a] for a in range(3))

    first = (mirror((1, 0, 0)), mirror((0, 1, 0)), mirror((1, 1, 0)))
    last = mirror((0, 0, 1))
    barrier = pltpu.get_barrier_semaphore()
    for target in first + (last,):
        pl.semaphore_signal(barrier, 1, device_id=target, device_id_type=pl.DeviceIdType.MESH)
    pl.semaphore_wait(barrier, 4)

    def send(source, slot, target):
        copy = pltpu.make_async_remote_copy(
            src_ref=source,
            dst_ref=received.at[slot],
            send_sem=send_sems.at[slot],
            recv_sem=recv_sems.at[slot],
            device_id=target,
            device_id_type=pl.DeviceIdType.MESH,
        )
        copy.start()
        return copy

    copies = [send(sums_ref, slot, target) for slot, target in enumerate(first)]
    for copy in copies:
        copy.wait()

    def halves(ref):
        return [ref[:, :voxels], ref[:, voxels:]]

    stage_x = averaged(halves(sums_ref), flipped(halves(received.at[0]), row_sizes, lane_sizes, 0))
    stage_x_there = averaged(
        halves(received.at[1]), flipped(halves(received.at[2]), row_sizes, lane_sizes, 0)
    )
    stage_y = averaged(stage_x, flipped(stage_x_there, row_sizes, lane_sizes, 1))
    held[:, :voxels] = stage_y[0]
    held[:, voxels:] = stage_y[1]
    copy = send(held, 3, last)
    copy.wait()
    stage_z = averaged(halves(held), flipped(halves(received.at[3]), row_sizes, lane_sizes, 2))
    out_ref[...] = stage_z[0] / jnp.maximum(stage_z[1], 1.0)


def laue_average(sums, row_sizes, lane_sizes):
    rows, width = sums.shape
    voxels = width // 2
    return pl.pallas_call(
        functools.partial(laue_kernel, row_sizes, lane_sizes),
        in_specs=[pl.BlockSpec(memory_space=pltpu.VMEM)],
        out_specs=pl.BlockSpec(memory_space=pltpu.VMEM),
        out_shape=jax.ShapeDtypeStruct((rows, voxels), jnp.float32),
        scratch_shapes=[
            pltpu.VMEM((4, rows, width), jnp.float32),
            pltpu.VMEM((rows, width), jnp.float32),
            pltpu.SemaphoreType.DMA((4,)),
            pltpu.SemaphoreType.DMA((4,)),
        ],
        compiler_params=pltpu.CompilerParams(collective_id=0, has_side_effects=True),
    )(sums)


def tile_kernel(
    capacity, tiles_frame, owner_ref, box_ref, angle_ref, lorentz_ref,
    counts_ref, eff_ref, rows_ref, cols_ref, out_ref, taken,
):
    block, unused_pixels, voxels = rows_ref.shape
    devices_all, unused_one, total = out_ref.shape
    width = 2 * voxels
    step = pl.program_id(0)

    @pl.when(step == 0)
    def _():
        out_ref[:, :, : capacity * width] = jnp.zeros((devices_all, 1, capacity * width), jnp.float32)
        out_ref[:, :, capacity * width :] = jnp.full((devices_all, 1, total - capacity * width), -1.0, jnp.float32)

        def clear(d, carry):
            taken[d] = 0
            return carry

        lax.fori_loop(0, devices_all, clear, 0)

    lanes = lax.broadcasted_iota(jnp.int32, (1, total - capacity * width), 1)
    for t in range(block):
        tile = step * block + t
        target = owner_ref[tile]
        rank = taken[target]
        taken[target] = rank + 1
        factor = lorentz_ref[angle_ref[tile // tiles_frame]]
        cols = cols_ref[t]
        rows = rows_ref[t].astype(jnp.float32)
        both = jnp.dot(
            jnp.concatenate([counts_ref[t], eff_ref[t]], axis=0), cols, preferred_element_type=jnp.float32
        )
        counted = both[: counts_ref.shape[1]]
        seen = both[counts_ref.shape[1] :]
        value = jnp.sum(rows * counted, axis=0, keepdims=True)
        weight = jnp.sum(rows * seen, axis=0, keepdims=True)
        start = pl.multiple_of(rank * width, width)
        out_ref[target, :, pl.ds(start, voxels)] = value * factor
        out_ref[target, :, pl.ds(start + voxels, voxels)] = weight
        label = jnp.full(lanes.shape, box_ref[tile], jnp.int32).astype(jnp.float32)
        out_ref[target, :, capacity * width :] = jnp.where(
            lanes == rank, label, out_ref[target, :, capacity * width :]
        )


def tile_payload(counts, row_split, col_split, efficiency, lorentz, angles, owner, box, devices_all, capacity):
    frames_here, tiles_frame, pixels, columns = counts.shape
    voxels = row_split.shape[-1]
    tiles_here = frames_here * tiles_frame
    label_width = 128
    block = 64
    per_frame = tiles_frame // block
    total = capacity * 2 * voxels + label_width
    return pl.pallas_call(
        functools.partial(tile_kernel, capacity, tiles_frame),
        grid_spec=pltpu.PrefetchScalarGridSpec(
            num_scalar_prefetch=3,
            grid=(tiles_here // block,),
            in_specs=[
                pl.BlockSpec(memory_space=pltpu.SMEM),
                pl.BlockSpec((block, pixels, columns), lambda i, *s: (i, 0, 0)),
                pl.BlockSpec((block, pixels, columns), lambda i, *s: (i % per_frame, 0, 0)),
                pl.BlockSpec((block, pixels, voxels), lambda i, *s: (i, 0, 0)),
                pl.BlockSpec((block, pixels, voxels), lambda i, *s: (i, 0, 0)),
            ],
            out_specs=pl.BlockSpec((devices_all, 1, total), lambda i, *s: (0, 0, 0)),
            scratch_shapes=[pltpu.SMEM((devices_all,), jnp.int32)],
        ),
        out_shape=jax.ShapeDtypeStruct((devices_all, 1, total), jnp.float32),
    )(
        owner,
        box,
        angles,
        lorentz,
        counts.reshape(tiles_here, pixels, columns),
        efficiency,
        row_split.reshape(tiles_here, pixels, voxels),
        col_split.reshape(tiles_here, pixels, voxels),
    )


def shards(counts, row_split, col_split, efficiency, lorentz, angles, tile_owner, tile_box):
    frames_here, tiles_frame, pixels, unused_width = counts.shape
    voxels = row_split.shape[-1]
    size_x = lax.axis_size("bx")
    size_y = lax.axis_size("by")
    size_z = lax.axis_size("bz")
    devices_all = size_x * size_y * size_z
    tiles_here = frames_here * tiles_frame
    capacity = max(4, 4 * tiles_here // devices_all)
    local_x = GX // size_x
    local_y = GY // size_y
    local_z = GZ // size_z
    boxes_here = local_x * local_y * local_z * BOX_BRICK
    packed = tile_payload(
        counts, row_split, col_split, efficiency, lorentz, angles,
        tile_owner[:, 0], tile_box, devices_all, capacity,
    )
    arrived = lax.all_to_all(packed, ("bx", "by", "bz"), split_axis=0, concat_axis=0, tiled=True)
    arrived = arrived.reshape(devices_all, -1)
    arrived_payload = arrived[:, : capacity * 2 * voxels].reshape(devices_all * capacity, 2 * voxels)
    arrived_ids = arrived[:, capacity * 2 * voxels : capacity * 2 * voxels + capacity].reshape(
        devices_all * capacity
    )
    wanted = (
        jnp.arange(boxes_here, dtype=jnp.float32)[:, None] == arrived_ids[None, :]
    ).astype(jnp.float32)
    sums = jnp.dot(
        wanted, arrived_payload, precision=lax.Precision.HIGHEST, preferred_element_type=jnp.float32
    )
    row_sizes = (local_x, local_y, local_z, BOXX, BOXY, BOXZ)
    lane_sizes = (VX, VY, VZ)
    result = laue_average(sums, row_sizes, lane_sizes)
    return result.reshape(local_x, local_y, local_z, BOX_BRICK, voxels)


def solution(mesh):
    return jax.shard_map(
        shards,
        mesh=mesh,
        in_specs=(
            P(("bx", "by", "bz"), None, None, None),
            P(("bx", "by", "bz"), None, None, None),
            P(("bx", "by", "bz"), None, None, None),
            P(),
            P(),
            P(("bx", "by", "bz")),
            P(("bx", "by", "bz"), None),
            P(("bx", "by", "bz")),
        ),
        out_specs=P("bx", "by", "bz", None, None),
        check_vma=False,
    )
```

```python
import functools

import numpy as np
import jax
import jax.numpy as jnp
from jax import lax
from jax.sharding import PartitionSpec as P
from jax.experimental import pallas as pl
from jax.experimental.pallas import tpu as pltpu

VX = 8
VY = 8
VZ = 4
GX = 8
GY = 8
GZ = 4
BOXX = 4
BOXY = 4
BOXZ = 4
BOX_BRICK = 64


def flip_mask(sizes, flipped):
    mask, stride = 0, 1
    for dim in reversed(range(len(sizes))):
        assert sizes[dim] & (sizes[dim] - 1) == 0
        if dim in flipped:
            mask |= (sizes[dim] - 1) * stride
        stride *= sizes[dim]
    return mask


def flip_matrices(row_sizes, lane_sizes, stage):
    rows = int(np.prod(row_sizes))
    lanes = int(np.prod(lane_sizes))
    out_row = lax.broadcasted_iota(jnp.int32, (rows, rows), 0)
    in_row = lax.broadcasted_iota(jnp.int32, (rows, rows), 1)
    row_flip = (in_row == (out_row ^ flip_mask(row_sizes, (stage, stage + 3)))).astype(jnp.float32)
    in_lane = lax.broadcasted_iota(jnp.int32, (lanes, lanes), 0)
    out_lane = lax.broadcasted_iota(jnp.int32, (lanes, lanes), 1)
    lane_flip = (in_lane == (out_lane ^ flip_mask(lane_sizes, (stage,)))).astype(jnp.float32)
    return row_flip, lane_flip


def split_three(x):
    hi = x.astype(jnp.bfloat16)
    rest = x - hi.astype(jnp.float32)
    mid = rest.astype(jnp.bfloat16)
    lo = (rest - mid.astype(jnp.float32)).astype(jnp.bfloat16)
    return hi, mid, lo


def flipped(pair, row_sizes, lane_sizes, stage):
    row_flip, lane_flip = flip_matrices(row_sizes, lane_sizes, stage)
    row_flip = row_flip.astype(jnp.bfloat16)
    lane_flip = lane_flip.astype(jnp.bfloat16)
    result = []
    for half in pair:
        parts = []
        for piece in split_three(half):
            moved = jnp.dot(row_flip, piece, preferred_element_type=jnp.float32).astype(jnp.bfloat16)
            parts.append(jnp.dot(moved, lane_flip, preferred_element_type=jnp.float32))
        result.append((parts[0] + parts[1]) + parts[2])
    return result


def averaged(pair, other):
    return [0.5 * (mine + moved) for mine, moved in zip(pair, other)]


def laue_kernel(row_sizes, lane_sizes, sums_ref, out_ref, received, held, send_sems, recv_sems):
    voxels = int(np.prod(lane_sizes))
    axes = ("bx", "by", "bz")
    here = tuple(lax.axis_index(axis) for axis in axes)
    sizes = tuple(lax.axis_size(axis) for axis in axes)

    def mirror(flags):
        return tuple(sizes[a] - 1 - here[a] if flags[a] else here[a] for a in range(3))

    first = (mirror((1, 0, 0)), mirror((0, 1, 0)), mirror((1, 1, 0)))
    last = mirror((0, 0, 1))
    barrier = pltpu.get_barrier_semaphore()
    for target in first + (last,):
        pl.semaphore_signal(barrier, 1, device_id=target, device_id_type=pl.DeviceIdType.MESH)
    pl.semaphore_wait(barrier, 4)

    def send(source, slot, target):
        copy = pltpu.make_async_remote_copy(
            src_ref=source,
            dst_ref=received.at[slot],
            send_sem=send_sems.at[slot],
            recv_sem=recv_sems.at[slot],
            device_id=target,
            device_id_type=pl.DeviceIdType.MESH,
        )
        copy.start()
        return copy

    copies = [send(sums_ref, slot, target) for slot, target in enumerate(first)]
    for copy in copies:
        copy.wait()

    def halves(ref):
        return [ref[:, :voxels], ref[:, voxels:]]

    stage_x = averaged(halves(sums_ref), flipped(halves(received.at[0]), row_sizes, lane_sizes, 0))
    stage_x_there = averaged(
        halves(received.at[1]), flipped(halves(received.at[2]), row_sizes, lane_sizes, 0)
    )
    stage_y = averaged(stage_x, flipped(stage_x_there, row_sizes, lane_sizes, 1))
    held[:, :voxels] = stage_y[0]
    held[:, voxels:] = stage_y[1]
    copy = send(held, 3, last)
    copy.wait()
    stage_z = averaged(halves(held), flipped(halves(received.at[3]), row_sizes, lane_sizes, 2))
    out_ref[...] = stage_z[0] / jnp.maximum(stage_z[1], 1.0)


def laue_average(sums, row_sizes, lane_sizes):
    rows, width = sums.shape
    voxels = width // 2
    return pl.pallas_call(
        functools.partial(laue_kernel, row_sizes, lane_sizes),
        in_specs=[pl.BlockSpec(memory_space=pltpu.VMEM)],
        out_specs=pl.BlockSpec(memory_space=pltpu.VMEM),
        out_shape=jax.ShapeDtypeStruct((rows, voxels), jnp.float32),
        scratch_shapes=[
            pltpu.VMEM((4, rows, width), jnp.float32),
            pltpu.VMEM((rows, width), jnp.float32),
            pltpu.SemaphoreType.DMA((4,)),
            pltpu.SemaphoreType.DMA((4,)),
        ],
        compiler_params=pltpu.CompilerParams(collective_id=0, has_side_effects=True),
    )(sums)


def tile_kernel(
    capacity, tiles_frame, owner_ref, box_ref, angle_ref, lorentz_ref,
    counts_ref, eff_ref, rows_ref, cols_ref, out_ref, taken,
):
    block, unused_pixels, voxels = rows_ref.shape
    devices_all, unused_one, total = out_ref.shape
    width = 2 * voxels
    step = pl.program_id(0)

    @pl.when(step == 0)
    def _():
        out_ref[:, :, : capacity * width] = jnp.zeros((devices_all, 1, capacity * width), jnp.float32)
        out_ref[:, :, capacity * width :] = jnp.full((devices_all, 1, total - capacity * width), -1.0, jnp.float32)

        def clear(d, carry):
            taken[d] = 0
            return carry

        lax.fori_loop(0, devices_all, clear, 0)

    lanes = lax.broadcasted_iota(jnp.int32, (1, total - capacity * width), 1)
    for t in range(block):
        tile = step * block + t
        target = owner_ref[tile]
        rank = taken[target]
        taken[target] = rank + 1
        factor = lorentz_ref[angle_ref[tile // tiles_frame]]
        cols = cols_ref[t]
        rows = rows_ref[t].astype(jnp.float32)
        position = (step * block + t) % tiles_frame
        both = jnp.dot(
            jnp.concatenate([counts_ref[t], eff_ref[position]], axis=0), cols, preferred_element_type=jnp.float32
        )
        counted = both[: counts_ref.shape[1]]
        seen = both[counts_ref.shape[1] :]
        value = jnp.sum(rows * counted, axis=0, keepdims=True)
        weight = jnp.sum(rows * seen, axis=0, keepdims=True)
        start = pl.multiple_of(rank * width, width)
        out_ref[target, :, pl.ds(start, voxels)] = value * factor
        out_ref[target, :, pl.ds(start + voxels, voxels)] = weight
        label = jnp.full(lanes.shape, box_ref[tile], jnp.int32).astype(jnp.float32)
        out_ref[target, :, capacity * width :] = jnp.where(
            lanes == rank, label, out_ref[target, :, capacity * width :]
        )


def tile_payload(counts, row_split, col_split, efficiency, lorentz, angles, owner, box, devices_all, capacity):
    frames_here, tiles_frame, pixels, columns = counts.shape
    voxels = row_split.shape[-1]
    tiles_here = frames_here * tiles_frame
    label_width = 128
    block = 32
    total = capacity * 2 * voxels + label_width
    return pl.pallas_call(
        functools.partial(tile_kernel, capacity, tiles_frame),
        grid_spec=pltpu.PrefetchScalarGridSpec(
            num_scalar_prefetch=3,
            grid=(tiles_here // block,),
            in_specs=[
                pl.BlockSpec(memory_space=pltpu.SMEM),
                pl.BlockSpec((block, pixels, columns), lambda i, *s: (i, 0, 0)),
                pl.BlockSpec((tiles_frame, pixels, columns), lambda i, *s: (0, 0, 0)),
                pl.BlockSpec((block, pixels, voxels), lambda i, *s: (i, 0, 0)),
                pl.BlockSpec((block, pixels, voxels), lambda i, *s: (i, 0, 0)),
            ],
            out_specs=pl.BlockSpec((devices_all, 1, total), lambda i, *s: (0, 0, 0)),
            scratch_shapes=[pltpu.SMEM((devices_all,), jnp.int32)],
        ),
        out_shape=jax.ShapeDtypeStruct((devices_all, 1, total), jnp.float32),
    )(
        owner,
        box,
        angles,
        lorentz,
        counts.reshape(tiles_here, pixels, columns),
        efficiency,
        row_split.reshape(tiles_here, pixels, voxels),
        col_split.reshape(tiles_here, pixels, voxels),
    )


def shards(counts, row_split, col_split, efficiency, lorentz, angles, tile_owner, tile_box):
    frames_here, tiles_frame, pixels, unused_width = counts.shape
    voxels = row_split.shape[-1]
    size_x = lax.axis_size("bx")
    size_y = lax.axis_size("by")
    size_z = lax.axis_size("bz")
    devices_all = size_x * size_y * size_z
    tiles_here = frames_here * tiles_frame
    capacity = max(4, 4 * tiles_here // devices_all)
    local_x = GX // size_x
    local_y = GY // size_y
    local_z = GZ // size_z
    boxes_here = local_x * local_y * local_z * BOX_BRICK
    packed = tile_payload(
        counts, row_split, col_split, efficiency, lorentz, angles,
        tile_owner[:, 0], tile_box, devices_all, capacity,
    )
    arrived = lax.all_to_all(packed, ("bx", "by", "bz"), split_axis=0, concat_axis=0, tiled=True)
    arrived = arrived.reshape(devices_all, -1)
    arrived_payload = arrived[:, : capacity * 2 * voxels].reshape(devices_all * capacity, 2 * voxels)
    arrived_ids = arrived[:, capacity * 2 * voxels : capacity * 2 * voxels + capacity].reshape(
        devices_all * capacity
    )
    wanted = (
        jnp.arange(boxes_here, dtype=jnp.float32)[:, None] == arrived_ids[None, :]
    ).astype(jnp.float32)
    sums = jnp.dot(
        wanted, arrived_payload, precision=lax.Precision.HIGHEST, preferred_element_type=jnp.float32
    )
    row_sizes = (local_x, local_y, local_z, BOXX, BOXY, BOXZ)
    lane_sizes = (VX, VY, VZ)
    result = laue_average(sums, row_sizes, lane_sizes)
    return result.reshape(local_x, local_y, local_z, BOX_BRICK, voxels)


def solution(mesh):
    return jax.shard_map(
        shards,
        mesh=mesh,
        in_specs=(
            P(("bx", "by", "bz"), None, None, None),
            P(("bx", "by", "bz"), None, None, None),
            P(("bx", "by", "bz"), None, None, None),
            P(),
            P(),
            P(("bx", "by", "bz")),
            P(("bx", "by", "bz"), None),
            P(("bx", "by", "bz")),
        ),
        out_specs=P("bx", "by", "bz", None, None),
        check_vma=False,
    )
```

```python
import functools

import numpy as np
import jax
import jax.numpy as jnp
from jax import lax
from jax.sharding import PartitionSpec as P
from jax.experimental import pallas as pl
from jax.experimental.pallas import tpu as pltpu

VX = 8
VY = 8
VZ = 4
GX = 8
GY = 8
GZ = 4
BOXX = 4
BOXY = 4
BOXZ = 4
BOX_BRICK = 64


def flip_mask(sizes, flipped):
    mask, stride = 0, 1
    for dim in reversed(range(len(sizes))):
        assert sizes[dim] & (sizes[dim] - 1) == 0
        if dim in flipped:
            mask |= (sizes[dim] - 1) * stride
        stride *= sizes[dim]
    return mask


def flip_matrices(row_sizes, lane_sizes, stage):
    rows = int(np.prod(row_sizes))
    lanes = int(np.prod(lane_sizes))
    out_row = lax.broadcasted_iota(jnp.int32, (rows, rows), 0)
    in_row = lax.broadcasted_iota(jnp.int32, (rows, rows), 1)
    row_flip = (in_row == (out_row ^ flip_mask(row_sizes, (stage, stage + 3)))).astype(jnp.float32)
    in_lane = lax.broadcasted_iota(jnp.int32, (lanes, lanes), 0)
    out_lane = lax.broadcasted_iota(jnp.int32, (lanes, lanes), 1)
    lane_flip = (in_lane == (out_lane ^ flip_mask(lane_sizes, (stage,)))).astype(jnp.float32)
    return row_flip, lane_flip


def split_three(x):
    hi = x.astype(jnp.bfloat16)
    rest = x - hi.astype(jnp.float32)
    mid = rest.astype(jnp.bfloat16)
    lo = (rest - mid.astype(jnp.float32)).astype(jnp.bfloat16)
    return hi, mid, lo


def flipped(pair, row_sizes, lane_sizes, stage):
    row_flip, lane_flip = flip_matrices(row_sizes, lane_sizes, stage)
    row_flip = row_flip.astype(jnp.bfloat16)
    lane_flip = lane_flip.astype(jnp.bfloat16)
    result = []
    for half in pair:
        parts = []
        for piece in split_three(half):
            moved = jnp.dot(row_flip, piece, preferred_element_type=jnp.float32).astype(jnp.bfloat16)
            parts.append(jnp.dot(moved, lane_flip, preferred_element_type=jnp.float32))
        result.append((parts[0] + parts[1]) + parts[2])
    return result


def averaged(pair, other):
    return [0.5 * (mine + moved) for mine, moved in zip(pair, other)]


def laue_kernel(row_sizes, lane_sizes, sums_ref, out_ref, received, held, send_sems, recv_sems):
    voxels = int(np.prod(lane_sizes))
    axes = ("bx", "by", "bz")
    here = tuple(lax.axis_index(axis) for axis in axes)
    sizes = tuple(lax.axis_size(axis) for axis in axes)

    def mirror(flags):
        return tuple(sizes[a] - 1 - here[a] if flags[a] else here[a] for a in range(3))

    first = (mirror((1, 0, 0)), mirror((0, 1, 0)), mirror((1, 1, 0)))
    last = mirror((0, 0, 1))
    barrier = pltpu.get_barrier_semaphore()
    for target in first + (last,):
        pl.semaphore_signal(barrier, 1, device_id=target, device_id_type=pl.DeviceIdType.MESH)
    pl.semaphore_wait(barrier, 4)

    def send(source, slot, target):
        copy = pltpu.make_async_remote_copy(
            src_ref=source,
            dst_ref=received.at[slot],
            send_sem=send_sems.at[slot],
            recv_sem=recv_sems.at[slot],
            device_id=target,
            device_id_type=pl.DeviceIdType.MESH,
        )
        copy.start()
        return copy

    copies = [send(sums_ref, slot, target) for slot, target in enumerate(first)]
    for copy in copies:
        copy.wait()

    def halves(ref):
        return [ref[:, :voxels], ref[:, voxels:]]

    stage_x = averaged(halves(sums_ref), flipped(halves(received.at[0]), row_sizes, lane_sizes, 0))
    stage_x_there = averaged(
        halves(received.at[1]), flipped(halves(received.at[2]), row_sizes, lane_sizes, 0)
    )
    stage_y = averaged(stage_x, flipped(stage_x_there, row_sizes, lane_sizes, 1))
    held[:, :voxels] = stage_y[0]
    held[:, voxels:] = stage_y[1]
    copy = send(held, 3, last)
    copy.wait()
    stage_z = averaged(halves(held), flipped(halves(received.at[3]), row_sizes, lane_sizes, 2))
    out_ref[...] = stage_z[0] / jnp.maximum(stage_z[1], 1.0)


def laue_average(sums, row_sizes, lane_sizes):
    rows, width = sums.shape
    voxels = width // 2
    return pl.pallas_call(
        functools.partial(laue_kernel, row_sizes, lane_sizes),
        in_specs=[pl.BlockSpec(memory_space=pltpu.VMEM)],
        out_specs=pl.BlockSpec(memory_space=pltpu.VMEM),
        out_shape=jax.ShapeDtypeStruct((rows, voxels), jnp.float32),
        scratch_shapes=[
            pltpu.VMEM((4, rows, width), jnp.float32),
            pltpu.VMEM((rows, width), jnp.float32),
            pltpu.SemaphoreType.DMA((4,)),
            pltpu.SemaphoreType.DMA((4,)),
        ],
        compiler_params=pltpu.CompilerParams(collective_id=0, has_side_effects=True),
    )(sums)


def tile_kernel(
    capacity, tiles_frame, owner_ref, box_ref, angle_ref, lorentz_ref,
    counts_ref, eff_ref, rows_ref, cols_ref, out_ref, taken,
):
    block, unused_pixels, voxels = rows_ref.shape
    devices_all, unused_one, total = out_ref.shape
    width = 2 * voxels
    step = pl.program_id(0)

    @pl.when(step == 0)
    def _():
        out_ref[:, :, : capacity * width] = jnp.zeros((devices_all, 1, capacity * width), jnp.float32)
        out_ref[:, :, capacity * width :] = jnp.full((devices_all, 1, total - capacity * width), -1.0, jnp.float32)

        def clear(d, carry):
            taken[d] = 0
            return carry

        lax.fori_loop(0, devices_all, clear, 0)

    lanes = lax.broadcasted_iota(jnp.int32, (1, total - capacity * width), 1)
    for t in range(block):
        tile = step * block + t
        target = owner_ref[tile]
        rank = taken[target]
        taken[target] = rank + 1
        factor = lorentz_ref[angle_ref[tile // tiles_frame]]
        cols = cols_ref[t]
        rows = rows_ref[t].astype(jnp.float32)
        both = jnp.dot(
            jnp.concatenate([counts_ref[t], eff_ref[t]], axis=0), cols, preferred_element_type=jnp.float32
        )
        counted = both[: counts_ref.shape[1]]
        seen = both[counts_ref.shape[1] :]
        value = jnp.sum(rows * counted, axis=0, keepdims=True)
        weight = jnp.sum(rows * seen, axis=0, keepdims=True)
        start = pl.multiple_of(rank * width, width)
        out_ref[target, :, pl.ds(start, voxels)] = value * factor
        out_ref[target, :, pl.ds(start + voxels, voxels)] = weight
        label = jnp.full(lanes.shape, box_ref[tile], jnp.int32).astype(jnp.float32)
        out_ref[target, :, capacity * width :] = jnp.where(
            lanes == rank, label, out_ref[target, :, capacity * width :]
        )


def tile_payload(counts, row_split, col_split, efficiency, lorentz, angles, owner, box, devices_all, capacity):
    frames_here, tiles_frame, pixels, columns = counts.shape
    voxels = row_split.shape[-1]
    tiles_here = frames_here * tiles_frame
    label_width = 128
    block = 32
    per_frame = tiles_frame // block
    total = capacity * 2 * voxels + label_width
    return pl.pallas_call(
        functools.partial(tile_kernel, capacity, tiles_frame),
        grid_spec=pltpu.PrefetchScalarGridSpec(
            num_scalar_prefetch=3,
            grid=(tiles_here // block,),
            in_specs=[
                pl.BlockSpec(memory_space=pltpu.SMEM),
                pl.BlockSpec((block, pixels, columns), lambda i, *s: (i, 0, 0)),
                pl.BlockSpec((block, pixels, columns), lambda i, *s: (i % per_frame, 0, 0)),
                pl.BlockSpec((block, pixels, voxels), lambda i, *s: (i, 0, 0)),
                pl.BlockSpec((block, pixels, voxels), lambda i, *s: (i, 0, 0)),
            ],
            out_specs=pl.BlockSpec((devices_all, 1, total), lambda i, *s: (0, 0, 0)),
            scratch_shapes=[pltpu.SMEM((devices_all,), jnp.int32)],
        ),
        out_shape=jax.ShapeDtypeStruct((devices_all, 1, total), jnp.float32),
    )(
        owner,
        box,
        angles,
        lorentz,
        counts.reshape(tiles_here, pixels, columns),
        efficiency,
        row_split.reshape(tiles_here, pixels, voxels),
        col_split.reshape(tiles_here, pixels, voxels),
    )


def shards(counts, row_split, col_split, efficiency, lorentz, angles, tile_owner, tile_box):
    frames_here, tiles_frame, pixels, unused_width = counts.shape
    voxels = row_split.shape[-1]
    size_x = lax.axis_size("bx")
    size_y = lax.axis_size("by")
    size_z = lax.axis_size("bz")
    devices_all = size_x * size_y * size_z
    tiles_here = frames_here * tiles_frame
    capacity = max(4, 4 * tiles_here // devices_all)
    local_x = GX // size_x
    local_y = GY // size_y
    local_z = GZ // size_z
    boxes_here = local_x * local_y * local_z * BOX_BRICK
    packed = tile_payload(
        counts, row_split, col_split, efficiency, lorentz, angles,
        tile_owner[:, 0], tile_box, devices_all, capacity,
    )
    packed = packed.reshape(size_x * size_y, size_z, 1, -1)
    packed = lax.all_to_all(packed, "bz", split_axis=1, concat_axis=1, tiled=True)
    arrived = lax.all_to_all(packed, ("bx", "by"), split_axis=0, concat_axis=0, tiled=True)
    arrived = arrived.reshape(devices_all, -1)
    arrived_payload = arrived[:, : capacity * 2 * voxels].reshape(devices_all * capacity, 2 * voxels)
    arrived_ids = arrived[:, capacity * 2 * voxels : capacity * 2 * voxels + capacity].reshape(
        devices_all * capacity
    )
    wanted = (
        jnp.arange(boxes_here, dtype=jnp.float32)[:, None] == arrived_ids[None, :]
    ).astype(jnp.float32)
    sums = jnp.dot(
        wanted, arrived_payload, precision=lax.Precision.HIGHEST, preferred_element_type=jnp.float32
    )
    row_sizes = (local_x, local_y, local_z, BOXX, BOXY, BOXZ)
    lane_sizes = (VX, VY, VZ)
    result = laue_average(sums, row_sizes, lane_sizes)
    return result.reshape(local_x, local_y, local_z, BOX_BRICK, voxels)


def solution(mesh):
    return jax.shard_map(
        shards,
        mesh=mesh,
        in_specs=(
            P(("bx", "by", "bz"), None, None, None),
            P(("bx", "by", "bz"), None, None, None),
            P(("bx", "by", "bz"), None, None, None),
            P(),
            P(),
            P(("bx", "by", "bz")),
            P(("bx", "by", "bz"), None),
            P(("bx", "by", "bz")),
        ),
        out_specs=P("bx", "by", "bz", None, None),
        check_vma=False,
    )
```

```python
import functools

import numpy as np
import jax
import jax.numpy as jnp
from jax import lax
from jax.sharding import PartitionSpec as P
from jax.experimental import pallas as pl
from jax.experimental.pallas import tpu as pltpu

VX = 8
VY = 8
VZ = 4
GX = 8
GY = 8
GZ = 4
BOXX = 4
BOXY = 4
BOXZ = 4
BOX_BRICK = 64


def flip_mask(sizes, flipped):
    mask, stride = 0, 1
    for dim in reversed(range(len(sizes))):
        assert sizes[dim] & (sizes[dim] - 1) == 0
        if dim in flipped:
            mask |= (sizes[dim] - 1) * stride
        stride *= sizes[dim]
    return mask


def flip_matrices(row_sizes, lane_sizes, stage):
    rows = int(np.prod(row_sizes))
    lanes = int(np.prod(lane_sizes))
    out_row = lax.broadcasted_iota(jnp.int32, (rows, rows), 0)
    in_row = lax.broadcasted_iota(jnp.int32, (rows, rows), 1)
    row_flip = (in_row == (out_row ^ flip_mask(row_sizes, (stage, stage + 3)))).astype(jnp.float32)
    in_lane = lax.broadcasted_iota(jnp.int32, (lanes, lanes), 0)
    out_lane = lax.broadcasted_iota(jnp.int32, (lanes, lanes), 1)
    lane_flip = (in_lane == (out_lane ^ flip_mask(lane_sizes, (stage,)))).astype(jnp.float32)
    return row_flip, lane_flip


def split_three(x):
    hi = x.astype(jnp.bfloat16)
    rest = x - hi.astype(jnp.float32)
    mid = rest.astype(jnp.bfloat16)
    lo = (rest - mid.astype(jnp.float32)).astype(jnp.bfloat16)
    return hi, mid, lo


def flipped(pair, row_sizes, lane_sizes, stage):
    row_flip, lane_flip = flip_matrices(row_sizes, lane_sizes, stage)
    row_flip = row_flip.astype(jnp.bfloat16)
    lane_flip = lane_flip.astype(jnp.bfloat16)
    result = []
    for half in pair:
        parts = []
        for piece in split_three(half):
            moved = jnp.dot(row_flip, piece, preferred_element_type=jnp.float32).astype(jnp.bfloat16)
            parts.append(jnp.dot(moved, lane_flip, preferred_element_type=jnp.float32))
        result.append((parts[0] + parts[1]) + parts[2])
    return result


def averaged(pair, other):
    return [0.5 * (mine + moved) for mine, moved in zip(pair, other)]


def laue_kernel(row_sizes, lane_sizes, sums_ref, out_ref, received, held, send_sems, recv_sems):
    voxels = int(np.prod(lane_sizes))
    axes = ("bx", "by", "bz")
    here = tuple(lax.axis_index(axis) for axis in axes)
    sizes = tuple(lax.axis_size(axis) for axis in axes)

    def mirror(flags):
        return tuple(sizes[a] - 1 - here[a] if flags[a] else here[a] for a in range(3))

    first = (mirror((1, 0, 0)), mirror((0, 1, 0)), mirror((1, 1, 0)))
    last = mirror((0, 0, 1))
    barrier = pltpu.get_barrier_semaphore()
    for target in first + (last,):
        pl.semaphore_signal(barrier, 1, device_id=target, device_id_type=pl.DeviceIdType.MESH)
    pl.semaphore_wait(barrier, 4)

    def send(source, slot, target):
        copy = pltpu.make_async_remote_copy(
            src_ref=source,
            dst_ref=received.at[slot],
            send_sem=send_sems.at[slot],
            recv_sem=recv_sems.at[slot],
            device_id=target,
            device_id_type=pl.DeviceIdType.MESH,
        )
        copy.start()
        return copy

    copies = [send(sums_ref, slot, target) for slot, target in enumerate(first)]
    for copy in copies:
        copy.wait()

    def halves(ref):
        return [ref[:, :voxels], ref[:, voxels:]]

    stage_x = averaged(halves(sums_ref), flipped(halves(received.at[0]), row_sizes, lane_sizes, 0))
    stage_x_there = averaged(
        halves(received.at[1]), flipped(halves(received.at[2]), row_sizes, lane_sizes, 0)
    )
    stage_y = averaged(stage_x, flipped(stage_x_there, row_sizes, lane_sizes, 1))
    held[:, :voxels] = stage_y[0]
    held[:, voxels:] = stage_y[1]
    copy = send(held, 3, last)
    copy.wait()
    stage_z = averaged(halves(held), flipped(halves(received.at[3]), row_sizes, lane_sizes, 2))
    out_ref[...] = stage_z[0] / jnp.maximum(stage_z[1], 1.0)


def laue_average(sums, row_sizes, lane_sizes):
    rows, width = sums.shape
    voxels = width // 2
    return pl.pallas_call(
        functools.partial(laue_kernel, row_sizes, lane_sizes),
        in_specs=[pl.BlockSpec(memory_space=pltpu.VMEM)],
        out_specs=pl.BlockSpec(memory_space=pltpu.VMEM),
        out_shape=jax.ShapeDtypeStruct((rows, voxels), jnp.float32),
        scratch_shapes=[
            pltpu.VMEM((4, rows, width), jnp.float32),
            pltpu.VMEM((rows, width), jnp.float32),
            pltpu.SemaphoreType.DMA((4,)),
            pltpu.SemaphoreType.DMA((4,)),
        ],
        compiler_params=pltpu.CompilerParams(collective_id=0, has_side_effects=True),
    )(sums)


def tile_kernel(
    capacity, tiles_frame, frames, owner_ref, box_ref, angle_ref, lorentz_ref,
    counts_ref, eff_ref, rows_ref, cols_ref, out_ref, taken,
):
    block, unused_pixels, voxels = rows_ref.shape
    devices_all, unused_one, total = out_ref.shape
    width = 2 * voxels
    step = pl.program_id(0)

    @pl.when(step == 0)
    def _():
        out_ref[:, :, : capacity * width] = jnp.zeros((devices_all, 1, capacity * width), jnp.float32)
        out_ref[:, :, capacity * width :] = jnp.full((devices_all, 1, total - capacity * width), -1.0, jnp.float32)

        def clear(d, carry):
            taken[d] = 0
            return carry

        lax.fori_loop(0, devices_all, clear, 0)

    lanes = lax.broadcasted_iota(jnp.int32, (1, total - capacity * width), 1)
    for t in range(block):
        tile = ((step % frames) * (tiles_frame // block) + step // frames) * block + t
        target = owner_ref[tile]
        rank = taken[target]
        taken[target] = rank + 1
        factor = lorentz_ref[angle_ref[tile // tiles_frame]]
        cols = cols_ref[t]
        rows = rows_ref[t].astype(jnp.float32)
        both = jnp.dot(
            jnp.concatenate([counts_ref[t], eff_ref[t]], axis=0), cols, preferred_element_type=jnp.float32
        )
        counted = both[: counts_ref.shape[1]]
        seen = both[counts_ref.shape[1] :]
        value = jnp.sum(rows * counted, axis=0, keepdims=True)
        weight = jnp.sum(rows * seen, axis=0, keepdims=True)
        start = pl.multiple_of(rank * width, width)
        out_ref[target, :, pl.ds(start, voxels)] = value * factor
        out_ref[target, :, pl.ds(start + voxels, voxels)] = weight
        label = jnp.full(lanes.shape, box_ref[tile], jnp.int32).astype(jnp.float32)
        out_ref[target, :, capacity * width :] = jnp.where(
            lanes == rank, label, out_ref[target, :, capacity * width :]
        )


def tile_payload(counts, row_split, col_split, efficiency, lorentz, angles, owner, box, devices_all, capacity):
    frames_here, tiles_frame, pixels, columns = counts.shape
    voxels = row_split.shape[-1]
    tiles_here = frames_here * tiles_frame
    label_width = 128
    block = 32
    per_frame = tiles_frame // block

    def order(i):
        return (i % frames_here) * per_frame + i // frames_here

    total = capacity * 2 * voxels + label_width
    return pl.pallas_call(
        functools.partial(tile_kernel, capacity, tiles_frame, frames_here),
        grid_spec=pltpu.PrefetchScalarGridSpec(
            num_scalar_prefetch=3,
            grid=(tiles_here // block,),
            in_specs=[
                pl.BlockSpec(memory_space=pltpu.SMEM),
                pl.BlockSpec((block, pixels, columns), lambda i, *s: (order(i), 0, 0)),
                pl.BlockSpec((block, pixels, columns), lambda i, *s: (i // frames_here, 0, 0)),
                pl.BlockSpec((block, pixels, voxels), lambda i, *s: (order(i), 0, 0)),
                pl.BlockSpec((block, pixels, voxels), lambda i, *s: (order(i), 0, 0)),
            ],
            out_specs=pl.BlockSpec((devices_all, 1, total), lambda i, *s: (0, 0, 0)),
            scratch_shapes=[pltpu.SMEM((devices_all,), jnp.int32)],
        ),
        out_shape=jax.ShapeDtypeStruct((devices_all, 1, total), jnp.float32),
    )(
        owner,
        box,
        angles,
        lorentz,
        counts.reshape(tiles_here, pixels, columns),
        efficiency,
        row_split.reshape(tiles_here, pixels, voxels),
        col_split.reshape(tiles_here, pixels, voxels),
    )


def shards(counts, row_split, col_split, efficiency, lorentz, angles, tile_owner, tile_box):
    frames_here, tiles_frame, pixels, unused_width = counts.shape
    voxels = row_split.shape[-1]
    size_x = lax.axis_size("bx")
    size_y = lax.axis_size("by")
    size_z = lax.axis_size("bz")
    devices_all = size_x * size_y * size_z
    tiles_here = frames_here * tiles_frame
    capacity = max(4, 4 * tiles_here // devices_all)
    local_x = GX // size_x
    local_y = GY // size_y
    local_z = GZ // size_z
    boxes_here = local_x * local_y * local_z * BOX_BRICK
    packed = tile_payload(
        counts, row_split, col_split, efficiency, lorentz, angles,
        tile_owner[:, 0], tile_box, devices_all, capacity,
    )
    arrived = lax.all_to_all(packed, ("bx", "by", "bz"), split_axis=0, concat_axis=0, tiled=True)
    arrived = arrived.reshape(devices_all, -1)
    arrived_payload = arrived[:, : capacity * 2 * voxels].reshape(devices_all * capacity, 2 * voxels)
    arrived_ids = arrived[:, capacity * 2 * voxels : capacity * 2 * voxels + capacity].reshape(
        devices_all * capacity
    )
    wanted = (
        jnp.arange(boxes_here, dtype=jnp.float32)[:, None] == arrived_ids[None, :]
    ).astype(jnp.float32)
    sums = jnp.dot(
        wanted, arrived_payload, precision=lax.Precision.HIGHEST, preferred_element_type=jnp.float32
    )
    row_sizes = (local_x, local_y, local_z, BOXX, BOXY, BOXZ)
    lane_sizes = (VX, VY, VZ)
    result = laue_average(sums, row_sizes, lane_sizes)
    return result.reshape(local_x, local_y, local_z, BOX_BRICK, voxels)


def solution(mesh):
    return jax.shard_map(
        shards,
        mesh=mesh,
        in_specs=(
            P(("bx", "by", "bz"), None, None, None),
            P(("bx", "by", "bz"), None, None, None),
            P(("bx", "by", "bz"), None, None, None),
            P(),
            P(),
            P(("bx", "by", "bz")),
            P(("bx", "by", "bz"), None),
            P(("bx", "by", "bz")),
        ),
        out_specs=P("bx", "by", "bz", None, None),
        check_vma=False,
    )
```

```python
import functools

import numpy as np
import jax
import jax.numpy as jnp
from jax import lax
from jax.sharding import PartitionSpec as P
from jax.experimental import pallas as pl
from jax.experimental.pallas import tpu as pltpu

VX = 8
VY = 8
VZ = 4
GX = 8
GY = 8
GZ = 4
BOXX = 4
BOXY = 4
BOXZ = 4
BOX_BRICK = 64


def flip_mask(sizes, flipped):
    mask, stride = 0, 1
    for dim in reversed(range(len(sizes))):
        assert sizes[dim] & (sizes[dim] - 1) == 0
        if dim in flipped:
            mask |= (sizes[dim] - 1) * stride
        stride *= sizes[dim]
    return mask


def flip_matrices(row_sizes, lane_sizes, stage):
    rows = int(np.prod(row_sizes))
    lanes = int(np.prod(lane_sizes))
    out_row = lax.broadcasted_iota(jnp.int32, (rows, rows), 0)
    in_row = lax.broadcasted_iota(jnp.int32, (rows, rows), 1)
    row_flip = (in_row == (out_row ^ flip_mask(row_sizes, (stage, stage + 3)))).astype(jnp.float32)
    in_lane = lax.broadcasted_iota(jnp.int32, (lanes, lanes), 0)
    out_lane = lax.broadcasted_iota(jnp.int32, (lanes, lanes), 1)
    lane_flip = (in_lane == (out_lane ^ flip_mask(lane_sizes, (stage,)))).astype(jnp.float32)
    return row_flip, lane_flip


def split_three(x):
    hi = x.astype(jnp.bfloat16)
    rest = x - hi.astype(jnp.float32)
    mid = rest.astype(jnp.bfloat16)
    lo = (rest - mid.astype(jnp.float32)).astype(jnp.bfloat16)
    return hi, mid, lo


def flipped(pair, row_sizes, lane_sizes, stage):
    row_flip, lane_flip = flip_matrices(row_sizes, lane_sizes, stage)
    row_flip = row_flip.astype(jnp.bfloat16)
    lane_flip = lane_flip.astype(jnp.bfloat16)
    result = []
    for half in pair:
        parts = []
        for piece in split_three(half):
            moved = jnp.dot(row_flip, piece, preferred_element_type=jnp.float32).astype(jnp.bfloat16)
            parts.append(jnp.dot(moved, lane_flip, preferred_element_type=jnp.float32))
        result.append((parts[0] + parts[1]) + parts[2])
    return result


def averaged(pair, other):
    return [0.5 * (mine + moved) for mine, moved in zip(pair, other)]


def laue_kernel(row_sizes, lane_sizes, sums_ref, out_ref, received, held, send_sems, recv_sems):
    voxels = int(np.prod(lane_sizes))
    axes = ("bx", "by", "bz")
    here = tuple(lax.axis_index(axis) for axis in axes)
    sizes = tuple(lax.axis_size(axis) for axis in axes)

    def mirror(flags):
        return tuple(sizes[a] - 1 - here[a] if flags[a] else here[a] for a in range(3))

    first = (mirror((1, 0, 0)), mirror((0, 1, 0)), mirror((1, 1, 0)))
    last = mirror((0, 0, 1))
    barrier = pltpu.get_barrier_semaphore()
    for target in first + (last,):
        pl.semaphore_signal(barrier, 1, device_id=target, device_id_type=pl.DeviceIdType.MESH)
    pl.semaphore_wait(barrier, 4)

    def send(source, slot, target):
        copy = pltpu.make_async_remote_copy(
            src_ref=source,
            dst_ref=received.at[slot],
            send_sem=send_sems.at[slot],
            recv_sem=recv_sems.at[slot],
            device_id=target,
            device_id_type=pl.DeviceIdType.MESH,
        )
        copy.start()
        return copy

    copies = [send(sums_ref, slot, target) for slot, target in enumerate(first)]

    def halves(ref):
        return [ref[:, :voxels], ref[:, voxels:]]

    copies[0].wait()
    stage_x = averaged(halves(sums_ref), flipped(halves(received.at[0]), row_sizes, lane_sizes, 0))
    copies[1].wait()
    copies[2].wait()
    stage_x_there = averaged(
        halves(received.at[1]), flipped(halves(received.at[2]), row_sizes, lane_sizes, 0)
    )
    stage_y = averaged(stage_x, flipped(stage_x_there, row_sizes, lane_sizes, 1))
    held[:, :voxels] = stage_y[0]
    held[:, voxels:] = stage_y[1]
    copy = send(held, 3, last)
    copy.wait()
    stage_z = averaged(halves(held), flipped(halves(received.at[3]), row_sizes, lane_sizes, 2))
    out_ref[...] = stage_z[0] / jnp.maximum(stage_z[1], 1.0)


def laue_average(sums, row_sizes, lane_sizes):
    rows, width = sums.shape
    voxels = width // 2
    return pl.pallas_call(
        functools.partial(laue_kernel, row_sizes, lane_sizes),
        in_specs=[pl.BlockSpec(memory_space=pltpu.VMEM)],
        out_specs=pl.BlockSpec(memory_space=pltpu.VMEM),
        out_shape=jax.ShapeDtypeStruct((rows, voxels), jnp.float32),
        scratch_shapes=[
            pltpu.VMEM((4, rows, width), jnp.float32),
            pltpu.VMEM((rows, width), jnp.float32),
            pltpu.SemaphoreType.DMA((4,)),
            pltpu.SemaphoreType.DMA((4,)),
        ],
        compiler_params=pltpu.CompilerParams(collective_id=0, has_side_effects=True),
    )(sums)


def tile_kernel(
    capacity, tiles_frame, frames, owner_ref, box_ref, angle_ref, lorentz_ref,
    counts_ref, eff_ref, rows_ref, cols_ref, out_ref, taken,
):
    block, unused_pixels, voxels = rows_ref.shape
    devices_all, unused_one, total = out_ref.shape
    width = 2 * voxels
    step = pl.program_id(0)

    @pl.when(step == 0)
    def _():
        out_ref[:, :, : capacity * width] = jnp.zeros((devices_all, 1, capacity * width), jnp.float32)
        out_ref[:, :, capacity * width :] = jnp.full((devices_all, 1, total - capacity * width), -1.0, jnp.float32)

        def clear(d, carry):
            taken[d] = 0
            return carry

        lax.fori_loop(0, devices_all, clear, 0)

    lanes = lax.broadcasted_iota(jnp.int32, (1, total - capacity * width), 1)
    for t in range(block):
        tile = ((step % frames) * (tiles_frame // block) + step // frames) * block + t
        target = owner_ref[tile]
        rank = taken[target]
        taken[target] = rank + 1
        factor = lorentz_ref[angle_ref[tile // tiles_frame]]
        cols = cols_ref[t]
        rows = rows_ref[t].astype(jnp.float32)
        both = jnp.dot(
            jnp.concatenate([counts_ref[t], eff_ref[t]], axis=0), cols, preferred_element_type=jnp.float32
        )
        counted = both[: counts_ref.shape[1]]
        seen = both[counts_ref.shape[1] :]
        value = jnp.sum(rows * counted, axis=0, keepdims=True)
        weight = jnp.sum(rows * seen, axis=0, keepdims=True)
        start = pl.multiple_of(rank * width, width)
        out_ref[target, :, pl.ds(start, voxels)] = value * factor
        out_ref[target, :, pl.ds(start + voxels, voxels)] = weight
        label = jnp.full(lanes.shape, box_ref[tile], jnp.int32).astype(jnp.float32)
        out_ref[target, :, capacity * width :] = jnp.where(
            lanes == rank, label, out_ref[target, :, capacity * width :]
        )


def tile_payload(counts, row_split, col_split, efficiency, lorentz, angles, owner, box, devices_all, capacity):
    frames_here, tiles_frame, pixels, columns = counts.shape
    voxels = row_split.shape[-1]
    tiles_here = frames_here * tiles_frame
    label_width = 128
    block = 32
    per_frame = tiles_frame // block

    def order(i):
        return (i % frames_here) * per_frame + i // frames_here

    total = capacity * 2 * voxels + label_width
    return pl.pallas_call(
        functools.partial(tile_kernel, capacity, tiles_frame, frames_here),
        grid_spec=pltpu.PrefetchScalarGridSpec(
            num_scalar_prefetch=3,
            grid=(tiles_here // block,),
            in_specs=[
                pl.BlockSpec(memory_space=pltpu.SMEM),
                pl.BlockSpec((block, pixels, columns), lambda i, *s: (order(i), 0, 0)),
                pl.BlockSpec((block, pixels, columns), lambda i, *s: (i // frames_here, 0, 0)),
                pl.BlockSpec((block, pixels, voxels), lambda i, *s: (order(i), 0, 0)),
                pl.BlockSpec((block, pixels, voxels), lambda i, *s: (order(i), 0, 0)),
            ],
            out_specs=pl.BlockSpec((devices_all, 1, total), lambda i, *s: (0, 0, 0)),
            scratch_shapes=[pltpu.SMEM((devices_all,), jnp.int32)],
        ),
        out_shape=jax.ShapeDtypeStruct((devices_all, 1, total), jnp.float32),
    )(
        owner,
        box,
        angles,
        lorentz,
        counts.reshape(tiles_here, pixels, columns),
        efficiency,
        row_split.reshape(tiles_here, pixels, voxels),
        col_split.reshape(tiles_here, pixels, voxels),
    )


def shards(counts, row_split, col_split, efficiency, lorentz, angles, tile_owner, tile_box):
    frames_here, tiles_frame, pixels, unused_width = counts.shape
    voxels = row_split.shape[-1]
    size_x = lax.axis_size("bx")
    size_y = lax.axis_size("by")
    size_z = lax.axis_size("bz")
    devices_all = size_x * size_y * size_z
    tiles_here = frames_here * tiles_frame
    capacity = max(4, 4 * tiles_here // devices_all)
    local_x = GX // size_x
    local_y = GY // size_y
    local_z = GZ // size_z
    boxes_here = local_x * local_y * local_z * BOX_BRICK
    packed = tile_payload(
        counts, row_split, col_split, efficiency, lorentz, angles,
        tile_owner[:, 0], tile_box, devices_all, capacity,
    )
    arrived = lax.all_to_all(packed, ("bx", "by", "bz"), split_axis=0, concat_axis=0, tiled=True)
    arrived = arrived.reshape(devices_all, -1)
    arrived_payload = arrived[:, : capacity * 2 * voxels].reshape(devices_all * capacity, 2 * voxels)
    arrived_ids = arrived[:, capacity * 2 * voxels : capacity * 2 * voxels + capacity].reshape(
        devices_all * capacity
    )
    wanted = (
        jnp.arange(boxes_here, dtype=jnp.float32)[:, None] == arrived_ids[None, :]
    ).astype(jnp.float32)
    sums = jnp.dot(
        wanted, arrived_payload, precision=lax.Precision.HIGHEST, preferred_element_type=jnp.float32
    )
    row_sizes = (local_x, local_y, local_z, BOXX, BOXY, BOXZ)
    lane_sizes = (VX, VY, VZ)
    result = laue_average(sums, row_sizes, lane_sizes)
    return result.reshape(local_x, local_y, local_z, BOX_BRICK, voxels)


def solution(mesh):
    return jax.shard_map(
        shards,
        mesh=mesh,
        in_specs=(
            P(("bx", "by", "bz"), None, None, None),
            P(("bx", "by", "bz"), None, None, None),
            P(("bx", "by", "bz"), None, None, None),
            P(),
            P(),
            P(("bx", "by", "bz")),
            P(("bx", "by", "bz"), None),
            P(("bx", "by", "bz")),
        ),
        out_specs=P("bx", "by", "bz", None, None),
        check_vma=False,
    )
```

```python
import functools

import numpy as np
import jax
import jax.numpy as jnp
from jax import lax
from jax.sharding import PartitionSpec as P
from jax.experimental import pallas as pl
from jax.experimental.pallas import tpu as pltpu

VX = 8
VY = 8
VZ = 4
GX = 8
GY = 8
GZ = 4
BOXX = 4
BOXY = 4
BOXZ = 4
BOX_BRICK = 64


def flip_mask(sizes, flipped):
    mask, stride = 0, 1
    for dim in reversed(range(len(sizes))):
        assert sizes[dim] & (sizes[dim] - 1) == 0
        if dim in flipped:
            mask |= (sizes[dim] - 1) * stride
        stride *= sizes[dim]
    return mask


def flip_matrices(row_sizes, lane_sizes, stage):
    rows = int(np.prod(row_sizes))
    lanes = int(np.prod(lane_sizes))
    out_row = lax.broadcasted_iota(jnp.int32, (rows, rows), 0)
    in_row = lax.broadcasted_iota(jnp.int32, (rows, rows), 1)
    row_flip = (in_row == (out_row ^ flip_mask(row_sizes, (stage, stage + 3)))).astype(jnp.float32)
    in_lane = lax.broadcasted_iota(jnp.int32, (lanes, lanes), 0)
    out_lane = lax.broadcasted_iota(jnp.int32, (lanes, lanes), 1)
    lane_flip = (in_lane == (out_lane ^ flip_mask(lane_sizes, (stage,)))).astype(jnp.float32)
    return row_flip, lane_flip


def split_three(x):
    hi = x.astype(jnp.bfloat16)
    rest = x - hi.astype(jnp.float32)
    mid = rest.astype(jnp.bfloat16)
    lo = (rest - mid.astype(jnp.float32)).astype(jnp.bfloat16)
    return hi, mid, lo


def flipped(pair, matrices):
    row_flip, lane_flip = matrices
    result = []
    for half in pair:
        parts = []
        for piece in split_three(half):
            moved = jnp.dot(row_flip, piece, preferred_element_type=jnp.float32).astype(jnp.bfloat16)
            parts.append(jnp.dot(moved, lane_flip, preferred_element_type=jnp.float32))
        result.append((parts[0] + parts[1]) + parts[2])
    return result


def averaged(pair, other):
    return [0.5 * (mine + moved) for mine, moved in zip(pair, other)]


def laue_kernel(row_sizes, lane_sizes, sums_ref, out_ref, received, held, send_sems, recv_sems):
    voxels = int(np.prod(lane_sizes))
    axes = ("bx", "by", "bz")
    here = tuple(lax.axis_index(axis) for axis in axes)
    sizes = tuple(lax.axis_size(axis) for axis in axes)

    def mirror(flags):
        return tuple(sizes[a] - 1 - here[a] if flags[a] else here[a] for a in range(3))

    first = (mirror((1, 0, 0)), mirror((0, 1, 0)), mirror((1, 1, 0)))
    last = mirror((0, 0, 1))
    barrier = pltpu.get_barrier_semaphore()
    for target in first + (last,):
        pl.semaphore_signal(barrier, 1, device_id=target, device_id_type=pl.DeviceIdType.MESH)
    flips = [
        tuple(m.astype(jnp.bfloat16) for m in flip_matrices(row_sizes, lane_sizes, stage))
        for stage in range(3)
    ]
    pl.semaphore_wait(barrier, 4)

    def send(source, slot, target):
        copy = pltpu.make_async_remote_copy(
            src_ref=source,
            dst_ref=received.at[slot],
            send_sem=send_sems.at[slot],
            recv_sem=recv_sems.at[slot],
            device_id=target,
            device_id_type=pl.DeviceIdType.MESH,
        )
        copy.start()
        return copy

    copies = [send(sums_ref, slot, target) for slot, target in enumerate(first)]

    def halves(ref):
        return [ref[:, :voxels], ref[:, voxels:]]

    copies[0].wait()
    stage_x = averaged(halves(sums_ref), flipped(halves(received.at[0]), flips[0]))
    copies[1].wait()
    copies[2].wait()
    stage_x_there = averaged(
        halves(received.at[1]), flipped(halves(received.at[2]), flips[0])
    )
    stage_y = averaged(stage_x, flipped(stage_x_there, flips[1]))
    held[:, :voxels] = stage_y[0]
    held[:, voxels:] = stage_y[1]
    copy = send(held, 3, last)
    copy.wait()
    stage_z = averaged(halves(held), flipped(halves(received.at[3]), flips[2]))
    out_ref[...] = stage_z[0] / jnp.maximum(stage_z[1], 1.0)


def laue_average(sums, row_sizes, lane_sizes):
    rows, width = sums.shape
    voxels = width // 2
    return pl.pallas_call(
        functools.partial(laue_kernel, row_sizes, lane_sizes),
        in_specs=[pl.BlockSpec(memory_space=pltpu.VMEM)],
        out_specs=pl.BlockSpec(memory_space=pltpu.VMEM),
        out_shape=jax.ShapeDtypeStruct((rows, voxels), jnp.float32),
        scratch_shapes=[
            pltpu.VMEM((4, rows, width), jnp.float32),
            pltpu.VMEM((rows, width), jnp.float32),
            pltpu.SemaphoreType.DMA((4,)),
            pltpu.SemaphoreType.DMA((4,)),
        ],
        compiler_params=pltpu.CompilerParams(collective_id=0, has_side_effects=True),
    )(sums)


def tile_kernel(
    capacity, tiles_frame, frames, owner_ref, box_ref, angle_ref, lorentz_ref,
    counts_ref, eff_ref, rows_ref, cols_ref, out_ref, taken,
):
    block, unused_pixels, voxels = rows_ref.shape
    devices_all, unused_one, total = out_ref.shape
    width = 2 * voxels
    step = pl.program_id(0)

    @pl.when(step == 0)
    def _():
        out_ref[:, :, : capacity * width] = jnp.zeros((devices_all, 1, capacity * width), jnp.float32)
        out_ref[:, :, capacity * width :] = jnp.full((devices_all, 1, total - capacity * width), -1.0, jnp.float32)

        def clear(d, carry):
            taken[d] = 0
            return carry

        lax.fori_loop(0, devices_all, clear, 0)

    lanes = lax.broadcasted_iota(jnp.int32, (1, total - capacity * width), 1)
    for t in range(block):
        tile = ((step % frames) * (tiles_frame // block) + step // frames) * block + t
        target = owner_ref[tile]
        rank = taken[target]
        taken[target] = rank + 1
        factor = lorentz_ref[angle_ref[tile // tiles_frame]]
        cols = cols_ref[t]
        rows = rows_ref[t].astype(jnp.float32)
        both = jnp.dot(
            jnp.concatenate([counts_ref[t], eff_ref[t]], axis=0), cols, preferred_element_type=jnp.float32
        )
        counted = both[: counts_ref.shape[1]]
        seen = both[counts_ref.shape[1] :]
        value = jnp.sum(rows * counted, axis=0, keepdims=True)
        weight = jnp.sum(rows * seen, axis=0, keepdims=True)
        start = pl.multiple_of(rank * width, width)
        out_ref[target, :, pl.ds(start, voxels)] = value * factor
        out_ref[target, :, pl.ds(start + voxels, voxels)] = weight
        label = jnp.full(lanes.shape, box_ref[tile], jnp.int32).astype(jnp.float32)
        out_ref[target, :, capacity * width :] = jnp.where(
            lanes == rank, label, out_ref[target, :, capacity * width :]
        )


def tile_payload(counts, row_split, col_split, efficiency, lorentz, angles, owner, box, devices_all, capacity):
    frames_here, tiles_frame, pixels, columns = counts.shape
    voxels = row_split.shape[-1]
    tiles_here = frames_here * tiles_frame
    label_width = 128
    block = 32
    per_frame = tiles_frame // block

    def order(i):
        return (i % frames_here) * per_frame + i // frames_here

    total = capacity * 2 * voxels + label_width
    return pl.pallas_call(
        functools.partial(tile_kernel, capacity, tiles_frame, frames_here),
        grid_spec=pltpu.PrefetchScalarGridSpec(
            num_scalar_prefetch=3,
            grid=(tiles_here // block,),
            in_specs=[
                pl.BlockSpec(memory_space=pltpu.SMEM),
                pl.BlockSpec((block, pixels, columns), lambda i, *s: (order(i), 0, 0)),
                pl.BlockSpec((block, pixels, columns), lambda i, *s: (i // frames_here, 0, 0)),
                pl.BlockSpec((block, pixels, voxels), lambda i, *s: (order(i), 0, 0)),
                pl.BlockSpec((block, pixels, voxels), lambda i, *s: (order(i), 0, 0)),
            ],
            out_specs=pl.BlockSpec((devices_all, 1, total), lambda i, *s: (0, 0, 0)),
            scratch_shapes=[pltpu.SMEM((devices_all,), jnp.int32)],
        ),
        out_shape=jax.ShapeDtypeStruct((devices_all, 1, total), jnp.float32),
    )(
        owner,
        box,
        angles,
        lorentz,
        counts.reshape(tiles_here, pixels, columns),
        efficiency,
        row_split.reshape(tiles_here, pixels, voxels),
        col_split.reshape(tiles_here, pixels, voxels),
    )


def shards(counts, row_split, col_split, efficiency, lorentz, angles, tile_owner, tile_box):
    frames_here, tiles_frame, pixels, unused_width = counts.shape
    voxels = row_split.shape[-1]
    size_x = lax.axis_size("bx")
    size_y = lax.axis_size("by")
    size_z = lax.axis_size("bz")
    devices_all = size_x * size_y * size_z
    tiles_here = frames_here * tiles_frame
    capacity = max(4, 4 * tiles_here // devices_all)
    local_x = GX // size_x
    local_y = GY // size_y
    local_z = GZ // size_z
    boxes_here = local_x * local_y * local_z * BOX_BRICK
    packed = tile_payload(
        counts, row_split, col_split, efficiency, lorentz, angles,
        tile_owner[:, 0], tile_box, devices_all, capacity,
    )
    arrived = lax.all_to_all(packed, ("bx", "by", "bz"), split_axis=0, concat_axis=0, tiled=True)
    arrived = arrived.reshape(devices_all, -1)
    arrived_payload = arrived[:, : capacity * 2 * voxels].reshape(devices_all * capacity, 2 * voxels)
    arrived_ids = arrived[:, capacity * 2 * voxels : capacity * 2 * voxels + capacity].reshape(
        devices_all * capacity
    )
    wanted = (
        jnp.arange(boxes_here, dtype=jnp.float32)[:, None] == arrived_ids[None, :]
    ).astype(jnp.float32)
    sums = jnp.dot(
        wanted, arrived_payload, precision=lax.Precision.HIGHEST, preferred_element_type=jnp.float32
    )
    row_sizes = (local_x, local_y, local_z, BOXX, BOXY, BOXZ)
    lane_sizes = (VX, VY, VZ)
    result = laue_average(sums, row_sizes, lane_sizes)
    return result.reshape(local_x, local_y, local_z, BOX_BRICK, voxels)


def solution(mesh):
    return jax.shard_map(
        shards,
        mesh=mesh,
        in_specs=(
            P(("bx", "by", "bz"), None, None, None),
            P(("bx", "by", "bz"), None, None, None),
            P(("bx", "by", "bz"), None, None, None),
            P(),
            P(),
            P(("bx", "by", "bz")),
            P(("bx", "by", "bz"), None),
            P(("bx", "by", "bz")),
        ),
        out_specs=P("bx", "by", "bz", None, None),
        check_vma=False,
    )
```
